32 devices in a mesh: seq: 8 (over z, y), tensor: 4 (over x, core).
Axes of the slice: x: 2, y: 2, z: 4, core: 2. Of those that a mesh axis runs over, the one named last changes fastest.
Arguments:
- inputs: bfloat16 [1024, 3, 4096], P('seq', None, 'tensor'), may hold values from -6 to 6
- short_taps: float32 [7, 3, 4096], P(None, None, 'tensor'), may hold values from -2 to 2
- medium_taps: float32 [120, 4096], P(None, 'tensor'), may hold values from -0.5 to 0.5
- long_filter: float32 [1024, 4096], P('seq', 'tensor'), may hold values from -4 to 4
- out_weight: bfloat16 [8192, 4096], P(None, 'tensor'), may hold values from -0.09375 to 0.09375
- out_cotangent: bfloat16 [1024, 8192], P('seq', 'tensor'), may hold values from -6 to 6
Outputs:
- output: bfloat16 [1024, 8192], P('seq', 'tensor')
- input_grad: bfloat16 [1024, 3, 4096], P('seq', None, 'tensor')
- filter_grad: float32 [1024, 4096], P('seq', 'tensor')
- medium_grad: float32 [120, 4096], P(None, 'tensor')
- short_grad: float32 [7, 3, 4096], P(None, None, 'tensor')
The draws below stay inside these ranges and needn't reach their ends.
All inputs are finite; a program needn't handle non-finite values.
Results may differ from the reference program's by a relative error of at most 0.013.
Values may be sent and summed in bfloat16 or wider, within the bound.
No kernel may reach another device: no remote copies, remote signals or barrier semaphores. Data moves between devices by JAX's collectives and lax.ppermute only.
A program may use at most 128 MiB of HBM per device.

```python
import math
import jax
import jax.numpy as jnp
from jax import lax

D = 8192
C = 4096
SHORT = 7
MEDIUM = 120
TOKENS = 1024


def draw_long_filter(key, part):
    flag_key, fast_key, slow_key, amplitude_key, cut_key, drop_key = jax.random.split(key, 6)
    slow_share = 0.5
    slow_flag = jax.random.uniform(flag_key, (C,)) < slow_share
    fast_rate = jnp.exp(jax.random.uniform(fast_key, (C,), minval=math.log(0.06), maxval=math.log(0.15)))
    slow_rate = jnp.exp(jax.random.uniform(slow_key, (C,), minval=math.log(0.05 / TOKENS), maxval=math.log(2.0 / TOKENS)))
    decay_rate = jnp.where(slow_flag, slow_rate, fast_rate)
    step_dimension = jnp.arange(TOKENS, dtype=jnp.float32)[:, None]
    decay_envelope = jnp.exp(-decay_rate[None, :] * step_dimension)
    split_positions = jax.random.randint(cut_key, (4,), 0, TOKENS).astype(jnp.float32)
    removed_lengths = jax.random.uniform(drop_key, (4,), minval=0.2, maxval=0.5)
    for spike_index in range(4):
        decay_envelope = decay_envelope * jnp.where(step_dimension >= split_positions[spike_index], 1.0 - removed_lengths[spike_index], 1.0)
    energy = jnp.expm1(-2.0 * decay_rate * TOKENS) / jnp.expm1(-2.0 * decay_rate)
    amplitude = jax.random.truncated_normal(amplitude_key, -6.0, 6.0, (TOKENS, C))
    return (amplitude * decay_envelope * (1.0 / jnp.sqrt(energy))[None, :]).astype(jnp.float32)


def shard_levels(own_key, shape, shards, smallest, top_value):
    def one(dim, shards_of):
        heights = jax.random.uniform(jax.random.fold_in(jax.random.fold_in(own_key, 6), dim), (shards_of,), jnp.float32, smallest / len(shards), top_value / len(shards))
        return jnp.repeat(jnp.exp(heights), shape[dim] // shards_of).reshape((-1,) + (1,) * (len(shape) - dim - 1))

    factor_of = one(*shards[0])
    for cut in shards[1:]:
        factor_of = factor_of * one(*cut)
    return factor_of


def scatter_about(key, extent, width, reach, cuts=(), held_as=jnp.bfloat16):
    loudness = shard_levels(key, extent, cuts, -0.22, 0.18) if cuts else 1.0
    array = jax.random.normal(key, extent, jnp.float32) * width * loudness
    return jnp.minimum(jnp.maximum(array, -reach), reach).astype(held_as)


def setup_inputs(seed: int = 0) -> dict:
    key_of = jax.random.split(jax.random.key(seed), 7)
    inputs = scatter_about(key_of[0], (TOKENS, 3, C), 1.0, 6.0, ((0, 8), (2, 4)))
    short_taps = scatter_about(key_of[1], (SHORT, 3, C), SHORT ** -0.5, 2.0, ((2, 4),), jnp.float32)
    medium_taps = scatter_about(key_of[2], (MEDIUM, C), MEDIUM ** -0.5, 0.5, ((1, 4),), jnp.float32)
    long_filter = draw_long_filter(jax.random.fold_in(key_of[6], 71), 0)
    out_weight = scatter_about(key_of[4], (D, C), C ** -0.5, 0.09375, ((1, 4),))
    out_cotangent = scatter_about(key_of[5], (TOKENS, D), 1.0, 6.0, ((0, 8), (1, 4)))
    return dict(inputs=inputs, short_taps=short_taps, medium_taps=medium_taps, long_filter=long_filter, out_weight=out_weight, out_cotangent=out_cotangent)


def causal_filter(signal, tap_weights):
    length = signal.shape[0]
    tap_count = tap_weights.shape[0]
    padded = jnp.concatenate([jnp.zeros((tap_count - 1,) + signal.shape[1:], jnp.float32), signal], 0)

    def add_tap(offset, running):
        window = lax.dynamic_slice_in_dim(padded, (tap_count - 1 - offset).astype(jnp.int32), length, 0)
        return running + tap_weights[offset] * window
    return lax.fori_loop(0, tap_count, add_tap, jnp.zeros(signal.shape, jnp.float32))

def anticausal_filter(signal, tap_weights):
    length = signal.shape[0]
    tap_count = tap_weights.shape[0]
    padded = jnp.concatenate([signal, jnp.zeros((tap_count - 1,) + signal.shape[1:], jnp.float32)], 0)

    def add_tap(offset, running):
        window = lax.dynamic_slice_in_dim(padded, jnp.asarray(offset).astype(jnp.int32), length, 0)
        return running + tap_weights[offset] * window
    return lax.fori_loop(0, tap_count, add_tap, jnp.zeros(signal.shape, jnp.float32))

def tap_gradient(signal, output_gradient, tap_count):
    length = signal.shape[0]
    padded = jnp.concatenate([jnp.zeros((tap_count - 1,) + signal.shape[1:], jnp.float32), signal], 0)

    def one_tap(offset):
        window = lax.dynamic_slice_in_dim(padded, (tap_count - 1 - offset).astype(jnp.int32), length, 0)
        return lax.optimization_barrier(jnp.sum(window * output_gradient, axis=0))
    return lax.map(one_tap, jnp.arange(tap_count, dtype=jnp.int32))

def spectrum(signal):
    return jnp.fft.rfft(signal, n=2 * TOKENS, axis=0)

def back_to_time(spectral):
    return jnp.fft.irfft(spectral, n=2 * TOKENS, axis=0)[:TOKENS].astype(jnp.float32)

def reference(inputs, short_taps, medium_taps, long_filter, out_weight, out_cotangent):
    scale = 1.0 / math.sqrt(TOKENS)
    widened = inputs.astype(jnp.float32)
    featured = causal_filter(widened, short_taps)
    query_branch = featured[:, 0]
    key_branch = featured[:, 1]
    value_branch = featured[:, 2]
    gated = key_branch * value_branch
    mixed = causal_filter(gated, medium_taps)
    mixed_spec = spectrum(mixed)
    filter_spec = spectrum(long_filter)
    convolved = back_to_time(mixed_spec * filter_spec)
    product = (query_branch * convolved).astype(jnp.bfloat16)
    output = jnp.dot(product, out_weight.T, preferred_element_type=jnp.float32).astype(jnp.bfloat16)
    product_grad = jnp.dot(out_cotangent, out_weight, preferred_element_type=jnp.float32)
    query_grad = product_grad * convolved
    convolved_grad = product_grad * query_branch
    grad_spec = spectrum(convolved_grad)
    mixed_grad = back_to_time(jnp.conj(filter_spec) * grad_spec)
    filter_grad = back_to_time(jnp.conj(mixed_spec) * grad_spec) * scale
    gated_grad = anticausal_filter(mixed_grad, medium_taps)
    medium_grad = tap_gradient(gated, mixed_grad, MEDIUM) * scale
    feature_gradient = jnp.stack([query_grad, gated_grad * value_branch, gated_grad * key_branch], 1)
    input_grad = anticausal_filter(feature_gradient, short_taps).astype(jnp.bfloat16)
    short_grad = tap_gradient(widened, feature_gradient, SHORT) * scale
    return (output, input_grad, filter_grad, medium_grad, short_grad)
```

```python
import math
from functools import partial

import jax
import jax.numpy as jnp
import numpy as np
from jax import lax
from jax.experimental import pallas as pl
from jax.experimental.pallas import tpu as pltpu
from jax.sharding import PartitionSpec as P

F32 = jnp.float32
BF16 = jnp.bfloat16
HALO = 8
GROUP = 32
TABLE_LIMIT = 1 << 23


def dot(a, b):
    return lax.dot_general(a, b, (((1,), (0,)), ((), ())), preferred_element_type=F32)


def back_to_time(columns, spectrum):
    contracted = 0 if columns.shape[0] == spectrum.shape[0] and columns.shape[1] != spectrum.shape[0] else 1
    return lax.dot_general(
        columns, spectrum, (((contracted,), (0,)), ((), ())), preferred_element_type=F32
    )


def exchange(value, axis, flip):
    count = lax.axis_size(axis)
    return lax.ppermute(value, axis, [(source, source ^ flip) for source in range(count)])


def shift(value, axis, steps):
    count = lax.axis_size(axis)
    pairs = [(s, s + steps) for s in range(count) if 0 <= s + steps < count]
    return lax.ppermute(value, axis, pairs)


def whole(shape):
    return pl.BlockSpec(shape, lambda *_: (0,) * len(shape))


def bit_reverse(value, bits):
    return sum(((value >> i) & 1) << (bits - 1 - i) for i in range(bits))


def spectral_sizes(tokens, medium_reach):
    need = tokens + -(-(medium_reach - 2) // 2)
    block = 384
    blocks = -(-need // block)
    return blocks * block, block


def dft_tables(tokens, freqs, block):
    period = 4 * freqs
    unit = 2.0 * math.pi / period

    def turned(coarse, fine):
        first = (coarse % period).astype(F32) * unit
        second = (fine % period).astype(F32) * unit
        return (jnp.cos(first) * jnp.cos(second) - jnp.sin(first) * jnp.sin(second)).astype(BF16)

    blocks = freqs // block
    time = jnp.arange(tokens, dtype=jnp.int32)
    base = GROUP * jnp.arange(2 * freqs // GROUP, dtype=jnp.int32)
    within = base % (2 * block)
    first_freq = base // (2 * block) * block + within % block
    quarter = jnp.where(within >= block, freqs, 0)
    coarse = 2 * first_freq[:, None] * time[None, :] + (period - quarter)[:, None]
    inner = jnp.arange(GROUP, dtype=jnp.int32)
    fine = (2 * inner[:, None] + 1) * time[None, :]
    rows = turned(coarse[:, None, :], fine[None, :, :]).reshape(blocks, 2 * block, tokens)
    if rows.size > TABLE_LIMIT:
        return rows, rows

    column = jnp.arange(2 * block, dtype=jnp.int32)
    freq = jnp.arange(blocks, dtype=jnp.int32)[:, None] * block + column[None, :] % block
    odd = 2 * freq + 1
    offset = jnp.where(column >= block, freqs, 0)
    start = GROUP * jnp.arange(tokens // GROUP, dtype=jnp.int32)
    coarse = odd[:, None, :] * start[None, :, None] + (period - offset)[None, None, :]
    fine = odd[:, None, :] * inner[None, :, None]
    columns = turned(coarse[:, :, None, :], fine[:, None, :, :]).reshape(blocks, tokens, 2 * block)
    return rows, columns


def pack_kernel(x_ref, filter_ref, out_ref):
    parts, rows, width = out_ref.shape
    length = rows // 3
    for j in range(parts):
        lanes = slice(j * width, (j + 1) * width)
        out_ref[j, 0:length, :] = x_ref[1, :, lanes]
        out_ref[j, length : 2 * length, :] = x_ref[2, :, lanes]
        out_ref[j, 2 * length :, :] = filter_ref[:, lanes].astype(BF16)


def query_kernel(x_ref, edge_ref, taps_ref, out_ref, ext):
    length = out_ref.shape[0]
    reach = taps_ref.shape[0]
    ext[0:HALO, :] = edge_ref[...].astype(F32)
    ext[HALO:, :] = x_ref[0].astype(F32)
    total = taps_ref[0:1, :] * ext[HALO : HALO + length, :]
    for i in range(1, reach):
        total = total + taps_ref[i : i + 1, :] * ext[HALO - i : HALO - i + length, :]
    out_ref[...] = total


def grad_first_kernel(_, x0_ref, x1_ref, w_ref, out_ref, *, per):
    step = pl.program_id(0)

    @pl.when(step == 0)
    def _():
        out_ref[...] = jnp.zeros_like(out_ref)

    @pl.when(step < per)
    def _():
        out_ref[...] += dot(x0_ref[...], w_ref[...])

    @pl.when(step >= per)
    def _():
        out_ref[...] += dot(x1_ref[...], w_ref[...])


def grad_second_kernel(_, x0_ref, x1_ref, w_ref, acc_ref, query_ref, out_ref, sent_ref, *, per):
    step = pl.program_id(0)

    @pl.when(step == 0)
    def _():
        out_ref[...] = acc_ref[...]

    @pl.when(step < per)
    def _():
        out_ref[...] += dot(x0_ref[...], w_ref[...])

    @pl.when(step >= per)
    def _():
        out_ref[...] += dot(x1_ref[...], w_ref[...])

    @pl.when(step == 2 * per - 1)
    def _():
        parts, _, width = sent_ref.shape
        for j in range(parts):
            lanes = slice(j * width, (j + 1) * width)
            sent_ref[j] = (out_ref[:, lanes] * query_ref[:, lanes]).astype(BF16)


def product_grad_of(x0, x1, weight, shards, acc=None, query=None, parts=None):
    length, features = x0.shape
    channels = weight.shape[1]
    deep = math.gcd(features, 1024)
    per = features // deep
    in_specs = [
        pl.BlockSpec((length, deep), lambda k, s: (0, jnp.minimum(k, per - 1))),
        pl.BlockSpec((length, deep), lambda k, s: (0, jnp.maximum(k - per, 0))),
        pl.BlockSpec((deep, channels), lambda k, s: (s[k // per] * per + k % per, 0)),
    ]
    full = whole((length, channels))
    if acc is None:
        return pl.pallas_call(
            partial(grad_first_kernel, per=per),
            grid_spec=pltpu.PrefetchScalarGridSpec(
                num_scalar_prefetch=1, grid=(2 * per,), in_specs=in_specs, out_specs=full
            ),
            out_shape=jax.ShapeDtypeStruct((length, channels), F32),
            name="grad_first",
        )(shards, x0, x1, weight)
    width = channels // parts
    return pl.pallas_call(
        partial(grad_second_kernel, per=per),
        grid_spec=pltpu.PrefetchScalarGridSpec(
            num_scalar_prefetch=1,
            grid=(2 * per,),
            in_specs=in_specs + [full, full],
            out_specs=[full, pl.BlockSpec((parts, length, width), lambda k, s: (0, 1, 0))],
        ),
        out_shape=[
            jax.ShapeDtypeStruct((length, channels), F32),
            jax.ShapeDtypeStruct((parts, 2 * length, width), BF16),
        ],
        name="grad_second",
    )(shards, x0, x1, weight, acc, query)


def forward_kernel(
    got_ref, taps_ref, medium_ref, rows_ref, columns_ref, _,
    out_ref, key_ref, value_ref, a_ref, m_ref, h_ref,
    ext, signals, medium, acc, *, length, freqs,
):
    step = pl.program_id(0)
    parts, _, width = got_ref.shape
    reach = taps_ref.shape[0]
    block = rows_ref.shape[1] // 2

    @pl.when(step == 0)
    def _():
        ext[:, 0:HALO, :] = jnp.zeros((2, HALO, width), F32)
        for s in range(parts):
            here = slice(HALO + s * length, HALO + (s + 1) * length)
            ext[0, here, :] = got_ref[s, 0:length, :].astype(F32)
            ext[1, here, :] = got_ref[s, length : 2 * length, :].astype(F32)
        for s in range(parts):
            begin = HALO + s * length
            here = slice(s * length, (s + 1) * length)
            key = taps_ref[0, 0:1, :] * ext[0, begin : begin + length, :]
            value = taps_ref[0, 1:2, :] * ext[1, begin : begin + length, :]
            for i in range(1, reach):
                key = key + taps_ref[i, 0:1, :] * ext[0, begin - i : begin - i + length, :]
                value = value + taps_ref[i, 1:2, :] * ext[1, begin - i : begin - i + length, :]
            key_ref[here, :] = key
            value_ref[here, :] = value
            signals[here, 0:width] = (key * value).astype(BF16)
            signals[here, width : 2 * width] = got_ref[s, 2 * length : 3 * length, :]
        medium[...] = jnp.zeros_like(medium)
        medium[0 : medium_ref.shape[0], :] = medium_ref[...].astype(BF16)
        acc[...] = jnp.zeros_like(acc)

    rows = rows_ref[0]
    spectra = dot(rows, signals[...])
    m = dot(rows[:, 0 : medium.shape[0]], medium[...])
    a = spectra[:, 0:width]
    h = spectra[:, width : 2 * width]
    a_ref[0] = a
    m_ref[0] = m
    h_ref[0] = h
    ac, as_, mc, ms = (a[:block], a[block:], m[:block], m[block:])
    hc, hs = (h[:block], h[block:])
    xc = ac * mc - as_ * ms
    xs = ac * ms + as_ * mc
    y = jnp.concatenate([xc * hc - xs * hs, xc * hs + xs * hc], 0).astype(BF16)
    acc[...] += back_to_time(columns_ref[0], y)

    @pl.when(step == pl.num_programs(0) - 1)
    def _():
        for s in range(parts):
            out_ref[s] = (acc[s * length : (s + 1) * length, :] * (1.0 / freqs)).astype(BF16)


def forward_call(got, taps, medium_taps, rows, columns, sent, freqs):
    parts, tall, width = got.shape
    length = tall // 3
    blocks, double, tokens = rows.shape
    padded = -(-medium_taps.shape[0] // 128) * 128
    per_block = pl.BlockSpec((1, double, width), lambda j: (j, 0, 0))
    spectrum = jax.ShapeDtypeStruct((blocks, double, width), F32)
    timed = jax.ShapeDtypeStruct((tokens, width), F32)
    return pl.pallas_call(
        partial(forward_kernel, length=length, freqs=freqs),
        grid=(blocks,),
        in_specs=[
            whole(got.shape),
            whole(taps.shape),
            whole(medium_taps.shape),
            pl.BlockSpec((1, double, tokens), lambda j: (j, 0, 0)),
            pl.BlockSpec((1,) + columns.shape[1:], lambda j: (j, 0, 0)),
            pl.BlockSpec(memory_space=pl.ANY),
        ],
        out_specs=[
            pl.BlockSpec((parts, length, width), lambda j: (0, 0, 0)),
            whole((tokens, width)),
            whole((tokens, width)),
            per_block,
            per_block,
            per_block,
        ],
        out_shape=[jax.ShapeDtypeStruct(sent.shape, BF16), timed, timed, spectrum, spectrum, spectrum],
        scratch_shapes=[
            pltpu.VMEM((2, tokens + HALO, width), F32),
            pltpu.VMEM((tokens, 2 * width), BF16),
            pltpu.VMEM((padded, width), BF16),
            pltpu.VMEM((tokens, width), F32),
        ],
        input_output_aliases={5: 0},
        name="forward_spectral",
    )(got, taps, medium_taps, rows, columns, sent)


def backward_kernel(
    got_ref, grads_ref, taps_ref, key_ref, value_ref, a_ref, m_ref, h_ref, rows_ref, columns_ref,
    out_ref, small_ref,
    ext, after, signal, acc, tap_acc, *, length, freqs, scale, medium_reach,
):
    step = pl.program_id(0)
    parts, _, width = got_ref.shape
    reach = taps_ref.shape[0]
    block = rows_ref.shape[1] // 2
    tokens = signal.shape[0]

    @pl.when(step == 0)
    def _():
        for s in range(parts):
            signal[s * length : (s + 1) * length, :] = grads_ref[s]
        acc[...] = jnp.zeros_like(acc)
        tap_acc[...] = jnp.zeros_like(tap_acc)

    g = dot(rows_ref[0], signal[...])
    a, m, h = (a_ref[0], m_ref[0], h_ref[0])
    ac, as_, mc, ms = (a[:block], a[block:], m[:block], m[block:])
    hc, hs, gc, gs = (h[:block], h[block:], g[:block], g[block:])
    uc = hc * gc + hs * gs
    us = hc * gs - hs * gc
    xc = ac * mc - as_ * ms
    xs = ac * ms + as_ * mc
    filter_part = jnp.concatenate([xc * gc + xs * gs, xc * gs - xs * gc], 0)
    gated_part = jnp.concatenate([mc * uc + ms * us, mc * us - ms * uc], 0)
    taps_part = jnp.concatenate([ac * uc + as_ * us, ac * us - as_ * uc], 0)
    both = jnp.concatenate([filter_part, gated_part], 1).astype(BF16)
    columns = columns_ref[0]
    acc[...] += back_to_time(columns, both)
    kept = tap_acc.shape[0]
    first = columns[0:kept, :] if columns.shape[0] == tokens else columns[:, 0:kept]
    tap_acc[...] += back_to_time(first, taps_part.astype(BF16))

    @pl.when(step == pl.num_programs(0) - 1)
    def _():
        inverse = 1.0 / freqs
        small_ref[...] = jnp.zeros_like(small_ref)
        small_ref[0:medium_reach, :] = tap_acc[0:medium_reach, :] * (inverse * scale)
        ext[:, 0:HALO, :] = jnp.zeros((2, HALO, width), F32)
        after[:, tokens : tokens + HALO, :] = jnp.zeros((2, HALO, width), F32)
        for s in range(parts):
            here = slice(s * length, (s + 1) * length)
            there = slice(HALO + s * length, HALO + (s + 1) * length)
            out_ref[s, 2 * length : 3 * length, :] = (acc[here, 0:width] * (inverse * scale)).astype(BF16)
            gated = acc[here, width : 2 * width] * inverse
            after[0, here, :] = gated * value_ref[here, :]
            after[1, here, :] = gated * key_ref[here, :]
            ext[0, there, :] = got_ref[s, 0:length, :].astype(F32)
            ext[1, there, :] = got_ref[s, length : 2 * length, :].astype(F32)
        for j in range(2):
            sums = [jnp.zeros((8, width), F32) for _ in range(reach)]
            for s in range(parts):
                begin = s * length
                own = after[j, begin : begin + length, :]
                total = taps_ref[0, j : j + 1, :] * own
                for i in range(reach):
                    if i:
                        total = total + taps_ref[i, j : j + 1, :] * after[j, begin + i : begin + i + length, :]
                    moved = ext[j, HALO + begin - i : HALO + begin - i + length, :]
                    sums[i] = sums[i] + jnp.sum((moved * own).reshape(length // 8, 8, width), 0)
                out_ref[s, j * length : (j + 1) * length, :] = total.astype(BF16)
            for i in range(reach):
                row = medium_reach + j * reach + i
                small_ref[row : row + 1, :] = jnp.sum(sums[i], 0, keepdims=True) * scale


def backward_call(got, grads, taps, key, value, spectra, rows, columns, freqs, scale, medium_reach):
    parts, tall, width = got.shape
    length = tall // 3
    reach = taps.shape[0]
    blocks, double, tokens = rows.shape
    padded = -(-medium_reach // 128) * 128
    small = -(-(medium_reach + 2 * reach) // 16) * 16
    per_block = pl.BlockSpec((1, double, width), lambda j: (j, 0, 0))
    return pl.pallas_call(
        partial(backward_kernel, length=length, freqs=freqs, scale=scale, medium_reach=medium_reach),
        grid=(blocks,),
        in_specs=[
            whole(got.shape),
            pl.BlockSpec((parts, length, width), lambda j: (0, 1, 0)),
            whole(taps.shape),
            whole((tokens, width)),
            whole((tokens, width)),
            per_block,
            per_block,
            per_block,
            pl.BlockSpec((1, double, tokens), lambda j: (j, 0, 0)),
            pl.BlockSpec((1,) + columns.shape[1:], lambda j: (j, 0, 0)),
        ],
        out_specs=[whole(got.shape), whole((small, width))],
        out_shape=[
            jax.ShapeDtypeStruct(got.shape, BF16),
            jax.ShapeDtypeStruct((small, width), F32),
        ],
        scratch_shapes=[
            pltpu.VMEM((2, tokens + HALO, width), F32),
            pltpu.VMEM((2, tokens + HALO, width), F32),
            pltpu.VMEM((tokens, width), BF16),
            pltpu.VMEM((tokens, 2 * width), F32),
            pltpu.VMEM((padded, width), F32),
        ],
        name="backward_spectral",
    )(got, grads, taps, key, value, *spectra, rows, columns)


def product_kernel(got_ref, query_ref, grad_ref, x_ref, edge_ref, product_ref, query_grad_ref, taps_ref, ext):
    parts, length, width = got_ref.shape
    reach = taps_ref.shape[0] - 1
    for j in range(parts):
        lanes = slice(j * width, (j + 1) * width)
        convolved = got_ref[j].astype(F32)
        product_ref[:, lanes] = (query_ref[:, lanes] * convolved).astype(BF16)
        query_grad_ref[:, lanes] = grad_ref[:, lanes] * convolved
    ext[0:HALO, :] = edge_ref[...].astype(F32)
    ext[HALO:, :] = x_ref[0].astype(F32)
    own = query_grad_ref[...]
    taps_ref[...] = jnp.zeros_like(taps_ref)
    for i in range(reach):
        moved = ext[HALO - i : HALO - i + length, :]
        taps_ref[i : i + 1, :] = jnp.sum(moved * own, 0, keepdims=True)


def project_kernel(_, product_ref, w_ref, out_ref):
    out_ref[...] = lax.dot_general(
        product_ref[...], w_ref[...], (((1,), (1,)), ((), ())), preferred_element_type=F32
    ).astype(out_ref.dtype)


def project(product, weight, shard, features, dtype):
    length, channels = product.shape
    deep = math.gcd(features, 1024)
    per = features // deep
    return pl.pallas_call(
        project_kernel,
        grid_spec=pltpu.PrefetchScalarGridSpec(
            num_scalar_prefetch=1,
            grid=(per,),
            in_specs=[
                whole((length, channels)),
                pl.BlockSpec((deep, channels), lambda k, s: (s[0] * per + k, 0)),
            ],
            out_specs=pl.BlockSpec((length, deep), lambda k, s: (0, k)),
        ),
        out_shape=jax.ShapeDtypeStruct((length, features), dtype),
        name="project",
    )(shard, product, weight)


def finish_kernel(
    where_ref, got_ref, query_grad_ref, next_ref, taps_ref, small_ref, query_short_ref,
    input_grad_ref, filter_ref, medium_ref, short_ref, ext, *, scale,
):
    parts, rows, width = got_ref.shape
    length = rows // 3
    reach = taps_ref.shape[0]
    medium_reach = medium_ref.shape[0]
    bits = parts.bit_length() - 1
    for j in range(parts):
        lanes = slice(j * width, (j + 1) * width)
        input_grad_ref[1, :, lanes] = got_ref[j, 0:length, :]
        input_grad_ref[2, :, lanes] = got_ref[j, length : 2 * length, :]
        filter_ref[:, lanes] = got_ref[j, 2 * length :, :].astype(F32)
        small = small_ref[jnp.bitwise_xor(where_ref[0], bit_reverse(j, bits))].astype(F32)
        medium_ref[:, lanes] = small[0:medium_reach, :]
        short_ref[1, :, lanes] = small[medium_reach : medium_reach + reach, :]
        short_ref[2, :, lanes] = small[medium_reach + reach : medium_reach + 2 * reach, :]
    short_ref[0] = query_short_ref[0:reach, :] * scale
    ext[0:length, :] = query_grad_ref[...]
    ext[length:, :] = next_ref[...]
    total = taps_ref[0:1, :] * ext[0:length, :]
    for i in range(1, reach):
        total = total + taps_ref[i : i + 1, :] * ext[i : i + length, :]
    input_grad_ref[0] = total.astype(BF16)


def reshard(value):
    return lax.all_to_all(value, "seq", split_axis=0, concat_axis=0, tiled=True)


def local(inputs, short_taps, medium_taps, long_filter, out_weight, out_cotangent):
    length, groups, channels = inputs.shape
    reach = short_taps.shape[0]
    medium_reach = medium_taps.shape[0]
    parts = lax.axis_size("seq")
    bits = parts.bit_length() - 1
    position = lax.axis_index("seq")
    place = lax.axis_index("tensor")
    features = out_cotangent.shape[1]
    width = channels // parts
    tokens = length * parts
    scale = 1.0 / math.sqrt(tokens)
    freqs, block = spectral_sizes(tokens, medium_reach)

    streams = inputs.transpose(1, 0, 2)
    cot_x = exchange(out_cotangent, "tensor", 2)
    cot_core = exchange(out_cotangent, "tensor", 1)
    query_edge = shift(streams[0, length - HALO :], "seq", 1)

    packed = pl.pallas_call(
        pack_kernel,
        out_shape=jax.ShapeDtypeStruct((parts, 3 * length, width), BF16),
        name="pack",
    )(streams, long_filter)
    got = reshard(packed)

    rows, columns = dft_tables(tokens, freqs, block)
    own_taps = lax.dynamic_slice_in_dim(short_taps[:, 1:], position * width, width, 2)
    own_medium = lax.dynamic_slice_in_dim(medium_taps, position * width, width, 1)
    query_taps = short_taps[:, 0]

    query = pl.pallas_call(
        query_kernel,
        out_shape=jax.ShapeDtypeStruct((length, channels), F32),
        scratch_shapes=[pltpu.VMEM((length + HALO, channels), F32)],
        name="query",
    )(streams, query_edge, query_taps)

    def shard(flip):
        return jnp.bitwise_xor(place, flip).astype(jnp.int32)

    acc = product_grad_of(out_cotangent, cot_core, out_weight, jnp.stack([shard(0), shard(1)]))
    cot_far = exchange(cot_x, "tensor", 1)
    product_grad, sent = product_grad_of(
        cot_x, cot_far, out_weight, jnp.stack([shard(2), shard(3)]), acc, query, parts
    )

    sent, key, value, *spectra = forward_call(
        got, own_taps, own_medium, rows, columns, sent, freqs
    )
    crossed = reshard(sent)

    product, query_grad, query_short = pl.pallas_call(
        product_kernel,
        grid=(1,),
        in_specs=[
            pl.BlockSpec((parts, length, width), lambda j: (0, 0, 0)),
            whole((length, channels)),
            whole((length, channels)),
            whole(streams.shape),
            whole((HALO, channels)),
        ],
        out_specs=[whole((length, channels)), whole((length, channels)), whole((reach + 1, channels))],
        out_shape=[
            jax.ShapeDtypeStruct((length, channels), BF16),
            jax.ShapeDtypeStruct((length, channels), F32),
            jax.ShapeDtypeStruct((reach + 1, channels), F32),
        ],
        scratch_shapes=[pltpu.VMEM((length + HALO, channels), F32)],
        name="product",
    )(crossed, query, product_grad, streams, query_edge)

    far = project(product, out_weight, shard(3)[None], features, BF16)
    far_core = exchange(far, "tensor", 1)
    across = project(product, out_weight, shard(2)[None], features, F32)
    across_sum = exchange((across + far_core.astype(F32)).astype(BF16), "tensor", 2)
    near = project(product, out_weight, shard(1)[None], features, BF16)
    near_core = exchange(near, "tensor", 1)
    own = project(product, out_weight, shard(0)[None], features, F32)

    back, small = backward_call(
        got, crossed, own_taps, key, value, spectra, rows, columns, freqs, scale, medium_reach
    )
    returned = reshard(back)

    gathered = small.astype(BF16)[None]
    for step in range(bits):
        gathered = jnp.concatenate([gathered, exchange(gathered, "seq", parts >> (step + 1))], 0)
    next_grad = shift(query_grad[:HALO].astype(BF16), "seq", -1).astype(F32)
    for step in range(bits):
        query_short = query_short + exchange(query_short, "seq", 1 << step)

    where = jnp.int32(0)
    for i in range(bits):
        where = where + (((position >> i) & 1) << (bits - 1 - i)).astype(jnp.int32)
    vmem = pl.BlockSpec(memory_space=pltpu.VMEM)
    input_grad, filter_grad, medium_grad, short_grad = pl.pallas_call(
        partial(finish_kernel, scale=scale),
        in_specs=[pl.BlockSpec(memory_space=pltpu.SMEM)] + [vmem] * 6,
        out_specs=[vmem] * 4,
        out_shape=[
            jax.ShapeDtypeStruct((groups, length, channels), BF16),
            jax.ShapeDtypeStruct((length, channels), F32),
            jax.ShapeDtypeStruct((medium_reach, channels), F32),
            jax.ShapeDtypeStruct((groups, reach, channels), F32),
        ],
        scratch_shapes=[pltpu.VMEM((length + HALO, channels), F32)],
        name="finish",
    )(where[None], returned, query_grad, next_grad, query_taps, gathered, query_short)

    output = (own + near_core.astype(F32) + across_sum.astype(F32)).astype(BF16)
    return (
        output,
        input_grad.transpose(1, 0, 2),
        filter_grad,
        medium_grad,
        short_grad.transpose(1, 0, 2),
    )


def solution(mesh):
    return jax.shard_map(
        local,
        mesh=mesh,
        in_specs=(
            P("seq", None, "tensor"),
            P(None, None, "tensor"),
            P(None, "tensor"),
            P("seq", "tensor"),
            P(None, "tensor"),
            P("seq", "tensor"),
        ),
        out_specs=(
            P("seq", "tensor"),
            P("seq", None, "tensor"),
            P("seq", "tensor"),
            P(None, "tensor"),
            P(None, None, "tensor"),
        ),
        check_vma=False,
    )
```

```python
import math
from functools import partial

import jax
import jax.numpy as jnp
from jax import lax
from jax.experimental import pallas as pl
from jax.experimental.pallas import tpu as pltpu
from jax.sharding import PartitionSpec as P


F32 = jnp.float32
BF16 = jnp.bfloat16
HALO = 8
GROUP = 32
CHUNK = 512
VMEM_SPECTRAL = 24
TABLE_LIMIT = 1 << 22


def dot(a, b):
    return lax.dot_general(a, b, (((1,), (0,)), ((), ())), preferred_element_type=F32)


def exchange(value, axis, flip):
    count = lax.axis_size(axis)
    return lax.ppermute(value, axis, [(source, source ^ flip) for source in range(count)])


def shift(value, axis, steps):
    count = lax.axis_size(axis)
    pairs = [(s, s + steps) for s in range(count) if 0 <= s + steps < count]
    return lax.ppermute(value, axis, pairs)


def whole(shape):
    return pl.BlockSpec(shape, lambda *_: (0,) * len(shape))


def spectral_sizes(tokens, medium_reach):
    need = tokens + -(-(medium_reach - 2) // 2)
    freqs = -(-need // 384) * 384
    return freqs, 384


def dft_tables(freqs):
    period = 8 * freqs
    unit = 2.0 * math.pi / period
    odd = 2 * jnp.arange(freqs, dtype=jnp.int32) + 1
    start = 2 * GROUP * jnp.arange(freqs // GROUP, dtype=jnp.int32)
    inner = 2 * jnp.arange(GROUP, dtype=jnp.int32) + 1
    first = (start[:, None] * odd[None, :] % period).astype(F32) * unit
    second = (inner[:, None] * odd[None, :] % period).astype(F32) * unit
    fc, fs = jnp.cos(first)[:, None], jnp.sin(first)[:, None]
    sc, ss = jnp.cos(second)[None], jnp.sin(second)[None]
    cosine = (fc * sc - fs * ss).astype(BF16).reshape(freqs, freqs)
    sine = (fs * sc + fc * ss).astype(BF16).reshape(freqs, freqs)
    return cosine, sine


def limit(mebibytes):
    return pltpu.CompilerParams(vmem_limit_bytes=mebibytes << 20)


def pack_kernel(x_ref, filter_ref, out_ref):
    parts, rows, width = out_ref.shape
    length = rows // 3
    for j in range(parts):
        lanes = slice(j * width, (j + 1) * width)
        out_ref[j, 0:length, :] = x_ref[1, :, lanes]
        out_ref[j, length : 2 * length, :] = x_ref[2, :, lanes]
        out_ref[j, 2 * length :, :] = filter_ref[:, lanes].astype(BF16)


def query_kernel(x_ref, edge_ref, taps_ref, out_ref, ext):
    length = out_ref.shape[0]
    reach = taps_ref.shape[1]
    ext[0:HALO, :] = edge_ref[...].astype(F32)
    ext[HALO:, :] = x_ref[0].astype(F32)
    total = taps_ref[0, 0:1, :] * ext[HALO : HALO + length, :]
    for i in range(1, reach):
        total = total + taps_ref[0, i : i + 1, :] * ext[HALO - i : HALO - i + length, :]
    out_ref[...] = total


def weight_chunks(place_ref, weight_ref, buffer, sems, flips, features):
    deep = buffer.shape[1]
    per = features // deep
    copies = []
    for i, flip in enumerate(flips):
        for k in range(per):
            start = jnp.bitwise_xor(place_ref[0], flip) * features + k * deep
            slot = i * per + k
            copies.append(
                pltpu.make_async_copy(
                    weight_ref.at[pl.ds(pl.multiple_of(start, deep), deep), :], buffer.at[slot], sems.at[slot]
                )
            )
    return copies


def chunk_scratch(weight, features, shards):
    deep = math.gcd(features, CHUNK)
    count = shards * (features // deep)
    return [pltpu.VMEM((count, deep, weight.shape[1]), weight.dtype), pltpu.SemaphoreType.DMA((count,))]


def summed(x_refs, copies, buffer, total):
    deep = buffer.shape[1]
    per = len(copies) // len(x_refs)
    for slot, copy in enumerate(copies):
        copy.wait()
        lanes = slice(slot % per * deep, (slot % per + 1) * deep)
        part = dot(x_refs[slot // per][:, lanes], buffer[slot])
        total = part if total is None else total + part
    return total


def grad_first_kernel(place_ref, x0_ref, x1_ref, w_ref, out_ref, buffer, sems, *, flips):
    copies = weight_chunks(place_ref, w_ref, buffer, sems, flips, x0_ref.shape[1])
    for copy in copies:
        copy.start()
    out_ref[...] = summed((x0_ref, x1_ref), copies, buffer, None)


def grad_second_kernel(
    place_ref, x0_ref, x1_ref, w_ref, acc_ref, query_ref, out_ref, sent_ref, buffer, sems, *, flips
):
    copies = weight_chunks(place_ref, w_ref, buffer, sems, flips, x0_ref.shape[1])
    for copy in copies:
        copy.start()
    total = summed((x0_ref, x1_ref), copies, buffer, acc_ref[...])
    out_ref[...] = total
    parts, _, width = sent_ref.shape
    for j in range(parts):
        lanes = slice(j * width, (j + 1) * width)
        sent_ref[j] = (total[:, lanes] * query_ref[:, lanes]).astype(BF16)


def product_grad_of(x0, x1, weight, place, flips, acc=None, query=None, parts=None):
    length, features = x0.shape
    channels = weight.shape[1]
    smem = pl.BlockSpec(memory_space=pltpu.SMEM)
    vmem = pl.BlockSpec(memory_space=pltpu.VMEM)
    in_specs = [smem, vmem, vmem, pl.BlockSpec(memory_space=pltpu.HBM)]
    full = jax.ShapeDtypeStruct((length, channels), F32)
    scratch = chunk_scratch(weight, features, 2)
    if acc is None:
        return pl.pallas_call(
            partial(grad_first_kernel, flips=flips),
            in_specs=in_specs,
            out_specs=vmem,
            out_shape=full,
            scratch_shapes=scratch,
            compiler_params=limit(16),
            name="grad_first",
        )(place, x0, x1, weight)
    width = channels // parts
    return pl.pallas_call(
        partial(grad_second_kernel, flips=flips),
        grid=(1,),
        in_specs=in_specs + [vmem, vmem],
        out_specs=[vmem, pl.BlockSpec((parts, length, width), lambda j: (0, 1, 0))],
        out_shape=[full, jax.ShapeDtypeStruct((parts, 2 * length, width), BF16)],
        scratch_shapes=scratch,
        compiler_params=limit(16),
        name="grad_second",
    )(place, x0, x1, weight, acc, query)


def filtered(taps_ref, stream, ext, begin, length):
    total = taps_ref[stream + 1, 0:1, :] * ext[stream, HALO + begin : HALO + begin + length, :]
    for i in range(1, taps_ref.shape[1]):
        first = HALO + begin - i
        total = total + taps_ref[stream + 1, i : i + 1, :] * ext[stream, first : first + length, :]
    return total


def extend(got_ref, ext):
    parts, rows, width = got_ref.shape
    length = rows // 3
    ext[:, 0:HALO, :] = jnp.zeros((2, HALO, width), F32)
    for s in range(parts):
        here = slice(HALO + s * length, HALO + (s + 1) * length)
        ext[0, here, :] = got_ref[s, 0:length, :].astype(F32)
        ext[1, here, :] = got_ref[s, length : 2 * length, :].astype(F32)


def forward_begin(got_ref, taps_ref, medium_ref, key_ref, value_ref, ext, signals, medium):
    parts, rows, width = got_ref.shape
    length = rows // 3
    extend(got_ref, ext)
    for s in range(parts):
        here = slice(s * length, (s + 1) * length)
        key = filtered(taps_ref, 0, ext, s * length, length)
        value = filtered(taps_ref, 1, ext, s * length, length)
        key_ref[here, :] = key
        value_ref[here, :] = value
        signals[here, 0:width] = (key * value).astype(BF16)
        signals[here, width : 2 * width] = got_ref[s, 2 * length : 3 * length, :]
    medium[...] = jnp.zeros_like(medium)
    medium[0 : medium_ref.shape[0], :] = medium_ref[...].astype(BF16)


def forward_spectra(cosine, sine, signals, medium):
    tokens, double = signals.shape
    width = double // 2
    kept = medium.shape[0]
    both_c = dot(cosine[:, 0:tokens], signals[...])
    both_s = dot(sine[:, 0:tokens], signals[...])
    mc = dot(cosine[:, 0:kept], medium[...])
    ms = dot(sine[:, 0:kept], medium[...])
    ac, hc, as_, hs = (both_c[:, :width], both_c[:, width:], both_s[:, :width], both_s[:, width:])
    xc = ac * mc - as_ * ms
    xs = ac * ms + as_ * mc
    saved = (ac, as_, mc, ms, hc, hs)
    return saved, (xc * hc - xs * hs).astype(BF16), (xc * hs + xs * hc).astype(BF16)


def forward_end(out_ref, acc, freqs):
    parts, length, _ = out_ref.shape
    for s in range(parts):
        first = s * length + 1
        out_ref[s, 0:length, :] = (acc[first : first + length, :] * (1.0 / freqs)).astype(BF16)


def forward_kernel(
    got_ref, taps_ref, medium_ref, cos_ref, sin_ref, cos_across_ref, sin_across_ref, _,
    out_ref, key_ref, value_ref, spectra_ref, ext, signals, medium, acc, *, freqs,
):
    step = pl.program_id(0)

    @pl.when(step == 0)
    def _():
        forward_begin(got_ref, taps_ref, medium_ref, key_ref, value_ref, ext, signals, medium)
        acc[...] = jnp.zeros_like(acc)

    saved, yc, ys = forward_spectra(cos_ref[...], sin_ref[...], signals, medium)
    for i, spectrum in enumerate(saved):
        spectra_ref[i] = spectrum
    rows = acc.shape[0]
    acc[...] += dot(cos_across_ref[0:rows, :], yc) + dot(sin_across_ref[0:rows, :], ys)

    @pl.when(step == pl.num_programs(0) - 1)
    def _():
        forward_end(out_ref, acc, freqs)


def backward_begin(got_ref, grads_ref, delayed, signal, ext):
    parts, rows, _ = got_ref.shape
    length = rows // 3
    delayed[...] = jnp.zeros_like(delayed)
    for s in range(parts):
        delayed[s * length + 1 : (s + 1) * length + 1, :] = grads_ref[s].astype(F32)
    signal[...] = delayed[...].astype(BF16)
    extend(got_ref, ext)


def backward_spectra(cosine, sine, signal, spectra):
    gc = dot(cosine, signal[...])
    gs = dot(sine, signal[...])
    ac, as_, mc, ms, hc, hs = spectra
    uc = hc * gc + hs * gs
    us = hc * gs - hs * gc
    xc = ac * mc - as_ * ms
    xs = ac * ms + as_ * mc
    both_c = jnp.concatenate([xc * gc + xs * gs, mc * uc + ms * us], 1).astype(BF16)
    both_s = jnp.concatenate([xc * gs - xs * gc, mc * us - ms * uc], 1).astype(BF16)
    return both_c, both_s, (ac * uc + as_ * us).astype(BF16), (ac * us - as_ * uc).astype(BF16)


def backward_end(
    taps_ref, query_short_ref, key_ref, value_ref, out_ref, small_ref, ext, after, acc, tap_acc, freqs, scale, medium_reach
):
    parts, _, width = out_ref.shape
    length = (ext.shape[1] - HALO) // parts
    tokens = parts * length
    reach = taps_ref.shape[1]
    inverse = 1.0 / freqs
    small_ref[...] = jnp.zeros_like(small_ref)
    small_ref[0:medium_reach, :] = tap_acc[0:medium_reach, :] * (inverse * scale)
    after[:, tokens : tokens + HALO, :] = jnp.zeros((2, HALO, width), F32)
    for s in range(parts):
        here = slice(s * length, (s + 1) * length)
        out_ref[s, 2 * length : 3 * length, :] = (acc[here, 0:width] * (inverse * scale)).astype(BF16)
        gated = acc[here, width : 2 * width] * inverse
        after[0, here, :] = gated * value_ref[here, :]
        after[1, here, :] = gated * key_ref[here, :]
    for j in range(2):
        sums = [jnp.zeros((8, width), F32) for _ in range(reach)]
        for s in range(parts):
            begin = s * length
            own = after[j, begin : begin + length, :]
            total = taps_ref[j + 1, 0:1, :] * own
            for i in range(reach):
                if i:
                    total = total + taps_ref[j + 1, i : i + 1, :] * after[j, begin + i : begin + i + length, :]
                moved = ext[j, HALO + begin - i : HALO + begin - i + length, :]
                sums[i] = sums[i] + jnp.sum((moved * own).reshape(length // 8, 8, width), 0)
            out_ref[s, j * length : (j + 1) * length, :] = total.astype(BF16)
        for i in range(reach):
            row = medium_reach + j * reach + i
            small_ref[row : row + 1, :] = jnp.sum(sums[i], 0, keepdims=True) * scale
    row = medium_reach + 2 * reach
    small_ref[row : row + query_short_ref.shape[0], :] = query_short_ref[...]
    small = small_ref[...].astype(BF16)
    for s in range(parts):
        out_ref[s, 3 * length :, :] = small


def backward_kernel(
    got_ref, grads_ref, taps_ref, query_short_ref, key_ref, value_ref, spectra_ref,
    cos_ref, sin_ref, cos_across_ref, sin_across_ref,
    out_ref, small, delayed, signal, ext, after, acc, tap_acc, *, freqs, scale, medium_reach,
):
    step = pl.program_id(0)

    @pl.when(step == 0)
    def _():
        backward_begin(got_ref, grads_ref, delayed, signal, ext)
        acc[...] = jnp.zeros_like(acc)
        tap_acc[...] = jnp.zeros_like(tap_acc)

    spectra = [spectra_ref[i] for i in range(spectra_ref.shape[0])]
    size = signal.shape[0]
    both_c, both_s, taps_c, taps_s = backward_spectra(cos_ref[:, 0:size], sin_ref[:, 0:size], signal, spectra)
    rows, kept = (acc.shape[0], tap_acc.shape[0])
    acc[...] += dot(cos_across_ref[0:rows, :], both_c) + dot(sin_across_ref[0:rows, :], both_s)
    tap_acc[...] += dot(cos_across_ref[0:kept, :], taps_c) + dot(sin_across_ref[0:kept, :], taps_s)

    @pl.when(step == pl.num_programs(0) - 1)
    def _():
        backward_end(
            taps_ref, query_short_ref, key_ref, value_ref, out_ref, small, ext, after, acc, tap_acc,
            freqs, scale, medium_reach,
        )


def table_specs(freqs, block):
    rows = pl.BlockSpec((block, freqs), lambda j: (j, 0))
    columns = pl.BlockSpec((freqs, block), lambda j: (0, j))
    return [rows, rows, columns, columns]


def forward_call(got, taps, medium_taps, tables, sent, freqs, block):
    parts, tall, width = got.shape
    length = tall // 3
    tokens = parts * length
    padded = -(-medium_taps.shape[0] // 128) * 128
    timed = jax.ShapeDtypeStruct((tokens, width), F32)
    return pl.pallas_call(
        partial(forward_kernel, freqs=freqs),
        grid=(freqs // block,),
        in_specs=[whole(got.shape), whole(taps.shape), whole(medium_taps.shape)]
        + table_specs(freqs, block)
        + [pl.BlockSpec(memory_space=pl.ANY)],
        out_specs=[
            pl.BlockSpec((parts, length, width), lambda j: (0, 0, 0)),
            whole((tokens, width)),
            whole((tokens, width)),
            pl.BlockSpec((6, block, width), lambda j: (0, j, 0)),
        ],
        out_shape=[
            jax.ShapeDtypeStruct(sent.shape, BF16),
            timed,
            timed,
            jax.ShapeDtypeStruct((6, freqs, width), F32),
        ],
        scratch_shapes=[
            pltpu.VMEM((2, tokens + HALO, width), F32),
            pltpu.VMEM((tokens, 2 * width), BF16),
            pltpu.VMEM((padded, width), BF16),
            pltpu.VMEM((tokens + HALO, width), F32),
        ],
        input_output_aliases={7: 0},
        compiler_params=limit(VMEM_SPECTRAL if freqs * freqs <= TABLE_LIMIT else 60),
        name="forward_spectral",
    )(got, taps, medium_taps, *tables, *tables, sent)


def backward_call(got, grads, taps, query_short, key, value, spectra, tables, freqs, block, scale, medium_reach):
    parts, tall, width = got.shape
    length = tall // 3
    tokens = parts * length
    reach = taps.shape[1]
    padded = -(-medium_reach // 128) * 128
    small = -(-(medium_reach + 2 * reach + query_short.shape[0]) // 16) * 16
    late = -(-(tokens + 1) // 128) * 128
    return pl.pallas_call(
        partial(backward_kernel, freqs=freqs, scale=scale, medium_reach=medium_reach),
        grid=(freqs // block,),
        in_specs=[
            whole(got.shape),
            pl.BlockSpec((parts, length, width), lambda j: (0, 1, 0)),
            whole(taps.shape),
            whole(query_short.shape),
            whole((tokens, width)),
            whole((tokens, width)),
            pl.BlockSpec((6, block, width), lambda j: (0, j, 0)),
        ]
        + table_specs(freqs, block),
        out_specs=whole((parts, tall + small, width)),
        out_shape=jax.ShapeDtypeStruct((parts, tall + small, width), BF16),
        scratch_shapes=[
            pltpu.VMEM((small, width), F32),
            pltpu.VMEM((late, width), F32),
            pltpu.VMEM((late, width), BF16),
            pltpu.VMEM((2, tokens + HALO, width), F32),
            pltpu.VMEM((2, tokens + HALO, width), F32),
            pltpu.VMEM((tokens, 2 * width), F32),
            pltpu.VMEM((padded, width), F32),
        ],
        compiler_params=limit(VMEM_SPECTRAL if freqs * freqs <= TABLE_LIMIT else 60),
        name="backward_spectral",
    )(got, grads, taps, query_short, key, value, spectra, *tables, *tables)


def product_kernel(
    got_ref, query_ref, grad_ref, x_ref, edge_ref, product_ref, query_grad_ref, first_ref, taps_ref, ext, *, reach
):
    parts, length, width = got_ref.shape
    ext[0:HALO, :] = edge_ref[...].astype(F32)
    ext[HALO:, :] = x_ref[0].astype(F32)
    for j in range(parts):
        lanes = slice(j * width, (j + 1) * width)
        convolved = got_ref[j].astype(F32)
        product_ref[:, lanes] = (query_ref[:, lanes] * convolved).astype(BF16)
        own = grad_ref[:, lanes] * convolved
        query_grad_ref[:, lanes] = own
        first_ref[:, lanes] = own[0:HALO].astype(BF16)
        for i in range(reach):
            moved = ext[HALO - i : HALO - i + length, lanes]
            taps_ref[j * reach + i : j * reach + i + 1, :] = jnp.sum(moved * own, 0, keepdims=True)


def project_kernel(place_ref, product_ref, w_ref, sent_ref, kept_ref, buffer, sems, *, flips):
    copies = weight_chunks(place_ref, w_ref, buffer, sems, flips, sent_ref.shape[1])
    for copy in copies:
        copy.start()
    deep = buffer.shape[1]
    per = len(copies) // 2
    for slot, copy in enumerate(copies):
        copy.wait()
        part = lax.dot_general(
            product_ref[...], buffer[slot], (((1,), (1,)), ((), ())), preferred_element_type=F32
        )
        lanes = slice(slot % per * deep, (slot % per + 1) * deep)
        if slot < per:
            sent_ref[:, lanes] = part.astype(sent_ref.dtype)
        else:
            kept_ref[:, lanes] = part


def project(product, weight, place, flips, features):
    length = product.shape[0]
    vmem = pl.BlockSpec(memory_space=pltpu.VMEM)
    return pl.pallas_call(
        partial(project_kernel, flips=flips),
        in_specs=[pl.BlockSpec(memory_space=pltpu.SMEM), vmem, pl.BlockSpec(memory_space=pltpu.HBM)],
        out_specs=[vmem, vmem],
        out_shape=[
            jax.ShapeDtypeStruct((length, features), BF16),
            jax.ShapeDtypeStruct((length, features), F32),
        ],
        scratch_shapes=chunk_scratch(weight, features, 2),
        compiler_params=limit(16),
        name="project",
    )(place, product, weight)


def finish_kernel(
    got_ref, query_grad_ref, next_ref, taps_ref, input_grad_ref, filter_ref, medium_ref, short_ref, ext, *, scale
):
    parts, _, width = got_ref.shape
    length = filter_ref.shape[0]
    reach = taps_ref.shape[1]
    medium_reach = medium_ref.shape[0]
    total = None
    for j in range(parts):
        lanes = slice(j * width, (j + 1) * width)
        input_grad_ref[1, :, lanes] = got_ref[j, 0:length, :]
        input_grad_ref[2, :, lanes] = got_ref[j, length : 2 * length, :]
        filter_ref[:, lanes] = got_ref[j, 2 * length : 3 * length, :].astype(F32)
        small = got_ref[j, 3 * length :, :].astype(F32)
        medium_ref[:, lanes] = small[0:medium_reach, :]
        first = medium_reach + reach
        short_ref[1, :, lanes] = small[medium_reach:first, :]
        short_ref[2, :, lanes] = small[first : first + reach, :]
        sums = small[first + reach : first + reach + parts * reach, :]
        total = sums if total is None else total + sums
    for j in range(parts):
        short_ref[0, :, j * width : (j + 1) * width] = total[j * reach : (j + 1) * reach] * scale
    ext[0:length, :] = query_grad_ref[...]
    ext[length:, :] = next_ref[...].astype(F32)
    total = taps_ref[0, 0:1, :] * ext[0:length, :]
    for i in range(1, reach):
        total = total + taps_ref[0, i : i + 1, :] * ext[i : i + length, :]
    input_grad_ref[0] = total.astype(BF16)


def reshard(value):
    return lax.all_to_all(value, "seq", split_axis=0, concat_axis=0, tiled=True)


def local(inputs, short_taps, medium_taps, long_filter, out_weight, out_cotangent):
    length, groups, channels = inputs.shape
    reach = short_taps.shape[0]
    medium_reach = medium_taps.shape[0]
    parts = lax.axis_size("seq")
    position = lax.axis_index("seq")
    place = lax.axis_index("tensor").astype(jnp.int32)[None]
    features = out_cotangent.shape[1]
    width = channels // parts
    tokens = length * parts
    scale = 1.0 / math.sqrt(tokens)
    freqs, block = spectral_sizes(tokens, medium_reach)
    vmem = pl.BlockSpec(memory_space=pltpu.VMEM)

    weight = pltpu.with_memory_space_constraint(out_weight, pltpu.HBM)
    streams = inputs.transpose(1, 0, 2)
    taps = short_taps.transpose(1, 0, 2)
    query_edge = shift(streams[0, length - HALO :], "seq", 1)
    packed = pl.pallas_call(
        pack_kernel,
        in_specs=[vmem, vmem],
        out_specs=vmem,
        out_shape=jax.ShapeDtypeStruct((parts, 3 * length, width), BF16),
        compiler_params=limit(8),
        name="pack",
    )(streams, long_filter)
    got = reshard(packed)
    packed, cotangent = lax.optimization_barrier((packed, out_cotangent))
    cot_x = exchange(cotangent, "tensor", 2)
    cot_core = exchange(cotangent, "tensor", 1)

    tables = dft_tables(freqs)
    own_taps = lax.dynamic_slice_in_dim(taps, position * width, width, 2)
    own_medium = lax.dynamic_slice_in_dim(medium_taps, position * width, width, 1)

    query = pl.pallas_call(
        query_kernel,
        in_specs=[vmem] * 3,
        out_specs=vmem,
        out_shape=jax.ShapeDtypeStruct((length, channels), F32),
        scratch_shapes=[pltpu.VMEM((length + HALO, channels), F32)],
        compiler_params=limit(8),
        name="query",
    )(streams, query_edge, taps)

    acc = product_grad_of(out_cotangent, cot_core, weight, place, (0, 1))
    cot_far = exchange(cot_x, "tensor", 1)
    product_grad, sent = product_grad_of(cot_x, cot_far, weight, place, (2, 3), acc, query, parts)

    sent, key, value, spectra = forward_call(got, own_taps, own_medium, tables, sent, freqs, block)
    crossed = reshard(sent)

    product, query_grad, first_rows, query_short = pl.pallas_call(
        partial(product_kernel, reach=reach),
        grid=(1,),
        in_specs=[
            pl.BlockSpec((parts, length, width), lambda j: (0, 0, 0)),
            whole((length, channels)),
            whole((length, channels)),
            whole(streams.shape),
            whole((HALO, channels)),
        ],
        out_specs=[
            whole((length, channels)),
            whole((length, channels)),
            whole((HALO, channels)),
            whole((parts * reach, width)),
        ],
        out_shape=[
            jax.ShapeDtypeStruct((length, channels), BF16),
            jax.ShapeDtypeStruct((length, channels), F32),
            jax.ShapeDtypeStruct((HALO, channels), BF16),
            jax.ShapeDtypeStruct((parts * reach, width), F32),
        ],
        scratch_shapes=[pltpu.VMEM((length + HALO, channels), F32)],
        compiler_params=limit(12),
        name="product",
    )(crossed, query, product_grad, streams, query_edge)

    back = backward_call(
        got, crossed, own_taps, query_short, key, value, spectra, tables, freqs, block, scale, medium_reach
    )
    returned = reshard(back)
    back, product = lax.optimization_barrier((back, product))

    far, across = project(product, weight, place, (3, 2), features)
    far_core = exchange(far, "tensor", 1)
    across_sum = exchange((across + far_core.astype(F32)).astype(BF16), "tensor", 2)
    near, own = project(product, weight, place, (1, 0), features)
    near_core = exchange(near, "tensor", 1)

    next_grad = shift(first_rows, "seq", -1)

    input_grad, filter_grad, medium_grad, short_grad = pl.pallas_call(
        partial(finish_kernel, scale=scale),
        in_specs=[vmem] * 4,
        out_specs=[vmem] * 4,
        out_shape=[
            jax.ShapeDtypeStruct((groups, length, channels), BF16),
            jax.ShapeDtypeStruct((length, channels), F32),
            jax.ShapeDtypeStruct((medium_reach, channels), F32),
            jax.ShapeDtypeStruct((groups, reach, channels), F32),
        ],
        scratch_shapes=[pltpu.VMEM((length + HALO, channels), F32)],
        compiler_params=limit(12),
        name="finish",
    )(returned, query_grad, next_grad, taps)

    output = (own + near_core.astype(F32) + across_sum.astype(F32)).astype(BF16)
    return (
        output,
        input_grad.transpose(1, 0, 2),
        filter_grad,
        medium_grad,
        short_grad.transpose(1, 0, 2),
    )


def solution(mesh):
    return jax.shard_map(
        local,
        mesh=mesh,
        in_specs=(
            P("seq", None, "tensor"),
            P(None, None, "tensor"),
            P(None, "tensor"),
            P("seq", "tensor"),
            P(None, "tensor"),
            P("seq", "tensor"),
        ),
        out_specs=(
            P("seq", "tensor"),
            P("seq", None, "tensor"),
            P("seq", "tensor"),
            P(None, "tensor"),
            P(None, None, "tensor"),
        ),
        check_vma=False,
    )
```

```python
import math
from functools import partial

import jax
import jax.numpy as jnp
from jax import lax
from jax.experimental import pallas as pl
from jax.experimental.pallas import tpu as pltpu
from jax.sharding import PartitionSpec as P


F32 = jnp.float32
BF16 = jnp.bfloat16
HALO = 8
GROUP = 32
CHUNK = 512
TABLE_LIMIT = 1 << 22


def dot(a, b):
    return lax.dot_general(a, b, (((1,), (0,)), ((), ())), preferred_element_type=F32)


def exchange(value, axis, flip):
    count = lax.axis_size(axis)
    return lax.ppermute(value, axis, [(source, source ^ flip) for source in range(count)])


def shift(value, axis, steps):
    count = lax.axis_size(axis)
    pairs = [(s, s + steps) for s in range(count) if 0 <= s + steps < count]
    return lax.ppermute(value, axis, pairs)


def whole(shape):
    return pl.BlockSpec(shape, lambda *_: (0,) * len(shape))


def spectral_sizes(tokens, medium_reach):
    need = tokens + -(-(medium_reach - 2) // 2)
    freqs = -(-need // 384) * 384
    return freqs, 384


def dft_tables(freqs):
    period = 8 * freqs
    unit = 2.0 * math.pi / period
    odd = 2 * jnp.arange(freqs, dtype=jnp.int32) + 1
    start = 2 * GROUP * jnp.arange(freqs // GROUP, dtype=jnp.int32)
    inner = 2 * jnp.arange(GROUP, dtype=jnp.int32) + 1
    first = (start[:, None] * odd[None, :] % period).astype(F32) * unit
    second = (inner[:, None] * odd[None, :] % period).astype(F32) * unit
    fc, fs = jnp.cos(first)[:, None], jnp.sin(first)[:, None]
    sc, ss = jnp.cos(second)[None], jnp.sin(second)[None]
    cosine = (fc * sc - fs * ss).astype(BF16).reshape(freqs, freqs)
    sine = (fs * sc + fc * ss).astype(BF16).reshape(freqs, freqs)
    return cosine, sine


def limit(mebibytes):
    return pltpu.CompilerParams(vmem_limit_bytes=mebibytes << 20)


def pack_kernel(x_ref, filter_ref, out_ref, streams, taps, rounded, sems):
    parts, rows, width = out_ref.shape
    length = rows // 3
    read_filter = pltpu.make_async_copy(filter_ref, taps, sems.at[0])
    read_streams = pltpu.make_async_copy(x_ref.at[pl.ds(1, 2)], streams, sems.at[1])
    read_filter.start()
    read_streams.start()
    read_filter.wait()
    for j in range(parts):
        rounded[j, 2 * length :, :] = taps[:, j * width : (j + 1) * width].astype(BF16)
    read_streams.wait()
    writes = []
    for j in range(parts):
        lanes = slice(j * width, (j + 1) * width)
        rounded[j, 0:length, :] = streams[0, :, lanes]
        rounded[j, length : 2 * length, :] = streams[1, :, lanes]
        writes.append(pltpu.make_async_copy(rounded.at[j], out_ref.at[j], sems.at[2 + j]))
        writes[j].start()
    for write in writes:
        write.wait()


def weight_chunks(place_ref, weight_ref, buffer, sems, flips, features):
    deep = buffer.shape[1]
    per = features // deep
    copies = []
    for i, flip in enumerate(flips):
        for k in range(per):
            start = jnp.bitwise_xor(place_ref[0], flip) * features + k * deep
            slot = i * per + k
            copies.append(
                pltpu.make_async_copy(
                    weight_ref.at[pl.ds(pl.multiple_of(start, deep), deep), :], buffer.at[slot], sems.at[slot]
                )
            )
    return copies


def chunk_scratch(weight, features, shards):
    deep = math.gcd(features, CHUNK)
    count = shards * (features // deep)
    return [pltpu.VMEM((count, deep, weight.shape[1]), weight.dtype), pltpu.SemaphoreType.DMA((count,))]


def summed(x_refs, copies, buffer, total):
    deep = buffer.shape[1]
    per = len(copies) // len(x_refs)
    for slot, copy in enumerate(copies):
        copy.wait()
        lanes = slice(slot % per * deep, (slot % per + 1) * deep)
        part = dot(x_refs[slot // per][:, lanes], buffer[slot])
        total = part if total is None else total + part
    return total


def product_grad_kernel(place_ref, w_ref, *refs, flips, added):
    x_refs = refs[: len(flips)]
    out_ref, buffer, sems = refs[-3:]
    copies = weight_chunks(place_ref, w_ref, buffer, sems, flips, x_refs[0].shape[1])
    for copy in copies:
        copy.start()
    out_ref[...] = summed(x_refs, copies, buffer, refs[len(flips)][...] if added else None)


def product_grad_of(shards, weight, place, flips, acc=None, out_memory=None):
    length, features = shards[0].shape
    channels = weight.shape[1]
    vmem = pl.BlockSpec(memory_space=pltpu.VMEM)
    extra = [] if acc is None else [acc]
    make = out_memory or jax.ShapeDtypeStruct
    return pl.pallas_call(
        partial(product_grad_kernel, flips=flips, added=bool(extra)),
        in_specs=[pl.BlockSpec(memory_space=pltpu.SMEM), pl.BlockSpec(memory_space=pltpu.HBM)]
        + [vmem] * (len(shards) + len(extra)),
        out_specs=vmem,
        out_shape=make((length, channels), F32),
        scratch_shapes=chunk_scratch(weight, features, len(flips)),
        compiler_params=limit(16),
        name="product_grad",
    )(place, weight, *shards, *extra)


def filtered(taps_ref, stream, ext, begin, length):
    total = taps_ref[stream + 1, 0:1, :] * ext[stream, HALO + begin : HALO + begin + length, :]
    for i in range(1, taps_ref.shape[1]):
        first = HALO + begin - i
        total = total + taps_ref[stream + 1, i : i + 1, :] * ext[stream, first : first + length, :]
    return total


def extend(got_ref, ext):
    parts, rows, width = got_ref.shape
    length = rows // 3
    ext[:, 0:HALO, :] = jnp.zeros((2, HALO, width), F32)
    for s in range(parts):
        here = slice(HALO + s * length, HALO + (s + 1) * length)
        ext[0, here, :] = got_ref[s, 0:length, :].astype(F32)
        ext[1, here, :] = got_ref[s, length : 2 * length, :].astype(F32)


def forward_begin(got_ref, taps_ref, medium_ref, key_ref, value_ref, ext, signals, medium):
    parts, rows, width = got_ref.shape
    length = rows // 3
    extend(got_ref, ext)
    for s in range(parts):
        here = slice(s * length, (s + 1) * length)
        key = filtered(taps_ref, 0, ext, s * length, length)
        value = filtered(taps_ref, 1, ext, s * length, length)
        key_ref[here, :] = key
        value_ref[here, :] = value
        signals[here, 0:width] = (key * value).astype(BF16)
        signals[here, width : 2 * width] = got_ref[s, 2 * length : 3 * length, :]
    medium[...] = jnp.zeros_like(medium)
    medium[0 : medium_ref.shape[0], :] = medium_ref[...].astype(BF16)


def forward_spectra(cosine, sine, signals, medium):
    tokens, double = signals.shape
    width = double // 2
    kept = medium.shape[0]
    both_c = dot(cosine[:, 0:tokens], signals[...])
    both_s = dot(sine[:, 0:tokens], signals[...])
    mc = dot(cosine[:, 0:kept], medium[...])
    ms = dot(sine[:, 0:kept], medium[...])
    ac, hc, as_, hs = (both_c[:, :width], both_c[:, width:], both_s[:, :width], both_s[:, width:])
    xc = ac * mc - as_ * ms
    xs = ac * ms + as_ * mc
    saved = (ac, as_, mc, ms, hc, hs)
    return saved, (xc * hc - xs * hs).astype(BF16), (xc * hs + xs * hc).astype(BF16)


def forward_end(out_ref, acc, freqs):
    parts, length, _ = out_ref.shape
    for s in range(parts):
        first = s * length + 1
        out_ref[s] = (acc[first : first + length, :] * (1.0 / freqs)).astype(BF16)


def query_part(x_ref, edge_ref, taps_ref, grad_ref, query_ref, out_ref, own):
    parts, rows, width = out_ref.shape
    length = rows // 2
    own[0:HALO, :] = edge_ref[...].astype(F32)
    own[HALO:, :] = x_ref[0].astype(F32)
    for j in range(parts):
        lanes = slice(j * width, (j + 1) * width)
        query = taps_ref[0, 0:1, lanes] * own[HALO : HALO + length, lanes]
        for i in range(1, taps_ref.shape[1]):
            query = query + taps_ref[0, i : i + 1, lanes] * own[HALO - i : HALO - i + length, lanes]
        query_ref[:, lanes] = query
        out_ref[j, length:, :] = (grad_ref[:, lanes] * query).astype(BF16)


def table_copies(tables, held, sems, blocks):
    size = held.shape[1] // blocks
    return [
        [
            pltpu.make_async_copy(
                table.at[pl.ds(b * size, size), :], held.at[i, pl.ds(b * size, size), :], sems.at[i, b]
            )
            for i, table in enumerate(tables)
        ]
        for b in range(blocks)
    ]


def forward_kernel(
    got_ref, x_ref, edge_ref, all_taps_ref, grad_ref, taps_ref, medium_ref, cos_ref, sin_ref, *refs, freqs, block,
    resident,
):
    if not resident:
        cos_across_ref, sin_across_ref, *refs = refs
    out_ref, query_ref, key_ref, value_ref, spectra_ref, ext, signals, medium, acc, own, *refs = refs
    rows = acc.shape[0]
    step = pl.program_id(0)
    length = x_ref.shape[1]
    half = out_ref.at[:, pl.ds(0, length), :]

    def begin():
        forward_begin(got_ref, taps_ref, medium_ref, key_ref, value_ref, ext, signals, medium)
        query_part(x_ref, edge_ref, all_taps_ref, grad_ref, query_ref, out_ref, own)

    if resident:
        held, yc_all, ys_all, sems = refs
        copies = table_copies((cos_ref, sin_ref), held, sems, freqs // block)
        for pair in copies:
            for copy in pair:
                copy.start()
        begin()
        for b, pair in enumerate(copies):
            for copy in pair:
                copy.wait()
            here = slice(b * block, (b + 1) * block)
            saved, yc, ys = forward_spectra(held[0, here, :], held[1, here, :], signals, medium)
            for i, spectrum in enumerate(saved):
                spectra_ref[i, here, :] = spectrum
            yc_all[here, :] = yc
            ys_all[here, :] = ys
        acc[...] = dot(held[0, 0:rows, :], yc_all[...]) + dot(held[1, 0:rows, :], ys_all[...])
        forward_end(half, acc, freqs)
        return

    @pl.when(step == 0)
    def _():
        begin()
        acc[...] = jnp.zeros_like(acc)

    saved, yc, ys = forward_spectra(cos_ref[...], sin_ref[...], signals, medium)
    for i, spectrum in enumerate(saved):
        spectra_ref[i] = spectrum
    acc[...] += dot(cos_across_ref[0:rows, :], yc) + dot(sin_across_ref[0:rows, :], ys)

    @pl.when(step == pl.num_programs(0) - 1)
    def _():
        forward_end(half, acc, freqs)


def backward_begin(got_ref, grads_ref, delayed, signal, ext):
    parts, rows, _ = got_ref.shape
    length = rows // 3
    delayed[...] = jnp.zeros_like(delayed)
    for s in range(parts):
        delayed[s * length + 1 : (s + 1) * length + 1, :] = grads_ref[s].astype(F32)
    signal[...] = delayed[...].astype(BF16)
    extend(got_ref, ext)


def backward_spectra(cosine, sine, signal, spectra):
    gc = dot(cosine, signal[...])
    gs = dot(sine, signal[...])
    ac, as_, mc, ms, hc, hs = spectra
    uc = hc * gc + hs * gs
    us = hc * gs - hs * gc
    xc = ac * mc - as_ * ms
    xs = ac * ms + as_ * mc
    both_c = jnp.concatenate([xc * gc + xs * gs, mc * uc + ms * us], 1).astype(BF16)
    both_s = jnp.concatenate([xc * gs - xs * gc, mc * us - ms * uc], 1).astype(BF16)
    return both_c, both_s, (ac * uc + as_ * us).astype(BF16), (ac * us - as_ * uc).astype(BF16)


def backward_end(
    taps_ref, query_short_ref, key_ref, value_ref, out_ref, small_ref, ext, after, acc, tap_acc, freqs, scale, medium_reach
):
    parts, _, width = out_ref.shape
    length = (ext.shape[1] - HALO) // parts
    tokens = parts * length
    reach = taps_ref.shape[1]
    inverse = 1.0 / freqs
    small_ref[...] = jnp.zeros_like(small_ref)
    small_ref[0:medium_reach, :] = tap_acc[0:medium_reach, :] * (inverse * scale)
    after[:, tokens : tokens + HALO, :] = jnp.zeros((2, HALO, width), F32)
    for s in range(parts):
        here = slice(s * length, (s + 1) * length)
        out_ref[s, 2 * length : 3 * length, :] = (acc[here, 0:width] * (inverse * scale)).astype(BF16)
        gated = acc[here, width : 2 * width] * inverse
        after[0, here, :] = gated * value_ref[here, :]
        after[1, here, :] = gated * key_ref[here, :]
    for j in range(2):
        sums = [jnp.zeros((8, width), F32) for _ in range(reach)]
        for s in range(parts):
            begin = s * length
            own = after[j, begin : begin + length, :]
            total = taps_ref[j + 1, 0:1, :] * own
            for i in range(reach):
                if i:
                    total = total + taps_ref[j + 1, i : i + 1, :] * after[j, begin + i : begin + i + length, :]
                moved = ext[j, HALO + begin - i : HALO + begin - i + length, :]
                sums[i] = sums[i] + jnp.sum((moved * own).reshape(length // 8, 8, width), 0)
            out_ref[s, j * length : (j + 1) * length, :] = total.astype(BF16)
        for i in range(reach):
            row = medium_reach + j * reach + i
            small_ref[row : row + 1, :] = jnp.sum(sums[i], 0, keepdims=True) * scale
    row = medium_reach + 2 * reach
    small_ref[row : row + query_short_ref.shape[0], :] = query_short_ref[...]
    small = small_ref[...].astype(BF16)
    for s in range(parts):
        out_ref[s, 3 * length :, :] = small


def backward_kernel(
    got_ref, grads_ref, taps_ref, query_short_ref, key_ref, value_ref, spectra_ref, cos_ref, sin_ref, *refs,
    freqs, block, scale, medium_reach, resident,
):
    if not resident:
        cos_across_ref, sin_across_ref, *refs = refs
    out_ref, small, delayed, signal, ext, after, acc, tap_acc, *refs = refs
    step = pl.program_id(0)
    size = signal.shape[0]
    rows, kept = (acc.shape[0], tap_acc.shape[0])

    def end():
        backward_end(
            taps_ref, query_short_ref, key_ref, value_ref, out_ref, small, ext, after, acc, tap_acc,
            freqs, scale, medium_reach,
        )

    if resident:
        held, both_c_all, both_s_all, taps_c_all, taps_s_all, sems = refs
        copies = table_copies((cos_ref, sin_ref), held, sems, freqs // block)
        for pair in copies:
            for copy in pair:
                copy.start()
        backward_begin(got_ref, grads_ref, delayed, signal, ext)
        for b, pair in enumerate(copies):
            for copy in pair:
                copy.wait()
            here = slice(b * block, (b + 1) * block)
            spectra = [spectra_ref[i, here, :] for i in range(spectra_ref.shape[0])]
            both_c_all[here, :], both_s_all[here, :], taps_c_all[here, :], taps_s_all[here, :] = backward_spectra(
                held[0, here, 0:size], held[1, here, 0:size], signal, spectra
            )
        acc[...] = dot(held[0, 0:rows, :], both_c_all[...]) + dot(held[1, 0:rows, :], both_s_all[...])
        tap_acc[...] = dot(held[0, 0:kept, :], taps_c_all[...]) + dot(held[1, 0:kept, :], taps_s_all[...])
        end()
        return

    @pl.when(step == 0)
    def _():
        backward_begin(got_ref, grads_ref, delayed, signal, ext)
        acc[...] = jnp.zeros_like(acc)
        tap_acc[...] = jnp.zeros_like(tap_acc)

    spectra = [spectra_ref[i] for i in range(spectra_ref.shape[0])]
    both_c, both_s, taps_c, taps_s = backward_spectra(cos_ref[:, 0:size], sin_ref[:, 0:size], signal, spectra)
    acc[...] += dot(cos_across_ref[0:rows, :], both_c) + dot(sin_across_ref[0:rows, :], both_s)
    tap_acc[...] += dot(cos_across_ref[0:kept, :], taps_c) + dot(sin_across_ref[0:kept, :], taps_s)
    pl.when(step == pl.num_programs(0) - 1)(end)


def spectral_plan(freqs, block, tables):
    if freqs * freqs <= TABLE_LIMIT:
        hbm = pl.BlockSpec(memory_space=pltpu.HBM)
        return True, 1, [hbm, hbm], [pltpu.with_memory_space_constraint(t, pltpu.HBM) for t in tables]
    rows = pl.BlockSpec((block, freqs), lambda j: (j, 0))
    columns = pl.BlockSpec((freqs, block), lambda j: (0, j))
    return False, freqs // block, [rows, rows, columns, columns], [*tables, *tables]


def held_scratch(freqs, block, widths):
    return (
        [pltpu.VMEM((2, freqs, freqs), BF16)]
        + [pltpu.VMEM((freqs, width), BF16) for width in widths]
        + [pltpu.SemaphoreType.DMA((2, freqs // block))]
    )


def forward_call(got, streams, edge, all_taps, grad, taps, medium_taps, tables, freqs, block):
    parts, tall, width = got.shape
    length = tall // 3
    tokens = parts * length
    channels = parts * width
    padded = -(-medium_taps.shape[0] // 128) * 128
    timed = jax.ShapeDtypeStruct((tokens, width), F32)
    resident, steps, specs, operands = spectral_plan(freqs, block, tables)
    per = freqs // steps
    return pl.pallas_call(
        partial(forward_kernel, freqs=freqs, block=block, resident=resident),
        grid=(steps,),
        in_specs=[
            whole(got.shape),
            whole((1, length, channels)),
            whole(edge.shape),
            whole(all_taps.shape),
            whole(grad.shape),
            whole(taps.shape),
            whole(medium_taps.shape),
        ]
        + specs,
        out_specs=[
            whole((parts, 2 * length, width)),
            whole((length, channels)),
            whole((tokens, width)),
            whole((tokens, width)),
            pl.BlockSpec((6, per, width), lambda j: (0, j, 0)),
        ],
        out_shape=[
            jax.ShapeDtypeStruct((parts, 2 * length, width), BF16),
            jax.ShapeDtypeStruct((length, channels), F32),
            timed,
            timed,
            jax.ShapeDtypeStruct((6, freqs, width), F32),
        ],
        scratch_shapes=[
            pltpu.VMEM((2, tokens + HALO, width), F32),
            pltpu.VMEM((tokens, 2 * width), BF16),
            pltpu.VMEM((padded, width), BF16),
            pltpu.VMEM((tokens + HALO, width), F32),
            pltpu.VMEM((length + HALO, channels), F32),
        ]
        + (held_scratch(freqs, block, (width, width)) if resident else []),
        compiler_params=limit(32 if resident else 60),
        name="forward_spectral",
    )(got, streams, edge, all_taps, grad, taps, medium_taps, *operands)


def backward_call(got, grads, taps, query_short, key, value, spectra, tables, freqs, block, scale, medium_reach):
    parts, tall, width = got.shape
    length = tall // 3
    tokens = parts * length
    reach = taps.shape[1]
    padded = -(-medium_reach // 128) * 128
    small = -(-(medium_reach + 2 * reach + query_short.shape[0]) // 16) * 16
    late = -(-(tokens + 1) // 128) * 128
    resident, steps, specs, operands = spectral_plan(freqs, block, tables)
    per = freqs // steps
    return pl.pallas_call(
        partial(
            backward_kernel, freqs=freqs, block=block, scale=scale, medium_reach=medium_reach, resident=resident
        ),
        grid=(steps,),
        in_specs=[
            whole(got.shape),
            pl.BlockSpec((parts, length, width), lambda j: (0, 1, 0)),
            whole(taps.shape),
            whole(query_short.shape),
            whole((tokens, width)),
            whole((tokens, width)),
            pl.BlockSpec((6, per, width), lambda j: (0, j, 0)),
        ]
        + specs,
        out_specs=whole((parts, tall + small, width)),
        out_shape=pltpu.HBM((parts, tall + small, width), BF16),
        scratch_shapes=[
            pltpu.VMEM((small, width), F32),
            pltpu.VMEM((late, width), F32),
            pltpu.VMEM((late, width), BF16),
            pltpu.VMEM((2, tokens + HALO, width), F32),
            pltpu.VMEM((2, tokens + HALO, width), F32),
            pltpu.VMEM((tokens, 2 * width), F32),
            pltpu.VMEM((padded, width), F32),
        ]
        + (held_scratch(freqs, block, (2 * width, 2 * width, width, width)) if resident else []),
        compiler_params=limit(32 if resident else 60),
        name="backward_spectral",
    )(got, grads, taps, query_short, key, value, spectra, *operands)


def product_kernel(
    got_ref, query_ref, grad_ref, x_ref, edge_ref, product_ref, query_grad_ref, first_ref, taps_ref, ext, *, reach
):
    parts, length, width = got_ref.shape
    ext[0:HALO, :] = edge_ref[...].astype(F32)
    ext[HALO:, :] = x_ref[0].astype(F32)
    for j in range(parts):
        lanes = slice(j * width, (j + 1) * width)
        convolved = got_ref[j].astype(F32)
        product_ref[:, lanes] = (query_ref[:, lanes] * convolved).astype(BF16)
        own = grad_ref[:, lanes] * convolved
        query_grad_ref[:, lanes] = own
        first_ref[:, lanes] = own[0:HALO].astype(BF16)
        for i in range(reach):
            moved = ext[HALO - i : HALO - i + length, lanes]
            taps_ref[j * reach + i : j * reach + i + 1, :] = jnp.sum(moved * own, 0, keepdims=True)


def project_kernel(place_ref, product_ref, w_ref, sent_ref, kept_ref, buffer, sems, *, flips):
    copies = weight_chunks(place_ref, w_ref, buffer, sems, flips, sent_ref.shape[1])
    for copy in copies:
        copy.start()
    deep = buffer.shape[1]
    per = len(copies) // 2
    for slot, copy in enumerate(copies):
        copy.wait()
        part = lax.dot_general(
            product_ref[...], buffer[slot], (((1,), (1,)), ((), ())), preferred_element_type=F32
        )
        lanes = slice(slot % per * deep, (slot % per + 1) * deep)
        if slot < per:
            sent_ref[:, lanes] = part.astype(sent_ref.dtype)
        else:
            kept_ref[:, lanes] = part


def project(product, weight, place, flips, features):
    length = product.shape[0]
    vmem = pl.BlockSpec(memory_space=pltpu.VMEM)
    return pl.pallas_call(
        partial(project_kernel, flips=flips),
        in_specs=[pl.BlockSpec(memory_space=pltpu.SMEM), vmem, pl.BlockSpec(memory_space=pltpu.HBM)],
        out_specs=[vmem, vmem],
        out_shape=[
            jax.ShapeDtypeStruct((length, features), BF16),
            jax.ShapeDtypeStruct((length, features), F32),
        ],
        scratch_shapes=chunk_scratch(weight, features, 2),
        compiler_params=limit(16),
        name="project",
    )(place, product, weight)


def finish_kernel(
    got_ref, query_grad_ref, next_ref, taps_ref, input_grad_ref, filter_ref, medium_ref, short_ref, ext, *, scale
):
    parts, _, width = got_ref.shape
    length = filter_ref.shape[0]
    reach = taps_ref.shape[1]
    medium_reach = medium_ref.shape[0]
    total = None
    for j in range(parts):
        lanes = slice(j * width, (j + 1) * width)
        input_grad_ref[1, :, lanes] = got_ref[j, 0:length, :]
        input_grad_ref[2, :, lanes] = got_ref[j, length : 2 * length, :]
        filter_ref[:, lanes] = got_ref[j, 2 * length : 3 * length, :].astype(F32)
        small = got_ref[j, 3 * length :, :].astype(F32)
        medium_ref[:, lanes] = small[0:medium_reach, :]
        first = medium_reach + reach
        short_ref[1, :, lanes] = small[medium_reach:first, :]
        short_ref[2, :, lanes] = small[first : first + reach, :]
        sums = small[first + reach : first + reach + parts * reach, :]
        total = sums if total is None else total + sums
    for j in range(parts):
        short_ref[0, :, j * width : (j + 1) * width] = total[j * reach : (j + 1) * reach] * scale
    ext[0:length, :] = query_grad_ref[...]
    ext[length:, :] = next_ref[...].astype(F32)
    total = taps_ref[0, 0:1, :] * ext[0:length, :]
    for i in range(1, reach):
        total = total + taps_ref[0, i : i + 1, :] * ext[i : i + length, :]
    input_grad_ref[0] = total.astype(BF16)


def reshard(value):
    return lax.all_to_all(value, "seq", split_axis=0, concat_axis=0, tiled=True)


def local(inputs, short_taps, medium_taps, long_filter, out_weight, out_cotangent):
    length, groups, channels = inputs.shape
    reach = short_taps.shape[0]
    medium_reach = medium_taps.shape[0]
    parts = lax.axis_size("seq")
    position = lax.axis_index("seq")
    place = lax.axis_index("tensor").astype(jnp.int32)[None]
    features = out_cotangent.shape[1]
    width = channels // parts
    tokens = length * parts
    scale = 1.0 / math.sqrt(tokens)
    freqs, block = spectral_sizes(tokens, medium_reach)
    vmem = pl.BlockSpec(memory_space=pltpu.VMEM)

    weight = pltpu.with_memory_space_constraint(out_weight, pltpu.HBM)
    streams = inputs.transpose(1, 0, 2)
    taps = short_taps.transpose(1, 0, 2)
    hbm = pl.BlockSpec(memory_space=pltpu.HBM)
    packed = pl.pallas_call(
        pack_kernel,
        in_specs=[hbm, hbm],
        out_specs=hbm,
        out_shape=pltpu.HBM((parts, 3 * length, width), BF16),
        scratch_shapes=[
            pltpu.VMEM((2, length, channels), BF16),
            pltpu.VMEM((length, channels), F32),
            pltpu.VMEM((parts, 3 * length, width), BF16),
            pltpu.SemaphoreType.DMA((2 + parts,)),
        ],
        compiler_params=limit(8),
        name="pack",
    )(
        pltpu.with_memory_space_constraint(streams, pltpu.HBM),
        pltpu.with_memory_space_constraint(long_filter, pltpu.HBM),
    )
    got = reshard(packed)
    query_edge = shift(streams[0, length - HALO :], "seq", 1)
    cot_x = exchange(out_cotangent, "tensor", 2)
    cot_core = exchange(out_cotangent, "tensor", 1)

    tables = dft_tables(freqs)
    own_taps = lax.dynamic_slice_in_dim(taps, position * width, width, 2)
    own_medium = lax.dynamic_slice_in_dim(medium_taps, position * width, width, 1)

    acc = product_grad_of((out_cotangent, cot_core), weight, place, (0, 1))
    cot_far = exchange(cot_x, "tensor", 1)
    acc = product_grad_of((cot_x,), weight, place, (2,), acc)
    product_grad = product_grad_of((cot_far,), weight, place, (3,), acc, pltpu.HBM)
    product_grad = pltpu.with_memory_space_constraint(product_grad, pltpu.HBM)

    sent, query, key, value, spectra = forward_call(
        got, streams, query_edge, taps, product_grad, own_taps, own_medium, tables, freqs, block
    )
    crossed = reshard(sent)

    product, query_grad, first_rows, query_short = pl.pallas_call(
        partial(product_kernel, reach=reach),
        grid=(1,),
        in_specs=[
            pl.BlockSpec((parts, length, width), lambda j: (0, 0, 0)),
            whole((length, channels)),
            whole((length, channels)),
            whole(streams.shape),
            whole((HALO, channels)),
        ],
        out_specs=[
            whole((length, channels)),
            whole((length, channels)),
            whole((HALO, channels)),
            whole((parts * reach, width)),
        ],
        out_shape=[
            jax.ShapeDtypeStruct((length, channels), BF16),
            pltpu.HBM((length, channels), F32),
            jax.ShapeDtypeStruct((HALO, channels), BF16),
            jax.ShapeDtypeStruct((parts * reach, width), F32),
        ],
        scratch_shapes=[pltpu.VMEM((length + HALO, channels), F32)],
        compiler_params=limit(12),
        name="product",
    )(crossed, query, product_grad, streams, query_edge)

    back = backward_call(
        got, crossed, own_taps, query_short, key, value, spectra, tables, freqs, block, scale, medium_reach
    )
    returned = reshard(back)
    back, product = lax.optimization_barrier((back, product))

    far, across = project(product, weight, place, (3, 2), features)
    far_core = exchange(far, "tensor", 1)
    across_sum = exchange((across + far_core.astype(F32)).astype(BF16), "tensor", 2)
    near, own = project(product, weight, place, (1, 0), features)
    near_core = exchange(near, "tensor", 1)

    next_grad = shift(first_rows, "seq", -1)

    input_grad, filter_grad, medium_grad, short_grad = pl.pallas_call(
        partial(finish_kernel, scale=scale),
        in_specs=[vmem] * 4,
        out_specs=[vmem] * 4,
        out_shape=[
            jax.ShapeDtypeStruct((groups, length, channels), BF16),
            jax.ShapeDtypeStruct((length, channels), F32),
            jax.ShapeDtypeStruct((medium_reach, channels), F32),
            jax.ShapeDtypeStruct((groups, reach, channels), F32),
        ],
        scratch_shapes=[pltpu.VMEM((length + HALO, channels), F32)],
        compiler_params=limit(12),
        name="finish",
    )(returned, query_grad, next_grad, taps)

    output = (own + near_core.astype(F32) + across_sum.astype(F32)).astype(BF16)
    return (
        output,
        input_grad.transpose(1, 0, 2),
        filter_grad,
        medium_grad,
        short_grad.transpose(1, 0, 2),
    )


def solution(mesh):
    return jax.shard_map(
        local,
        mesh=mesh,
        in_specs=(
            P("seq", None, "tensor"),
            P(None, None, "tensor"),
            P(None, "tensor"),
            P("seq", "tensor"),
            P(None, "tensor"),
            P("seq", "tensor"),
        ),
        out_specs=(
            P("seq", "tensor"),
            P("seq", None, "tensor"),
            P("seq", "tensor"),
            P(None, "tensor"),
            P(None, None, "tensor"),
        ),
        check_vma=False,
    )
```

```python
import math
from functools import partial

import jax
import jax.numpy as jnp
from jax import lax
from jax.experimental import pallas as pl
from jax.experimental.pallas import tpu as pltpu
from jax.sharding import PartitionSpec as P


F32 = jnp.float32
BF16 = jnp.bfloat16
HALO = 8
GROUP = 32
LANES = 128
CHUNK = 512
TABLE_LIMIT = 1 << 22


def dot(a, b):
    return lax.dot_general(a, b, (((1,), (0,)), ((), ())), preferred_element_type=F32)


def exchange(value, axis, flip):
    count = lax.axis_size(axis)
    return lax.ppermute(value, axis, [(source, source ^ flip) for source in range(count)])


def shift(value, axis, steps):
    count = lax.axis_size(axis)
    pairs = [(s, s + steps) for s in range(count) if 0 <= s + steps < count]
    return lax.ppermute(value, axis, pairs)


def whole(shape):
    return pl.BlockSpec(shape, lambda *_: (0,) * len(shape))


def spectral_sizes(tokens, medium_reach):
    need = tokens + -(-(medium_reach - 2) // 2)
    freqs = -(-need // 384) * 384
    return freqs, 384


def dft_tables(freqs):
    period = 8 * freqs
    unit = 2.0 * math.pi / period
    odd = 2 * jnp.arange(freqs, dtype=jnp.int32) + 1
    start = 2 * GROUP * jnp.arange(freqs // GROUP, dtype=jnp.int32)
    inner = 2 * jnp.arange(GROUP, dtype=jnp.int32) + 1
    first = (start[:, None] * odd[None, :] % period).astype(F32) * unit
    second = (inner[:, None] * odd[None, :] % period).astype(F32) * unit
    fc, fs = jnp.cos(first)[:, None], jnp.sin(first)[:, None]
    sc, ss = jnp.cos(second)[None], jnp.sin(second)[None]
    cosine = (fc * sc - fs * ss).astype(BF16).reshape(freqs, freqs)
    sine = (fs * sc + fc * ss).astype(BF16).reshape(freqs, freqs)
    return cosine, sine


def in_hbm(value):
    return pltpu.with_memory_space_constraint(value, pltpu.HBM)


def limit(mebibytes):
    return pltpu.CompilerParams(vmem_limit_bytes=mebibytes << 20)


def pack_kernel(x_ref, filter_ref, out_ref, streams, taps, rounded, sems):
    parts, rows, width = out_ref.shape
    length = rows // 3
    read_filter = pltpu.make_async_copy(filter_ref, taps, sems.at[0])
    read_streams = pltpu.make_async_copy(x_ref.at[pl.ds(1, 2)], streams, sems.at[1])
    read_filter.start()
    read_streams.start()
    read_filter.wait()
    for j in range(parts):
        rounded[j, 2 * length :, :] = taps[:, j * width : (j + 1) * width].astype(BF16)
    read_streams.wait()
    writes = []
    for j in range(parts):
        lanes = slice(j * width, (j + 1) * width)
        rounded[j, 0:length, :] = streams[0, :, lanes]
        rounded[j, length : 2 * length, :] = streams[1, :, lanes]
        writes.append(pltpu.make_async_copy(rounded.at[j], out_ref.at[j], sems.at[2 + j]))
        writes[j].start()
    for write in writes:
        write.wait()


def weight_chunks(place_ref, weight_ref, buffer, sems, flips, features):
    deep = buffer.shape[1]
    per = features // deep
    copies = []
    for i, flip in enumerate(flips):
        for k in range(per):
            start = jnp.bitwise_xor(place_ref[0], flip) * features + k * deep
            slot = i * per + k
            copies.append(
                pltpu.make_async_copy(
                    weight_ref.at[pl.ds(pl.multiple_of(start, deep), deep), :], buffer.at[slot], sems.at[slot]
                )
            )
    return copies


def chunk_scratch(weight, features, shards):
    deep = math.gcd(features, CHUNK)
    count = shards * (features // deep)
    return [pltpu.VMEM((count, deep, weight.shape[1]), weight.dtype), pltpu.SemaphoreType.DMA((count,))]


def summed(x_refs, copies, buffer, total):
    deep = buffer.shape[1]
    per = len(copies) // len(x_refs)
    for slot, copy in enumerate(copies):
        copy.wait()
        lanes = slice(slot % per * deep, (slot % per + 1) * deep)
        part = dot(x_refs[slot // per][:, lanes], buffer[slot])
        total = part if total is None else total + part
    return total


def product_grad_kernel(place_ref, w_ref, *refs, flips, last):
    x_refs = refs[: len(flips)]
    copies_in = []
    if last:
        acc_ref, x_ref, taps_ref, out_ref, query_ref, sent_ref, buffer, sems, ext, held, in_sems = refs[len(flips) :]
    else:
        out_ref, buffer, sems, held, in_sems = refs[len(flips) :]
    for i, ref in enumerate(x_refs):
        copies_in.append(pltpu.make_async_copy(ref, held.at[i], in_sems.at[i]))
        copies_in[i].start()
    copies = weight_chunks(place_ref, w_ref, buffer, sems, flips, held.shape[2])
    for copy in copies:
        copy.start()
    if last:
        length = x_ref.shape[1]
        ext[0:HALO, :] = jnp.zeros((HALO, ext.shape[1]), F32)
        ext[HALO:, :] = x_ref[0].astype(F32)
        query = taps_ref[0, 0:1, :] * ext[HALO : HALO + length, :]
        for i in range(1, taps_ref.shape[1]):
            query = query + taps_ref[0, i : i + 1, :] * ext[HALO - i : HALO - i + length, :]
        query_ref[...] = query
    for copy in copies_in:
        copy.wait()
    total = summed([held.at[i] for i in range(len(flips))], copies, buffer, acc_ref[...] if last else None)
    out_ref[...] = total
    if last:
        parts, _, width = sent_ref.shape
        for j in range(parts):
            lanes = slice(j * width, (j + 1) * width)
            sent_ref[j] = (total[:, lanes] * query_ref[:, lanes]).astype(BF16)


def grad_scratch(shards, weight, length, features):
    return chunk_scratch(weight, features, shards), [
        pltpu.VMEM((shards, length, features), BF16),
        pltpu.SemaphoreType.DMA((shards,)),
    ]


def product_grad_first(shards, weight, place, flips):
    length, features = shards[0].shape
    channels = weight.shape[1]
    hbm = pl.BlockSpec(memory_space=pltpu.HBM)
    chunks, inputs = grad_scratch(len(flips), weight, length, features)
    return pl.pallas_call(
        partial(product_grad_kernel, flips=flips, last=False),
        in_specs=[pl.BlockSpec(memory_space=pltpu.SMEM), hbm] + [pl.BlockSpec(memory_space=pl.ANY)] * len(shards),
        out_specs=pl.BlockSpec(memory_space=pltpu.VMEM),
        out_shape=jax.ShapeDtypeStruct((length, channels), F32),
        scratch_shapes=chunks + inputs,
        compiler_params=limit(16),
        name="grad_first",
    )(place, weight, in_hbm(shards[0]), *shards[1:])


def product_grad_last(shards, weight, place, flips, acc, streams, taps, parts):
    length, features = shards[0].shape
    channels = weight.shape[1]
    hbm = pl.BlockSpec(memory_space=pltpu.HBM)
    vmem = pl.BlockSpec(memory_space=pltpu.VMEM)
    full = whole((length, channels))
    chunks, inputs = grad_scratch(len(flips), weight, length, features)
    return pl.pallas_call(
        partial(product_grad_kernel, flips=flips, last=True),
        grid=(1,),
        in_specs=[pl.BlockSpec(memory_space=pltpu.SMEM)]
        + [hbm]
        + [pl.BlockSpec(memory_space=pl.ANY)] * len(shards)
        + [full, whole((1, length, channels)), whole(taps.shape)],
        out_specs=[full, full, whole((parts, length, channels // parts))],
        out_shape=[
            pltpu.HBM((length, channels), F32),
            pltpu.HBM((length, channels), F32),
            pltpu.HBM((parts, length, channels // parts), BF16),
        ],
        scratch_shapes=chunks + [pltpu.VMEM((length + HALO, channels), F32)] + inputs,
        compiler_params=limit(24),
        name="grad_last",
    )(place, weight, *shards, acc, streams, taps)


def edge_kernel(x_ref, edge_ref, taps_ref, grad_ref, _, __, query_ref, sent_ref, ext, query, sent, sems):
    parts, _, width = sent.shape
    ext[0:HALO, :] = edge_ref[0].astype(F32)
    ext[HALO:, :] = x_ref[0].astype(F32)[0:HALO]
    total = taps_ref[0, 0:1, :] * ext[HALO : 2 * HALO, :]
    for i in range(1, taps_ref.shape[1]):
        total = total + taps_ref[0, i : i + 1, :] * ext[HALO - i : 2 * HALO - i, :]
    query[...] = total
    for j in range(parts):
        lanes = slice(j * width, (j + 1) * width)
        sent[j] = (grad_ref[:, lanes] * total[:, lanes]).astype(BF16)
    copies = [
        pltpu.make_async_copy(query, query_ref.at[pl.ds(0, HALO), :], sems.at[0]),
        pltpu.make_async_copy(sent, sent_ref.at[:, pl.ds(0, HALO), :], sems.at[1]),
    ]
    for copy in copies:
        copy.start()
    for copy in copies:
        copy.wait()


def with_edge(streams, edge, taps, grad, query, sent):
    channels = streams.shape[2]
    parts, _, width = sent.shape
    hbm = pl.BlockSpec(memory_space=pltpu.HBM)
    return pl.pallas_call(
        edge_kernel,
        grid=(1,),
        in_specs=[
            whole((1, 2 * HALO, channels)),
            whole((1, HALO, channels)),
            whole(taps.shape),
            whole((HALO, channels)),
            hbm,
            hbm,
        ],
        out_specs=[hbm, hbm],
        out_shape=[pltpu.HBM(query.shape, F32), pltpu.HBM(sent.shape, BF16)],
        scratch_shapes=[
            pltpu.VMEM((2 * HALO, channels), F32),
            pltpu.VMEM((HALO, channels), F32),
            pltpu.VMEM((parts, HALO, width), BF16),
            pltpu.SemaphoreType.DMA((2,)),
        ],
        input_output_aliases={4: 0, 5: 1},
        compiler_params=limit(4),
        name="edge_rows",
    )(streams, edge, taps, in_hbm(grad), in_hbm(query), in_hbm(sent))


def filtered(taps_ref, stream, ext, begin, length):
    total = taps_ref[stream + 1, 0:1, :] * ext[stream, HALO + begin : HALO + begin + length, :]
    for i in range(1, taps_ref.shape[1]):
        first = HALO + begin - i
        total = total + taps_ref[stream + 1, i : i + 1, :] * ext[stream, first : first + length, :]
    return total


def extend(got_ref, ext):
    parts, _, width = got_ref.shape
    length = (ext.shape[1] - HALO) // parts
    ext[:, 0:HALO, :] = jnp.zeros((2, HALO, width), F32)
    for s in range(parts):
        here = slice(HALO + s * length, HALO + (s + 1) * length)
        ext[0, here, :] = got_ref[s, 0:length, :].astype(F32)
        ext[1, here, :] = got_ref[s, length : 2 * length, :].astype(F32)


def forward_begin(got_ref, taps_ref, medium_ref, kept, ext, signals, medium):
    parts, rows, width = got_ref.shape
    length = rows // 3
    extend(got_ref, ext)
    for s in range(parts):
        here = slice(s * length, (s + 1) * length)
        key = filtered(taps_ref, 0, ext, s * length, length)
        value = filtered(taps_ref, 1, ext, s * length, length)
        kept[0, here, :] = key
        kept[1, here, :] = value
        signals[here, 0:width] = (key * value).astype(BF16)
        signals[here, width : 2 * width] = got_ref[s, 2 * length : 3 * length, :]
    medium[...] = jnp.zeros_like(medium)
    medium[0 : medium_ref.shape[0], :] = medium_ref[...].astype(BF16)


def forward_spectra(cosine, sine, signals, medium):
    tokens, double = signals.shape
    width = double // 2
    kept = medium.shape[0]
    both_c = dot(cosine[:, 0:tokens], signals[...])
    both_s = dot(sine[:, 0:tokens], signals[...])
    mc = dot(cosine[:, 0:kept], medium[...])
    ms = dot(sine[:, 0:kept], medium[...])
    ac, hc, as_, hs = (both_c[:, :width], both_c[:, width:], both_s[:, :width], both_s[:, width:])
    xc = ac * mc - as_ * ms
    xs = ac * ms + as_ * mc
    saved = (ac, as_, mc, ms, hc, hs)
    return saved, (xc * hc - xs * hs).astype(BF16), (xc * hs + xs * hc).astype(BF16)


def forward_end(out_ref, acc, freqs):
    parts, length, _ = out_ref.shape
    for s in range(parts):
        first = s * length + 1
        out_ref[s] = (acc[first : first + length, :] * (1.0 / freqs)).astype(BF16)


def block_copies(tables, held, spectra, spectra_held, sems, blocks):
    size = held.shape[1] // blocks
    groups = []
    for b in range(blocks):
        here = pl.ds(b * size, size)
        group = [pltpu.make_async_copy(t.at[here, :], held.at[i, here, :], sems.at[i, b]) for i, t in enumerate(tables)]
        if spectra is not None:
            group.append(pltpu.make_async_copy(spectra.at[:, here, :], spectra_held.at[:, here, :], sems.at[2, b]))
        groups.append(group)
    return groups


def start_all(copies):
    for copy in copies:
        copy.start()


def wait_all(copies):
    for copy in copies:
        copy.wait()


def forward_kernel(got_ref, taps_ref, medium_ref, cos_ref, sin_ref, *refs, freqs, block, resident):
    if not resident:
        cos_across_ref, sin_across_ref, *refs = refs
    out_ref, kept_ref, spectra_ref, ext, signals, medium, acc, kept, kept_sem, *refs = refs
    rows = acc.shape[0]
    step = pl.program_id(0)
    keep = pltpu.make_async_copy(kept, kept_ref, kept_sem)

    if resident:
        held, yc_all, ys_all, spectra_held, sems, out_sems = refs
        blocks = freqs // block
        groups = block_copies((cos_ref, sin_ref), held, None, None, sems, blocks)
        for group in groups:
            start_all(group)
        forward_begin(got_ref, taps_ref, medium_ref, kept, ext, signals, medium)
        keep.start()
        writes = []
        for b, group in enumerate(groups):
            wait_all(group)
            here = slice(b * block, (b + 1) * block)
            saved, yc, ys = forward_spectra(held[0, here, :], held[1, here, :], signals, medium)
            for i, spectrum in enumerate(saved):
                spectra_held[i, here, :] = spectrum
            there = pl.ds(b * block, block)
            writes.append(
                pltpu.make_async_copy(spectra_held.at[:, there, :], spectra_ref.at[:, there, :], out_sems.at[b])
            )
            writes[b].start()
            yc_all[here, :] = yc
            ys_all[here, :] = ys
        acc[...] = dot(held[0, 0:rows, :], yc_all[...]) + dot(held[1, 0:rows, :], ys_all[...])
        forward_end(out_ref, acc, freqs)
        wait_all(writes)
        keep.wait()
        return

    @pl.when(step == 0)
    def _():
        forward_begin(got_ref, taps_ref, medium_ref, kept, ext, signals, medium)
        keep.start()
        keep.wait()
        acc[...] = jnp.zeros_like(acc)

    saved, yc, ys = forward_spectra(cos_ref[...], sin_ref[...], signals, medium)
    for i, spectrum in enumerate(saved):
        spectra_ref[i] = spectrum
    acc[...] += dot(cos_across_ref[0:rows, :], yc) + dot(sin_across_ref[0:rows, :], ys)

    @pl.when(step == pl.num_programs(0) - 1)
    def _():
        forward_end(out_ref, acc, freqs)


def backward_begin(grads_ref, delayed, signal):
    parts, length, _ = grads_ref.shape
    delayed[...] = jnp.zeros_like(delayed)
    for s in range(parts):
        delayed[s * length + 1 : (s + 1) * length + 1, :] = grads_ref[s].astype(F32)
    signal[...] = delayed[...].astype(BF16)


def backward_spectra(cosine, sine, signal, spectra):
    gc = dot(cosine, signal[...])
    gs = dot(sine, signal[...])
    ac, as_, mc, ms, hc, hs = spectra
    uc = hc * gc + hs * gs
    us = hc * gs - hs * gc
    xc = ac * mc - as_ * ms
    xs = ac * ms + as_ * mc
    both_c = jnp.concatenate([xc * gc + xs * gs, mc * uc + ms * us], 1).astype(BF16)
    both_s = jnp.concatenate([xc * gs - xs * gc, mc * us - ms * uc], 1).astype(BF16)
    return both_c, both_s, (ac * uc + as_ * us).astype(BF16), (ac * us - as_ * uc).astype(BF16)


def backward_end(
    streams, taps_ref, kept, out_ref, small_ref, ext, after, acc, tap_acc, freqs, scale, medium_reach
):
    parts, _, width = out_ref.shape
    extend(streams, ext)
    length = (ext.shape[1] - HALO) // parts
    tokens = parts * length
    reach = taps_ref.shape[1]
    inverse = 1.0 / freqs
    small_ref[...] = jnp.zeros_like(small_ref)
    small_ref[0:medium_reach, :] = tap_acc[0:medium_reach, :] * (inverse * scale)
    after[:, tokens : tokens + HALO, :] = jnp.zeros((2, HALO, width), F32)
    first = length + 2 * HALO
    for s in range(parts):
        here = slice(s * length, (s + 1) * length)
        out_ref[s, first : first + length, :] = (acc[here, 0:width] * (inverse * scale)).astype(BF16)
        gated = acc[here, width : 2 * width] * inverse
        out_ref[s, 0:length, :] = gated.astype(BF16)
        after[0, here, :] = gated * kept[1, here, :]
        after[1, here, :] = gated * kept[0, here, :]
    for j in range(2):
        sums = [jnp.zeros((8, width), F32) for _ in range(reach)]
        for s in range(parts):
            begin = s * length
            own = after[j, begin : begin + length, :]
            for i in range(reach):
                moved = ext[j, HALO + begin - i : HALO + begin - i + length, :]
                sums[i] = sums[i] + jnp.sum((moved * own).reshape(length // 8, 8, width), 0)
        for i in range(reach):
            row = medium_reach + j * reach + i
            small_ref[row : row + 1, :] = jnp.sum(sums[i], 0, keepdims=True) * scale
    small = small_ref[...].astype(BF16)
    first = 2 * length + 2 * HALO
    for s in range(parts):
        end = (s + 1) * length
        for j in range(2):
            rows = slice(length + j * HALO, length + (j + 1) * HALO)
            out_ref[s, rows, :] = after[j, end : end + HALO, :].astype(BF16)
        out_ref[s, first : first + small.shape[0], :] = small


def backward_kernel(
    grads_ref, taps_ref, got_ref, kept_ref, spectra_ref, cos_ref, sin_ref, *refs,
    freqs, block, scale, medium_reach, resident,
):
    if not resident:
        cos_across_ref, sin_across_ref, *refs = refs
    out_ref, small, delayed, signal, ext, after, acc, tap_acc, streams, kept, late_sems, *refs = refs
    step = pl.program_id(0)
    size = signal.shape[0]
    rows, taps_kept = (acc.shape[0], tap_acc.shape[0])
    late = [
        pltpu.make_async_copy(kept_ref, kept, late_sems.at[0]),
        pltpu.make_async_copy(got_ref.at[:, pl.ds(0, streams.shape[1]), :], streams, late_sems.at[1]),
    ]

    def end():
        wait_all(late)
        backward_end(
            streams, taps_ref, kept, out_ref, small, ext, after, acc, tap_acc, freqs, scale, medium_reach
        )

    if resident:
        held, both_c_all, both_s_all, taps_c_all, taps_s_all, spectra_held, sems = refs
        groups = block_copies((cos_ref, sin_ref), held, spectra_ref, spectra_held, sems, freqs // block)
        for group in groups:
            start_all(group)
        start_all(late)
        backward_begin(grads_ref, delayed, signal)
        for b, group in enumerate(groups):
            wait_all(group)
            here = slice(b * block, (b + 1) * block)
            spectra = [spectra_held[i, here, :] for i in range(spectra_held.shape[0])]
            both_c_all[here, :], both_s_all[here, :], taps_c_all[here, :], taps_s_all[here, :] = backward_spectra(
                held[0, here, 0:size], held[1, here, 0:size], signal, spectra
            )
        acc[...] = dot(held[0, 0:rows, :], both_c_all[...]) + dot(held[1, 0:rows, :], both_s_all[...])
        tap_acc[...] = dot(held[0, 0:taps_kept, :], taps_c_all[...]) + dot(held[1, 0:taps_kept, :], taps_s_all[...])
        end()
        return

    @pl.when(step == 0)
    def _():
        backward_begin(grads_ref, delayed, signal)
        acc[...] = jnp.zeros_like(acc)
        tap_acc[...] = jnp.zeros_like(tap_acc)

    spectra = [spectra_ref[i] for i in range(spectra_ref.shape[0])]
    both_c, both_s, taps_c, taps_s = backward_spectra(cos_ref[:, 0:size], sin_ref[:, 0:size], signal, spectra)
    acc[...] += dot(cos_across_ref[0:rows, :], both_c) + dot(sin_across_ref[0:rows, :], both_s)
    tap_acc[...] += dot(cos_across_ref[0:taps_kept, :], taps_c) + dot(sin_across_ref[0:taps_kept, :], taps_s)

    @pl.when(step == pl.num_programs(0) - 1)
    def _():
        start_all(late)
        end()


def spectral_plan(freqs, block, tables):
    if freqs * freqs <= TABLE_LIMIT:
        hbm = pl.BlockSpec(memory_space=pltpu.HBM)
        return True, 1, [hbm, hbm], [in_hbm(t) for t in tables]
    rows = pl.BlockSpec((block, freqs), lambda j: (j, 0))
    columns = pl.BlockSpec((freqs, block), lambda j: (0, j))
    return False, freqs // block, [rows, rows, columns, columns], [*tables, *tables]


def held_scratch(freqs, block, width, widths, kinds):
    blocks = freqs // block
    return (
        [pltpu.VMEM((2, freqs, freqs), BF16)]
        + [pltpu.VMEM((freqs, w), BF16) for w in widths]
        + [pltpu.VMEM((6, freqs, width), F32), pltpu.SemaphoreType.DMA((kinds, blocks))]
    )


def forward_call(got, taps, medium_taps, tables, freqs, block):
    parts, tall, width = got.shape
    length = tall // 3
    tokens = parts * length
    padded = -(-medium_taps.shape[0] // 128) * 128
    resident, steps, specs, operands = spectral_plan(freqs, block, tables)
    per = freqs // steps
    hbm = pl.BlockSpec(memory_space=pltpu.HBM)
    return pl.pallas_call(
        partial(forward_kernel, freqs=freqs, block=block, resident=resident),
        grid=(steps,),
        in_specs=[whole(got.shape), whole(taps.shape), whole(medium_taps.shape)] + specs,
        out_specs=[
            whole((parts, length, width)),
            hbm,
            hbm if resident else pl.BlockSpec((6, per, width), lambda j: (0, j, 0)),
        ],
        out_shape=[
            pltpu.HBM((parts, length, width), BF16),
            pltpu.HBM((2, tokens, width), F32),
            pltpu.HBM((6, freqs, width), F32),
        ],
        scratch_shapes=[
            pltpu.VMEM((2, tokens + HALO, width), F32),
            pltpu.VMEM((tokens, 2 * width), BF16),
            pltpu.VMEM((padded, width), BF16),
            pltpu.VMEM((tokens + HALO, width), F32),
            pltpu.VMEM((2, tokens, width), F32),
            pltpu.SemaphoreType.DMA,
        ]
        + (
            held_scratch(freqs, block, width, (width, width), 2) + [pltpu.SemaphoreType.DMA((freqs // block,))]
            if resident
            else []
        ),
        compiler_params=limit(32 if resident else 60),
        name="forward_spectral",
    )(in_hbm(got), taps, medium_taps, *operands)


def backward_call(got, grads, taps, kept, spectra, tables, freqs, block, scale, medium_reach, rows, small, extra):
    parts, tall, width = got.shape
    length = tall // 3
    tokens = parts * length
    padded = -(-medium_reach // 128) * 128
    late = -(-(tokens + 1) // 128) * 128
    resident, steps, specs, operands = spectral_plan(freqs, block, tables)
    per = freqs // steps
    hbm = pl.BlockSpec(memory_space=pltpu.HBM)
    return pl.pallas_call(
        partial(
            backward_kernel, freqs=freqs, block=block, scale=scale, medium_reach=medium_reach, resident=resident
        ),
        grid=(steps,),
        in_specs=[
            whole((parts, length, width)),
            whole(taps.shape),
            hbm,
            hbm,
            hbm if resident else pl.BlockSpec((6, per, width), lambda j: (0, j, 0)),
        ]
        + specs,
        out_specs=whole((parts, rows + small + extra, width)),
        out_shape=pltpu.HBM((parts, rows + small + extra, width), BF16),
        scratch_shapes=[
            pltpu.VMEM((small, width), F32),
            pltpu.VMEM((late, width), F32),
            pltpu.VMEM((late, width), BF16),
            pltpu.VMEM((2, tokens + HALO, width), F32),
            pltpu.VMEM((2, tokens + HALO, width), F32),
            pltpu.VMEM((tokens, 2 * width), F32),
            pltpu.VMEM((padded, width), F32),
            pltpu.VMEM((parts, 2 * length, width), BF16),
            pltpu.VMEM((2, tokens, width), F32),
            pltpu.SemaphoreType.DMA((2,)),
        ]
        + (held_scratch(freqs, block, width, (2 * width, 2 * width, width, width), 3) if resident else []),
        compiler_params=limit(40 if resident else 60),
        name="backward_spectral",
    )(in_hbm(grads), taps, in_hbm(got), in_hbm(kept), in_hbm(spectra), *operands)


def product_kernel(
    got_ref, query_ref, grad_ref, x_ref, edge_ref, _, product_ref, query_grad_ref, first_ref, back_ref,
    ext, taps, rounded, sem, *, reach, begin,
):
    parts, length, width = got_ref.shape
    ext[0:HALO, :] = edge_ref[0].astype(F32)
    ext[HALO:, :] = x_ref[0].astype(F32)
    taps[...] = jnp.zeros_like(taps)
    for j in range(parts):
        lanes = slice(j * width, (j + 1) * width)
        convolved = got_ref[j].astype(F32)
        product_ref[:, lanes] = (query_ref[:, lanes] * convolved).astype(BF16)
        own = grad_ref[:, lanes] * convolved
        query_grad_ref[:, lanes] = own
        first_ref[:, lanes] = own[0:HALO].astype(BF16)
        for i in range(reach):
            moved = ext[HALO - i : HALO - i + length, lanes]
            taps[j * reach + i : j * reach + i + 1, :] = jnp.sum(moved * own, 0, keepdims=True)
    for s in range(parts):
        rounded[s] = taps[...].astype(BF16)
    write = pltpu.make_async_copy(rounded, back_ref.at[:, pl.ds(begin, taps.shape[0]), :], sem)
    write.start()
    write.wait()


def product_call(convolved, query, grad, streams, edge, back, reach, begin):
    parts, length, width = convolved.shape
    channels = parts * width
    extra = back.shape[1] - begin
    hbm = pl.BlockSpec(memory_space=pltpu.HBM)
    full = whole((length, channels))
    return pl.pallas_call(
        partial(product_kernel, reach=reach, begin=begin),
        grid=(1,),
        in_specs=[
            whole((parts, length, width)),
            full,
            full,
            whole((1, length, channels)),
            whole((1, HALO, channels)),
            hbm,
        ],
        out_specs=[full, full, whole((HALO, channels)), hbm],
        out_shape=[
            pltpu.HBM((length, channels), BF16),
            pltpu.HBM((length, channels), F32),
            pltpu.HBM((HALO, channels), BF16),
            pltpu.HBM(back.shape, BF16),
        ],
        scratch_shapes=[
            pltpu.VMEM((length + HALO, channels), F32),
            pltpu.VMEM((extra, width), F32),
            pltpu.VMEM((parts, extra, width), BF16),
            pltpu.SemaphoreType.DMA,
        ],
        input_output_aliases={5: 3},
        compiler_params=limit(16),
        name="product",
    )(convolved, in_hbm(query), in_hbm(grad), streams, edge, in_hbm(back))


def project_kernel(place_ref, product_ref, w_ref, *refs, flips):
    out_refs = refs[: len(flips)]
    buffer, sems = refs[len(flips) :]
    copies = weight_chunks(place_ref, w_ref, buffer, sems, flips, out_refs[0].shape[1])
    start_all(copies)
    deep = buffer.shape[1]
    per = len(copies) // len(flips)
    for slot, copy in enumerate(copies):
        copy.wait()
        part = lax.dot_general(
            product_ref[...], buffer[slot], (((1,), (1,)), ((), ())), preferred_element_type=F32
        )
        lanes = slice(slot % per * deep, (slot % per + 1) * deep)
        out = out_refs[slot // per]
        out[:, lanes] = part.astype(out.dtype)


def project(product, weight, place, flips, features, dtypes):
    length = product.shape[0]
    vmem = pl.BlockSpec(memory_space=pltpu.VMEM)
    return pl.pallas_call(
        partial(project_kernel, flips=flips),
        in_specs=[pl.BlockSpec(memory_space=pltpu.SMEM), vmem, pl.BlockSpec(memory_space=pltpu.HBM)],
        out_specs=[vmem] * len(flips),
        out_shape=[jax.ShapeDtypeStruct((length, features), dtype) for dtype in dtypes],
        scratch_shapes=chunk_scratch(weight, features, len(flips)),
        compiler_params=limit(16),
        name="project",
    )(place, product, weight)


def local_kernel(x_ref, edge_ref, taps_ref, out_ref, ext):
    _, length, channels = out_ref.shape
    for j in range(2):
        ext[0:HALO, :] = edge_ref[j + 1].astype(F32)
        ext[HALO:, :] = x_ref[j + 1].astype(F32)
        for begin in range(0, channels, LANES):
            lanes = slice(begin, min(begin + LANES, channels))
            total = taps_ref[j + 1, 0:1, lanes] * ext[HALO : HALO + length, lanes]
            for i in range(1, taps_ref.shape[1]):
                total = total + taps_ref[j + 1, i : i + 1, lanes] * ext[HALO - i : HALO - i + length, lanes]
            out_ref[j, :, lanes] = total


def finish_kernel(
    got_ref, query_grad_ref, next_ref, taps_ref, local_ref,
    input_grad_ref, filter_ref, medium_ref, short_ref, ext, sums, *, scale, own_rows,
):
    parts, _, width = got_ref.shape
    length = filter_ref.shape[0]
    reach = taps_ref.shape[1]
    medium_reach = medium_ref.shape[0]
    ext[0, 0:length, :] = query_grad_ref[...]
    ext[0, length:, :] = next_ref[...].astype(F32)
    after = length + 2 * HALO
    for j in range(parts):
        lanes = slice(j * width, (j + 1) * width)
        gated = got_ref[j, 0:length, :].astype(F32)
        ext[1, 0:length, lanes] = gated * local_ref[1, :, lanes]
        ext[2, 0:length, lanes] = gated * local_ref[0, :, lanes]
        ext[1, length:, lanes] = got_ref[j, length : length + HALO, :].astype(F32)
        ext[2, length:, lanes] = got_ref[j, length + HALO : after, :].astype(F32)
        filter_ref[:, lanes] = got_ref[j, after : after + length, :].astype(F32)
        small = got_ref[j, after + length : after + length + own_rows, :].astype(F32)
        medium_ref[:, lanes] = small[0:medium_reach, :]
        first = medium_reach + reach
        short_ref[1, :, lanes] = small[medium_reach:first, :]
        short_ref[2, :, lanes] = small[first : first + reach, :]
        for k in range(3):
            total = taps_ref[k, 0:1, lanes] * ext[k, 0:length, lanes]
            for i in range(1, reach):
                total = total + taps_ref[k, i : i + 1, lanes] * ext[k, i : i + length, lanes]
            input_grad_ref[k, :, lanes] = total.astype(BF16)
    first = after + length + own_rows
    total = got_ref[0, first:, :].astype(F32)
    for j in range(1, parts):
        total = total + got_ref[j, first:, :].astype(F32)
    sums[...] = total
    for j in range(parts):
        short_ref[0, :, j * width : (j + 1) * width] = sums[j * reach : (j + 1) * reach, :] * scale


def reshard(value):
    return lax.all_to_all(value, "seq", split_axis=0, concat_axis=0, tiled=True)


def local(inputs, short_taps, medium_taps, long_filter, out_weight, out_cotangent):
    length, groups, channels = inputs.shape
    reach = short_taps.shape[0]
    medium_reach = medium_taps.shape[0]
    parts = lax.axis_size("seq")
    position = lax.axis_index("seq")
    place = lax.axis_index("tensor").astype(jnp.int32)[None]
    features = out_cotangent.shape[1]
    width = channels // parts
    tokens = length * parts
    scale = 1.0 / math.sqrt(tokens)
    freqs, block = spectral_sizes(tokens, medium_reach)
    vmem = pl.BlockSpec(memory_space=pltpu.VMEM)

    weight = pltpu.with_memory_space_constraint(out_weight, pltpu.HBM)
    streams = inputs.transpose(1, 0, 2)
    taps = short_taps.transpose(1, 0, 2)
    hbm = pl.BlockSpec(memory_space=pltpu.HBM)
    packed = pl.pallas_call(
        pack_kernel,
        in_specs=[hbm, hbm],
        out_specs=hbm,
        out_shape=pltpu.HBM((parts, 3 * length, width), BF16),
        scratch_shapes=[
            pltpu.VMEM((2, length, channels), BF16),
            pltpu.VMEM((length, channels), F32),
            pltpu.VMEM((parts, 3 * length, width), BF16),
            pltpu.SemaphoreType.DMA((2 + parts,)),
        ],
        compiler_params=limit(8),
        name="pack",
    )(
        pltpu.with_memory_space_constraint(streams, pltpu.HBM),
        pltpu.with_memory_space_constraint(long_filter, pltpu.HBM),
    )
    got = reshard(packed)
    edge = shift(streams[:, length - HALO :], "seq", 1)
    cot_x = exchange(out_cotangent, "tensor", 2)
    cot_core = exchange(out_cotangent, "tensor", 1)

    tables = dft_tables(freqs)
    own_taps = lax.dynamic_slice_in_dim(taps, position * width, width, 2)
    own_medium = lax.dynamic_slice_in_dim(medium_taps, position * width, width, 1)

    acc = product_grad_first((out_cotangent, cot_core), weight, place, (0, 1))
    cot_far = exchange(cot_x, "tensor", 1)
    product_grad, query, sent = product_grad_last((cot_x, cot_far), weight, place, (2, 3), acc, streams, taps, parts)
    query, sent = with_edge(streams, edge, taps, product_grad, query, sent)
    grads = reshard(sent)

    convolved, kept, spectra = forward_call(got, own_taps, own_medium, tables, freqs, block)
    convolved = reshard(convolved)

    rows = 2 * length + 2 * HALO
    small = -(-(medium_reach + 2 * reach) // 16) * 16
    extra = -(-parts * reach // 16) * 16
    back = backward_call(
        got, grads, own_taps, kept, spectra, tables, freqs, block, scale, medium_reach, rows, small, extra
    )
    product, query_grad, first_rows, back = product_call(
        convolved, query, product_grad, streams, edge, back, reach, rows + small
    )
    returned = reshard(back)

    (far,) = project(product, weight, place, (3,), features, (BF16,))
    far_core = exchange(far, "tensor", 1)
    (across,) = project(product, weight, place, (2,), features, (F32,))
    across_sum = exchange((across + far_core.astype(F32)).astype(BF16), "tensor", 2)
    near, own = project(product, weight, place, (1, 0), features, (BF16, F32))
    near_core = exchange(near, "tensor", 1)
    next_grad = shift(first_rows, "seq", -1)

    local_features = pl.pallas_call(
        local_kernel,
        in_specs=[vmem] * 3,
        out_specs=vmem,
        out_shape=pltpu.HBM((2, length, channels), F32),
        scratch_shapes=[pltpu.VMEM((length + HALO, channels), F32)],
        compiler_params=limit(8),
        name="local",
    )(in_hbm(streams), edge, taps)
    input_grad, filter_grad, medium_grad, short_grad = pl.pallas_call(
        partial(finish_kernel, scale=scale, own_rows=small),
        grid=(1,),
        in_specs=[
            whole((parts, rows + small + extra, width)),
            whole((length, channels)),
            whole((HALO, channels)),
            whole(taps.shape),
            whole((2, length, channels)),
        ],
        out_specs=[
            whole((groups, length, channels)),
            whole((length, channels)),
            whole((medium_reach, channels)),
            whole((groups, reach, channels)),
        ],
        out_shape=[
            jax.ShapeDtypeStruct((groups, length, channels), BF16),
            jax.ShapeDtypeStruct((length, channels), F32),
            jax.ShapeDtypeStruct((medium_reach, channels), F32),
            jax.ShapeDtypeStruct((groups, reach, channels), F32),
        ],
        scratch_shapes=[
            pltpu.VMEM((groups, length + HALO, channels), F32),
            pltpu.VMEM((extra, width), F32),
        ],
        compiler_params=limit(16),
        name="finish",
    )(returned, query_grad, next_grad, taps, in_hbm(local_features))

    output = (own + near_core.astype(F32) + across_sum.astype(F32)).astype(BF16)
    return (
        output,
        input_grad.transpose(1, 0, 2),
        filter_grad,
        medium_grad,
        short_grad.transpose(1, 0, 2),
    )


def solution(mesh):
    return jax.shard_map(
        local,
        mesh=mesh,
        in_specs=(
            P("seq", None, "tensor"),
            P(None, None, "tensor"),
            P(None, "tensor"),
            P("seq", "tensor"),
            P(None, "tensor"),
            P("seq", "tensor"),
        ),
        out_specs=(
            P("seq", "tensor"),
            P("seq", None, "tensor"),
            P("seq", "tensor"),
            P(None, "tensor"),
            P(None, None, "tensor"),
        ),
        check_vma=False,
    )
```

```python
import math
from functools import partial

import jax
import jax.numpy as jnp
from jax import lax
from jax.experimental import pallas as pl
from jax.experimental.pallas import tpu as pltpu
from jax.sharding import PartitionSpec as P


F32 = jnp.float32
BF16 = jnp.bfloat16
HALO = 8
GROUP = 32
LANES = 128
CHUNK = 512
TABLE_LIMIT = 1 << 22


def dot(a, b):
    return lax.dot_general(a, b, (((1,), (0,)), ((), ())), preferred_element_type=F32)


def exchange(value, axis, flip):
    count = lax.axis_size(axis)
    return lax.ppermute(value, axis, [(source, source ^ flip) for source in range(count)])


def shift(value, axis, steps):
    count = lax.axis_size(axis)
    pairs = [(s, s + steps) for s in range(count) if 0 <= s + steps < count]
    return lax.ppermute(value, axis, pairs)


def whole(shape):
    return pl.BlockSpec(shape, lambda *_: (0,) * len(shape))


def spectral_sizes(tokens, medium_reach):
    need = tokens + -(-(medium_reach - 2) // 2)
    freqs = -(-need // 384) * 384
    return freqs, 384


def dft_tables(freqs):
    period = 8 * freqs
    unit = 2.0 * math.pi / period
    odd = 2 * jnp.arange(freqs, dtype=jnp.int32) + 1
    start = 2 * GROUP * jnp.arange(freqs // GROUP, dtype=jnp.int32)
    inner = 2 * jnp.arange(GROUP, dtype=jnp.int32) + 1
    first = (start[:, None] * odd[None, :] % period).astype(F32) * unit
    second = (inner[:, None] * odd[None, :] % period).astype(F32) * unit
    fc, fs = jnp.cos(first)[:, None], jnp.sin(first)[:, None]
    sc, ss = jnp.cos(second)[None], jnp.sin(second)[None]
    cosine = (fc * sc - fs * ss).astype(BF16).reshape(freqs, freqs)
    sine = (fs * sc + fc * ss).astype(BF16).reshape(freqs, freqs)
    return cosine, sine


def in_hbm(value):
    return pltpu.with_memory_space_constraint(value, pltpu.HBM)


def limit(mebibytes):
    return pltpu.CompilerParams(vmem_limit_bytes=mebibytes << 20)


def pack_kernel(x_ref, filter_ref, out_ref, streams, taps, rounded, sems):
    parts, rows, width = out_ref.shape
    length = rows // 3
    read_filter = pltpu.make_async_copy(filter_ref, taps, sems.at[0])
    read_streams = pltpu.make_async_copy(x_ref.at[pl.ds(1, 2)], streams, sems.at[1])
    read_filter.start()
    read_streams.start()
    read_filter.wait()
    for j in range(parts):
        rounded[j, 2 * length :, :] = taps[:, j * width : (j + 1) * width].astype(BF16)
    read_streams.wait()
    writes = []
    for j in range(parts):
        lanes = slice(j * width, (j + 1) * width)
        rounded[j, 0:length, :] = streams[0, :, lanes]
        rounded[j, length : 2 * length, :] = streams[1, :, lanes]
        writes.append(pltpu.make_async_copy(rounded.at[j], out_ref.at[j], sems.at[2 + j]))
        writes[j].start()
    for write in writes:
        write.wait()


def weight_chunks(place_ref, weight_ref, buffer, sems, flips, features):
    deep = buffer.shape[1]
    per = features // deep
    copies = []
    for i, flip in enumerate(flips):
        for k in range(per):
            start = jnp.bitwise_xor(place_ref[0], flip) * features + k * deep
            slot = i * per + k
            copies.append(
                pltpu.make_async_copy(
                    weight_ref.at[pl.ds(pl.multiple_of(start, deep), deep), :], buffer.at[slot], sems.at[slot]
                )
            )
    return copies


def chunk_scratch(weight, features, shards):
    deep = math.gcd(features, CHUNK)
    count = shards * (features // deep)
    return [pltpu.VMEM((count, deep, weight.shape[1]), weight.dtype), pltpu.SemaphoreType.DMA((count,))]


def summed(x_refs, copies, buffer, total):
    deep = buffer.shape[1]
    per = len(copies) // len(x_refs)
    for slot, copy in enumerate(copies):
        copy.wait()
        lanes = slice(slot % per * deep, (slot % per + 1) * deep)
        part = dot(x_refs[slot // per][:, lanes], buffer[slot])
        total = part if total is None else total + part
    return total


def product_grad_kernel(place_ref, w_ref, *refs, flips, last):
    x_refs = refs[: len(flips)]
    copies_in = []
    if last:
        acc_ref, x_ref, taps_ref, out_ref, query_ref, sent_ref, buffer, sems, ext, held, in_sems = refs[len(flips) :]
    else:
        out_ref, buffer, sems, held, in_sems = refs[len(flips) :]
    for i, ref in enumerate(x_refs):
        copies_in.append(pltpu.make_async_copy(ref, held.at[i], in_sems.at[i]))
        copies_in[i].start()
    copies = weight_chunks(place_ref, w_ref, buffer, sems, flips, held.shape[2])
    for copy in copies:
        copy.start()
    if last:
        length = x_ref.shape[1]
        ext[0:HALO, :] = jnp.zeros((HALO, ext.shape[1]), F32)
        ext[HALO:, :] = x_ref[0].astype(F32)
        query = taps_ref[0, 0:1, :] * ext[HALO : HALO + length, :]
        for i in range(1, taps_ref.shape[1]):
            query = query + taps_ref[0, i : i + 1, :] * ext[HALO - i : HALO - i + length, :]
        query_ref[...] = query
    for copy in copies_in:
        copy.wait()
    total = summed([held.at[i] for i in range(len(flips))], copies, buffer, acc_ref[...] if last else None)
    out_ref[...] = total
    if last:
        parts, _, width = sent_ref.shape
        for j in range(parts):
            lanes = slice(j * width, (j + 1) * width)
            sent_ref[j] = (total[:, lanes] * query_ref[:, lanes]).astype(BF16)


def grad_scratch(shards, weight, length, features):
    return chunk_scratch(weight, features, shards), [
        pltpu.VMEM((shards, length, features), BF16),
        pltpu.SemaphoreType.DMA((shards,)),
    ]


def product_grad_first(shards, weight, place, flips):
    length, features = shards[0].shape
    channels = weight.shape[1]
    hbm = pl.BlockSpec(memory_space=pltpu.HBM)
    chunks, inputs = grad_scratch(len(flips), weight, length, features)
    return pl.pallas_call(
        partial(product_grad_kernel, flips=flips, last=False),
        in_specs=[pl.BlockSpec(memory_space=pltpu.SMEM), hbm] + [pl.BlockSpec(memory_space=pl.ANY)] * len(shards),
        out_specs=pl.BlockSpec(memory_space=pltpu.VMEM),
        out_shape=jax.ShapeDtypeStruct((length, channels), F32),
        scratch_shapes=chunks + inputs,
        compiler_params=limit(16),
        name="grad_first",
    )(place, weight, in_hbm(shards[0]), *shards[1:])


def product_grad_last(shards, weight, place, flips, acc, streams, taps, parts):
    length, features = shards[0].shape
    channels = weight.shape[1]
    hbm = pl.BlockSpec(memory_space=pltpu.HBM)
    vmem = pl.BlockSpec(memory_space=pltpu.VMEM)
    full = whole((length, channels))
    chunks, inputs = grad_scratch(len(flips), weight, length, features)
    return pl.pallas_call(
        partial(product_grad_kernel, flips=flips, last=True),
        grid=(1,),
        in_specs=[pl.BlockSpec(memory_space=pltpu.SMEM)]
        + [hbm]
        + [pl.BlockSpec(memory_space=pl.ANY)] * len(shards)
        + [full, whole((1, length, channels)), whole(taps.shape)],
        out_specs=[full, full, whole((parts, length, channels // parts))],
        out_shape=[
            pltpu.HBM((length, channels), F32),
            pltpu.HBM((length, channels), F32),
            pltpu.HBM((parts, length, channels // parts), BF16),
        ],
        scratch_shapes=chunks + [pltpu.VMEM((length + HALO, channels), F32)] + inputs,
        compiler_params=limit(24),
        name="grad_last",
    )(place, weight, *shards, acc, streams, taps)


def edge_kernel(x_ref, edge_ref, taps_ref, grad_ref, _, __, query_ref, sent_ref, ext, query, sent, sems):
    parts, _, width = sent.shape
    ext[0:HALO, :] = edge_ref[0].astype(F32)
    ext[HALO:, :] = x_ref[0].astype(F32)[0:HALO]
    total = taps_ref[0, 0:1, :] * ext[HALO : 2 * HALO, :]
    for i in range(1, taps_ref.shape[1]):
        total = total + taps_ref[0, i : i + 1, :] * ext[HALO - i : 2 * HALO - i, :]
    query[...] = total
    for j in range(parts):
        lanes = slice(j * width, (j + 1) * width)
        sent[j] = (grad_ref[:, lanes] * total[:, lanes]).astype(BF16)
    copies = [
        pltpu.make_async_copy(query, query_ref.at[pl.ds(0, HALO), :], sems.at[0]),
        pltpu.make_async_copy(sent, sent_ref.at[:, pl.ds(0, HALO), :], sems.at[1]),
    ]
    for copy in copies:
        copy.start()
    for copy in copies:
        copy.wait()


def with_edge(streams, edge, taps, grad, query, sent):
    channels = streams.shape[2]
    parts, _, width = sent.shape
    hbm = pl.BlockSpec(memory_space=pltpu.HBM)
    return pl.pallas_call(
        edge_kernel,
        grid=(1,),
        in_specs=[
            whole((1, 2 * HALO, channels)),
            whole((1, HALO, channels)),
            whole(taps.shape),
            whole((HALO, channels)),
            hbm,
            hbm,
        ],
        out_specs=[hbm, hbm],
        out_shape=[pltpu.HBM(query.shape, F32), pltpu.HBM(sent.shape, BF16)],
        scratch_shapes=[
            pltpu.VMEM((2 * HALO, channels), F32),
            pltpu.VMEM((HALO, channels), F32),
            pltpu.VMEM((parts, HALO, width), BF16),
            pltpu.SemaphoreType.DMA((2,)),
        ],
        input_output_aliases={4: 0, 5: 1},
        compiler_params=limit(4),
        name="edge_rows",
    )(streams, edge, taps, in_hbm(grad), in_hbm(query), in_hbm(sent))


def filtered(taps_ref, stream, ext, begin, length):
    total = taps_ref[stream + 1, 0:1, :] * ext[stream, HALO + begin : HALO + begin + length, :]
    for i in range(1, taps_ref.shape[1]):
        first = HALO + begin - i
        total = total + taps_ref[stream + 1, i : i + 1, :] * ext[stream, first : first + length, :]
    return total


def extend(got_ref, ext):
    parts, _, width = got_ref.shape
    length = (ext.shape[1] - HALO) // parts
    ext[:, 0:HALO, :] = jnp.zeros((2, HALO, width), F32)
    for s in range(parts):
        here = slice(HALO + s * length, HALO + (s + 1) * length)
        ext[0, here, :] = got_ref[s, 0:length, :].astype(F32)
        ext[1, here, :] = got_ref[s, length : 2 * length, :].astype(F32)


def forward_begin(got_ref, taps_ref, medium_ref, kept, ext, signals, medium):
    parts, rows, width = got_ref.shape
    length = rows // 3
    extend(got_ref, ext)
    for s in range(parts):
        here = slice(s * length, (s + 1) * length)
        key = filtered(taps_ref, 0, ext, s * length, length)
        value = filtered(taps_ref, 1, ext, s * length, length)
        kept[0, here, :] = key
        kept[1, here, :] = value
        signals[here, 0:width] = (key * value).astype(BF16)
        signals[here, width : 2 * width] = got_ref[s, 2 * length : 3 * length, :]
    medium[...] = jnp.zeros_like(medium)
    medium[0 : medium_ref.shape[0], :] = medium_ref[...].astype(BF16)


def forward_spectra(cosine, sine, signals, medium):
    tokens, double = signals.shape
    width = double // 2
    kept = medium.shape[0]
    both_c = dot(cosine[:, 0:tokens], signals[...])
    both_s = dot(sine[:, 0:tokens], signals[...])
    mc = dot(cosine[:, 0:kept], medium[...])
    ms = dot(sine[:, 0:kept], medium[...])
    ac, hc, as_, hs = (both_c[:, :width], both_c[:, width:], both_s[:, :width], both_s[:, width:])
    xc = ac * mc - as_ * ms
    xs = ac * ms + as_ * mc
    saved = (ac, as_, hc, hs)
    return saved, (xc * hc - xs * hs).astype(BF16), (xc * hs + xs * hc).astype(BF16)


def forward_end(out_ref, acc, freqs):
    parts, length, _ = out_ref.shape
    for s in range(parts):
        first = s * length + 1
        out_ref[s] = (acc[first : first + length, :] * (1.0 / freqs)).astype(BF16)


def block_copies(tables, held, spectra, spectra_held, sems, blocks):
    size = held.shape[1] // blocks
    groups = []
    for b in range(blocks):
        here = pl.ds(b * size, size)
        group = [pltpu.make_async_copy(t.at[here, :], held.at[i, here, :], sems.at[i, b]) for i, t in enumerate(tables)]
        if spectra is not None:
            group.append(pltpu.make_async_copy(spectra.at[:, here, :], spectra_held.at[:, here, :], sems.at[2, b]))
        groups.append(group)
    return groups


def start_all(copies):
    for copy in copies:
        copy.start()


def wait_all(copies):
    for copy in copies:
        copy.wait()


def forward_kernel(got_ref, taps_ref, medium_ref, cos_ref, sin_ref, *refs, freqs, block, resident):
    if not resident:
        cos_across_ref, sin_across_ref, *refs = refs
    out_ref, kept_ref, spectra_ref, ext, signals, medium, acc, kept, kept_sem, *refs = refs
    rows = acc.shape[0]
    step = pl.program_id(0)
    keep = pltpu.make_async_copy(kept, kept_ref, kept_sem)

    if resident:
        held, yc_all, ys_all, spectra_held, sems, out_sems = refs
        blocks = freqs // block
        groups = block_copies((cos_ref, sin_ref), held, None, None, sems, blocks)
        for group in groups:
            start_all(group)
        forward_begin(got_ref, taps_ref, medium_ref, kept, ext, signals, medium)
        keep.start()
        writes = []
        for b, group in enumerate(groups):
            wait_all(group)
            here = slice(b * block, (b + 1) * block)
            saved, yc, ys = forward_spectra(held[0, here, :], held[1, here, :], signals, medium)
            for i, spectrum in enumerate(saved):
                spectra_held[i, here, :] = spectrum
            there = pl.ds(b * block, block)
            writes.append(
                pltpu.make_async_copy(spectra_held.at[:, there, :], spectra_ref.at[:, there, :], out_sems.at[b])
            )
            writes[b].start()
            yc_all[here, :] = yc
            ys_all[here, :] = ys
        acc[...] = dot(held[0, 0:rows, :], yc_all[...]) + dot(held[1, 0:rows, :], ys_all[...])
        forward_end(out_ref, acc, freqs)
        wait_all(writes)
        keep.wait()
        return

    @pl.when(step == 0)
    def _():
        forward_begin(got_ref, taps_ref, medium_ref, kept, ext, signals, medium)
        keep.start()
        keep.wait()
        acc[...] = jnp.zeros_like(acc)

    saved, yc, ys = forward_spectra(cos_ref[...], sin_ref[...], signals, medium)
    for i, spectrum in enumerate(saved):
        spectra_ref[i] = spectrum
    acc[...] += dot(cos_across_ref[0:rows, :], yc) + dot(sin_across_ref[0:rows, :], ys)

    @pl.when(step == pl.num_programs(0) - 1)
    def _():
        forward_end(out_ref, acc, freqs)


def backward_begin(grads, medium_ref, delayed, signal, medium):
    parts, length, _ = grads.shape
    medium[...] = jnp.zeros_like(medium)
    medium[0 : medium_ref.shape[0], :] = medium_ref[...].astype(BF16)
    delayed[...] = jnp.zeros_like(delayed)
    for s in range(parts):
        delayed[s * length + 1 : (s + 1) * length + 1, :] = grads[s].astype(F32)
    signal[...] = delayed[...].astype(BF16)


def backward_spectra(cosine, sine, signal, medium, spectra):
    gc = dot(cosine, signal[...])
    gs = dot(sine, signal[...])
    ac, as_, hc, hs = spectra
    kept = medium.shape[0]
    mc = dot(cosine[:, 0:kept], medium[...])
    ms = dot(sine[:, 0:kept], medium[...])
    uc = hc * gc + hs * gs
    us = hc * gs - hs * gc
    xc = ac * mc - as_ * ms
    xs = ac * ms + as_ * mc
    both_c = jnp.concatenate([xc * gc + xs * gs, mc * uc + ms * us], 1).astype(BF16)
    both_s = jnp.concatenate([xc * gs - xs * gc, mc * us - ms * uc], 1).astype(BF16)
    return both_c, both_s, (ac * uc + as_ * us).astype(BF16), (ac * us - as_ * uc).astype(BF16)


def backward_end(
    streams, taps_ref, kept, out_ref, packed, small_ref, ext, after, acc, tap_acc, sems, freqs, scale, medium_reach
):
    parts, rows, width = packed.shape
    length = (ext.shape[1] - HALO) // parts
    tokens = parts * length
    reach = taps_ref.shape[1]
    inverse = 1.0 / freqs
    first = length + 2 * HALO
    head = first + length
    after[:, tokens : tokens + HALO, :] = jnp.zeros((2, HALO, width), F32)
    for s in range(parts):
        here = slice(s * length, (s + 1) * length)
        packed[s, first:head, :] = (acc[here, 0:width] * (inverse * scale)).astype(BF16)
        gated = acc[here, width : 2 * width] * inverse
        packed[s, 0:length, :] = gated.astype(BF16)
        after[0, here, :] = gated * kept[1, here, :]
        after[1, here, :] = gated * kept[0, here, :]
    for s in range(parts):
        end = (s + 1) * length
        for j in range(2):
            begin = length + j * HALO
            packed[s, begin : begin + HALO, :] = after[j, end : end + HALO, :].astype(BF16)
    writes = [
        pltpu.make_async_copy(packed.at[:, pl.ds(0, head), :], out_ref.at[:, pl.ds(0, head), :], sems.at[0]),
        pltpu.make_async_copy(
            packed.at[:, pl.ds(head, rows - head), :], out_ref.at[:, pl.ds(head, rows - head), :], sems.at[1]
        ),
    ]
    writes[0].start()
    extend(streams, ext)
    small_ref[...] = jnp.zeros_like(small_ref)
    small_ref[0:medium_reach, :] = tap_acc[0:medium_reach, :] * (inverse * scale)
    for j in range(2):
        sums = [jnp.zeros((8, width), F32) for _ in range(reach)]
        for s in range(parts):
            begin = s * length
            own = after[j, begin : begin + length, :]
            for i in range(reach):
                moved = ext[j, HALO + begin - i : HALO + begin - i + length, :]
                sums[i] = sums[i] + jnp.sum((moved * own).reshape(length // 8, 8, width), 0)
        for i in range(reach):
            row = medium_reach + j * reach + i
            small_ref[row : row + 1, :] = jnp.sum(sums[i], 0, keepdims=True) * scale
    small = small_ref[...].astype(BF16)
    for s in range(parts):
        packed[s, head:, :] = small
    writes[1].start()
    wait_all(writes)


def backward_kernel(
    taps_ref, medium_ref, grads_ref, got_ref, kept_ref, spectra_ref, cos_ref, sin_ref, *refs,
    freqs, block, scale, medium_reach, resident,
):
    if not resident:
        cos_across_ref, sin_across_ref, *refs = refs
    out_ref, packed, small, delayed, signal, ext, after, acc, tap_acc, streams, kept, grads, medium, *refs = refs
    late_sems, write_sems, *refs = refs
    step = pl.program_id(0)
    size = signal.shape[0]
    rows, taps_kept = (acc.shape[0], tap_acc.shape[0])
    late = [
        pltpu.make_async_copy(kept_ref, kept, late_sems.at[0]),
        pltpu.make_async_copy(got_ref.at[:, pl.ds(0, streams.shape[1]), :], streams, late_sems.at[1]),
    ]
    early = pltpu.make_async_copy(grads_ref, grads, late_sems.at[2])

    def end():
        wait_all(late)
        backward_end(
            streams, taps_ref, kept, out_ref, packed, small, ext, after, acc, tap_acc, write_sems,
            freqs, scale, medium_reach,
        )

    if resident:
        held, both_c_all, both_s_all, taps_c_all, taps_s_all, spectra_held, sems = refs
        groups = block_copies((cos_ref, sin_ref), held, spectra_ref, spectra_held, sems, freqs // block)
        early.start()
        for group in groups:
            start_all(group)
        start_all(late)
        early.wait()
        backward_begin(grads, medium_ref, delayed, signal, medium)
        for b, group in enumerate(groups):
            wait_all(group)
            here = slice(b * block, (b + 1) * block)
            spectra = [spectra_held[i, here, :] for i in range(spectra_held.shape[0])]
            both_c_all[here, :], both_s_all[here, :], taps_c_all[here, :], taps_s_all[here, :] = backward_spectra(
                held[0, here, 0:size], held[1, here, 0:size], signal, medium, spectra
            )
        acc[...] = dot(held[0, 0:rows, :], both_c_all[...]) + dot(held[1, 0:rows, :], both_s_all[...])
        tap_acc[...] = dot(held[0, 0:taps_kept, :], taps_c_all[...]) + dot(held[1, 0:taps_kept, :], taps_s_all[...])
        end()
        return

    @pl.when(step == 0)
    def _():
        early.start()
        early.wait()
        backward_begin(grads, medium_ref, delayed, signal, medium)
        acc[...] = jnp.zeros_like(acc)
        tap_acc[...] = jnp.zeros_like(tap_acc)

    spectra = [spectra_ref[i] for i in range(spectra_ref.shape[0])]
    both_c, both_s, taps_c, taps_s = backward_spectra(cos_ref[:, 0:size], sin_ref[:, 0:size], signal, medium, spectra)
    acc[...] += dot(cos_across_ref[0:rows, :], both_c) + dot(sin_across_ref[0:rows, :], both_s)
    tap_acc[...] += dot(cos_across_ref[0:taps_kept, :], taps_c) + dot(sin_across_ref[0:taps_kept, :], taps_s)

    @pl.when(step == pl.num_programs(0) - 1)
    def _():
        start_all(late)
        end()


def spectral_plan(freqs, block, tables):
    if freqs * freqs <= TABLE_LIMIT:
        hbm = pl.BlockSpec(memory_space=pltpu.HBM)
        return True, 1, [hbm, hbm], [in_hbm(t) for t in tables]
    rows = pl.BlockSpec((block, freqs), lambda j: (j, 0))
    columns = pl.BlockSpec((freqs, block), lambda j: (0, j))
    return False, freqs // block, [rows, rows, columns, columns], [*tables, *tables]


def held_scratch(freqs, block, width, widths, kinds):
    blocks = freqs // block
    return (
        [pltpu.VMEM((2, freqs, freqs), BF16)]
        + [pltpu.VMEM((freqs, w), BF16) for w in widths]
        + [pltpu.VMEM((4, freqs, width), F32), pltpu.SemaphoreType.DMA((kinds, blocks))]
    )


def forward_call(got, taps, medium_taps, tables, freqs, block):
    parts, tall, width = got.shape
    length = tall // 3
    tokens = parts * length
    padded = -(-medium_taps.shape[0] // 128) * 128
    resident, steps, specs, operands = spectral_plan(freqs, block, tables)
    per = freqs // steps
    hbm = pl.BlockSpec(memory_space=pltpu.HBM)
    return pl.pallas_call(
        partial(forward_kernel, freqs=freqs, block=block, resident=resident),
        grid=(steps,),
        in_specs=[whole(got.shape), whole(taps.shape), whole(medium_taps.shape)] + specs,
        out_specs=[
            whole((parts, length, width)),
            hbm,
            hbm if resident else pl.BlockSpec((4, per, width), lambda j: (0, j, 0)),
        ],
        out_shape=[
            pltpu.HBM((parts, length, width), BF16),
            pltpu.HBM((2, tokens, width), F32),
            pltpu.HBM((4, freqs, width), F32),
        ],
        scratch_shapes=[
            pltpu.VMEM((2, tokens + HALO, width), F32),
            pltpu.VMEM((tokens, 2 * width), BF16),
            pltpu.VMEM((padded, width), BF16),
            pltpu.VMEM((tokens + HALO, width), F32),
            pltpu.VMEM((2, tokens, width), F32),
            pltpu.SemaphoreType.DMA,
        ]
        + (
            held_scratch(freqs, block, width, (width, width), 2) + [pltpu.SemaphoreType.DMA((freqs // block,))]
            if resident
            else []
        ),
        compiler_params=limit(32 if resident else 60),
        name="forward_spectral",
    )(in_hbm(got), taps, medium_taps, *operands)


def backward_call(got, grads, taps, medium_taps, kept, spectra, tables, freqs, block, scale, medium_reach, rows, small, extra):
    parts, tall, width = got.shape
    length = tall // 3
    tokens = parts * length
    padded = -(-medium_reach // 128) * 128
    late = -(-(tokens + 1) // 128) * 128
    resident, steps, specs, operands = spectral_plan(freqs, block, tables)
    per = freqs // steps
    hbm = pl.BlockSpec(memory_space=pltpu.HBM)
    return pl.pallas_call(
        partial(
            backward_kernel, freqs=freqs, block=block, scale=scale, medium_reach=medium_reach, resident=resident
        ),
        grid=(steps,),
        in_specs=[
            whole(taps.shape),
            whole(medium_taps.shape),
            pl.BlockSpec(memory_space=pl.ANY),
            hbm,
            hbm,
            hbm if resident else pl.BlockSpec((4, per, width), lambda j: (0, j, 0)),
        ]
        + specs,
        out_specs=hbm,
        out_shape=pltpu.HBM((parts, rows + small + extra, width), BF16),
        scratch_shapes=[
            pltpu.VMEM((parts, rows + small, width), BF16),
            pltpu.VMEM((small, width), F32),
            pltpu.VMEM((late, width), F32),
            pltpu.VMEM((late, width), BF16),
            pltpu.VMEM((2, tokens + HALO, width), F32),
            pltpu.VMEM((2, tokens + HALO, width), F32),
            pltpu.VMEM((tokens, 2 * width), F32),
            pltpu.VMEM((padded, width), F32),
            pltpu.VMEM((parts, 2 * length, width), BF16),
            pltpu.VMEM((2, tokens, width), F32),
            pltpu.VMEM((parts, length, width), BF16),
            pltpu.VMEM((padded, width), BF16),
            pltpu.SemaphoreType.DMA((3,)),
            pltpu.SemaphoreType.DMA((2,)),
        ]
        + (held_scratch(freqs, block, width, (2 * width, 2 * width, width, width), 3) if resident else []),
        compiler_params=limit(40 if resident else 60),
        name="backward_spectral",
    )(taps, medium_taps, grads, in_hbm(got), in_hbm(kept), in_hbm(spectra), *operands)


def product_kernel(
    got_ref, query_ref, grad_ref, x_ref, edge_ref, _, product_ref, query_grad_ref, first_ref, back_ref,
    got, query, grad, x, product, query_grad, first, ext, taps, rounded, sems, *, reach, begin,
):
    parts, length, width = got.shape
    reads = [
        pltpu.make_async_copy(source, held, sems.at[i])
        for i, (source, held) in enumerate(((x_ref.at[0], x), (got_ref, got), (grad_ref, grad), (query_ref, query)))
    ]
    start_all(reads)
    ext[0:HALO, :] = edge_ref[0].astype(F32)
    taps[...] = jnp.zeros_like(taps)
    reads[0].wait()
    ext[HALO:, :] = x[...].astype(F32)
    wait_all(reads[1:3])
    for j in range(parts):
        lanes = slice(j * width, (j + 1) * width)
        own = grad[:, lanes] * got[j].astype(F32)
        query_grad[:, lanes] = own
        first[:, lanes] = own[0:HALO].astype(BF16)
        for i in range(reach):
            moved = ext[HALO - i : HALO - i + length, lanes]
            taps[j * reach + i : j * reach + i + 1, :] = jnp.sum(moved * own, 0, keepdims=True)
    for s in range(parts):
        rounded[s] = taps[...].astype(BF16)
    writes = [
        pltpu.make_async_copy(rounded, back_ref.at[:, pl.ds(begin, taps.shape[0]), :], sems.at[4]),
        pltpu.make_async_copy(query_grad, query_grad_ref, sems.at[5]),
        pltpu.make_async_copy(first, first_ref, sems.at[6]),
        pltpu.make_async_copy(product, product_ref, sems.at[7]),
    ]
    start_all(writes[0:3])
    reads[3].wait()
    for j in range(parts):
        lanes = slice(j * width, (j + 1) * width)
        product[:, lanes] = (query[:, lanes] * got[j].astype(F32)).astype(BF16)
    writes[3].start()
    wait_all(writes)


def product_call(convolved, query, grad, streams, edge, back, reach, begin):
    parts, length, width = convolved.shape
    channels = parts * width
    extra = back.shape[1] - begin
    hbm = pl.BlockSpec(memory_space=pltpu.HBM)
    return pl.pallas_call(
        partial(product_kernel, reach=reach, begin=begin),
        grid=(1,),
        in_specs=[pl.BlockSpec(memory_space=pl.ANY), hbm, hbm, hbm, whole((1, HALO, channels)), hbm],
        out_specs=[hbm] * 4,
        out_shape=[
            pltpu.HBM((length, channels), BF16),
            pltpu.HBM((length, channels), F32),
            pltpu.HBM((HALO, channels), BF16),
            pltpu.HBM(back.shape, BF16),
        ],
        scratch_shapes=[
            pltpu.VMEM((parts, length, width), BF16),
            pltpu.VMEM((length, channels), F32),
            pltpu.VMEM((length, channels), F32),
            pltpu.VMEM((length, channels), BF16),
            pltpu.VMEM((length, channels), BF16),
            pltpu.VMEM((length, channels), F32),
            pltpu.VMEM((HALO, channels), BF16),
            pltpu.VMEM((length + HALO, channels), F32),
            pltpu.VMEM((extra, width), F32),
            pltpu.VMEM((parts, extra, width), BF16),
            pltpu.SemaphoreType.DMA((8,)),
        ],
        input_output_aliases={5: 3},
        compiler_params=limit(16),
        name="product",
    )(convolved, in_hbm(query), in_hbm(grad), in_hbm(streams), edge, in_hbm(back))


def project_kernel(place_ref, product_ref, w_ref, *refs, flips):
    out_refs = refs[: len(flips)]
    buffer, sems = refs[len(flips) :]
    copies = weight_chunks(place_ref, w_ref, buffer, sems, flips, out_refs[0].shape[1])
    start_all(copies)
    deep = buffer.shape[1]
    per = len(copies) // len(flips)
    for slot, copy in enumerate(copies):
        copy.wait()
        part = lax.dot_general(
            product_ref[...], buffer[slot], (((1,), (1,)), ((), ())), preferred_element_type=F32
        )
        lanes = slice(slot % per * deep, (slot % per + 1) * deep)
        out = out_refs[slot // per]
        out[:, lanes] = part.astype(out.dtype)


def project(product, weight, place, flips, features, dtypes):
    length = product.shape[0]
    vmem = pl.BlockSpec(memory_space=pltpu.VMEM)
    return pl.pallas_call(
        partial(project_kernel, flips=flips),
        in_specs=[pl.BlockSpec(memory_space=pltpu.SMEM), vmem, pl.BlockSpec(memory_space=pltpu.HBM)],
        out_specs=[vmem] * len(flips),
        out_shape=[jax.ShapeDtypeStruct((length, features), dtype) for dtype in dtypes],
        scratch_shapes=chunk_scratch(weight, features, len(flips)),
        compiler_params=limit(16),
        name="project",
    )(place, product, weight)


def local_kernel(x_ref, edge_ref, taps_ref, out_ref, ext):
    _, length, channels = out_ref.shape
    for j in range(2):
        ext[0:HALO, :] = edge_ref[j + 1].astype(F32)
        ext[HALO:, :] = x_ref[j + 1].astype(F32)
        for begin in range(0, channels, LANES):
            lanes = slice(begin, min(begin + LANES, channels))
            total = taps_ref[j + 1, 0:1, lanes] * ext[HALO : HALO + length, lanes]
            for i in range(1, taps_ref.shape[1]):
                total = total + taps_ref[j + 1, i : i + 1, lanes] * ext[HALO - i : HALO - i + length, lanes]
            out_ref[j, :, lanes] = total


def finish_kernel(
    got_ref, query_grad_ref, next_ref, taps_ref, local_ref,
    input_grad_ref, filter_ref, medium_ref, short_ref,
    got, local, ext, input_grad, filtering, medium, sums, sems, *, own_rows, scale,
):
    parts, _, width = got.shape
    length = filtering.shape[0]
    reach = taps_ref.shape[1]
    medium_reach = medium.shape[0]
    reads = [
        pltpu.make_async_copy(query_grad_ref, ext.at[0, pl.ds(0, length), :], sems.at[0]),
        pltpu.make_async_copy(got_ref, got, sems.at[1]),
        pltpu.make_async_copy(local_ref, local, sems.at[2]),
    ]
    start_all(reads)

    def convolve(k):
        for j in range(parts):
            lanes = slice(j * width, (j + 1) * width)
            total = taps_ref[k, 0:1, lanes] * ext[k, 0:length, lanes]
            for i in range(1, reach):
                total = total + taps_ref[k, i : i + 1, lanes] * ext[k, i : i + length, lanes]
            input_grad[k, :, lanes] = total.astype(BF16)

    writes = [
        pltpu.make_async_copy(input_grad.at[k], input_grad_ref.at[k], sems.at[3 + k]) for k in range(3)
    ]
    more = [
        pltpu.make_async_copy(filtering, filter_ref, sems.at[6]),
        pltpu.make_async_copy(medium, medium_ref, sems.at[7]),
    ]
    ext[0, length:, :] = next_ref[...].astype(F32)
    reads[0].wait()
    convolve(0)
    writes[0].start()
    reads[1].wait()
    after = length + 2 * HALO
    first = after + length
    taps = first + own_rows
    total = got[0, taps:, :].astype(F32)
    for j in range(1, parts):
        total = total + got[j, taps:, :].astype(F32)
    sums[...] = total
    for j in range(parts):
        lanes = slice(j * width, (j + 1) * width)
        filtering[:, lanes] = got[j, after:first, :].astype(F32)
        small = got[j, first:taps, :].astype(F32)
        medium[:, lanes] = small[0:medium_reach, :]
        second = medium_reach + reach
        short_ref[0, :, lanes] = sums[j * reach : (j + 1) * reach, :] * scale
        short_ref[1, :, lanes] = small[medium_reach:second, :]
        short_ref[2, :, lanes] = small[second : second + reach, :]
    start_all(more)
    reads[2].wait()
    for k in range(1, 3):
        for j in range(parts):
            lanes = slice(j * width, (j + 1) * width)
            ext[k, 0:length, lanes] = got[j, 0:length, :].astype(F32) * local[2 - k, :, lanes]
            begin = length + (k - 1) * HALO
            ext[k, length:, lanes] = got[j, begin : begin + HALO, :].astype(F32)
        convolve(k)
        writes[k].start()
    wait_all(writes + more)


def finish_call(returned, query_grad, next_grad, taps, features, medium_reach, own_rows, scale):
    parts, _, width = returned.shape
    groups, reach, channels = taps.shape
    length = query_grad.shape[0]
    hbm = pl.BlockSpec(memory_space=pltpu.HBM)
    return pl.pallas_call(
        partial(finish_kernel, own_rows=own_rows, scale=scale),
        grid=(1,),
        in_specs=[pl.BlockSpec(memory_space=pl.ANY), hbm, whole((HALO, channels)), whole(taps.shape), hbm],
        out_specs=[hbm, hbm, hbm, whole((groups, reach, channels))],
        out_shape=[
            pltpu.HBM((groups, length, channels), BF16),
            pltpu.HBM((length, channels), F32),
            pltpu.HBM((medium_reach, channels), F32),
            jax.ShapeDtypeStruct((groups, reach, channels), F32),
        ],
        scratch_shapes=[
            pltpu.VMEM(returned.shape, BF16),
            pltpu.VMEM((2, length, channels), F32),
            pltpu.VMEM((groups, length + HALO, channels), F32),
            pltpu.VMEM((groups, length, channels), BF16),
            pltpu.VMEM((length, channels), F32),
            pltpu.VMEM((medium_reach, channels), F32),
            pltpu.VMEM((-(-parts * reach // 16) * 16, width), F32),
            pltpu.SemaphoreType.DMA((8,)),
        ],
        compiler_params=limit(16),
        name="finish",
    )(returned, in_hbm(query_grad), next_grad, taps, in_hbm(features))


def reshard(value):
    return lax.all_to_all(value, "seq", split_axis=0, concat_axis=0, tiled=True)


def local(inputs, short_taps, medium_taps, long_filter, out_weight, out_cotangent):
    length, _, channels = inputs.shape
    reach = short_taps.shape[0]
    medium_reach = medium_taps.shape[0]
    parts = lax.axis_size("seq")
    position = lax.axis_index("seq")
    place = lax.axis_index("tensor").astype(jnp.int32)[None]
    features = out_cotangent.shape[1]
    width = channels // parts
    tokens = length * parts
    scale = 1.0 / math.sqrt(tokens)
    freqs, block = spectral_sizes(tokens, medium_reach)
    vmem = pl.BlockSpec(memory_space=pltpu.VMEM)

    weight = pltpu.with_memory_space_constraint(out_weight, pltpu.HBM)
    streams = inputs.transpose(1, 0, 2)
    taps = short_taps.transpose(1, 0, 2)
    hbm = pl.BlockSpec(memory_space=pltpu.HBM)
    packed = pl.pallas_call(
        pack_kernel,
        in_specs=[hbm, hbm],
        out_specs=hbm,
        out_shape=pltpu.HBM((parts, 3 * length, width), BF16),
        scratch_shapes=[
            pltpu.VMEM((2, length, channels), BF16),
            pltpu.VMEM((length, channels), F32),
            pltpu.VMEM((parts, 3 * length, width), BF16),
            pltpu.SemaphoreType.DMA((2 + parts,)),
        ],
        compiler_params=limit(8),
        name="pack",
    )(
        pltpu.with_memory_space_constraint(streams, pltpu.HBM),
        pltpu.with_memory_space_constraint(long_filter, pltpu.HBM),
    )
    got = reshard(packed)
    edge = shift(streams[:, length - HALO :], "seq", 1)
    cot_x = exchange(out_cotangent, "tensor", 2)
    cot_core = exchange(out_cotangent, "tensor", 1)

    tables = dft_tables(freqs)
    own_taps = lax.dynamic_slice_in_dim(taps, position * width, width, 2)
    own_medium = lax.dynamic_slice_in_dim(medium_taps, position * width, width, 1)

    acc = product_grad_first((out_cotangent, cot_core), weight, place, (0, 1))
    cot_far = exchange(cot_x, "tensor", 1)
    product_grad, query, sent = product_grad_last((cot_x, cot_far), weight, place, (2, 3), acc, streams, taps, parts)
    query, sent = with_edge(streams, edge, taps, product_grad, query, sent)
    grads = reshard(sent)

    convolved, kept, spectra = forward_call(got, own_taps, own_medium, tables, freqs, block)
    convolved = reshard(convolved)

    rows = 2 * length + 2 * HALO
    small = -(-(medium_reach + 2 * reach) // 16) * 16
    extra = -(-parts * reach // 16) * 16
    back = backward_call(
        got, grads, own_taps, own_medium, kept, spectra, tables, freqs, block, scale, medium_reach, rows, small, extra
    )
    product, query_grad, first_rows, back = product_call(
        convolved, query, product_grad, streams, edge, back, reach, rows + small
    )
    returned = reshard(back)

    (far,) = project(product, weight, place, (3,), features, (BF16,))
    far_core = exchange(far, "tensor", 1)
    (across,) = project(product, weight, place, (2,), features, (F32,))
    across_sum = exchange((across + far_core.astype(F32)).astype(BF16), "tensor", 2)
    near, own = project(product, weight, place, (1, 0), features, (BF16, F32))
    near_core = exchange(near, "tensor", 1)
    next_grad = shift(first_rows, "seq", -1)

    local_features = pl.pallas_call(
        local_kernel,
        in_specs=[vmem] * 3,
        out_specs=vmem,
        out_shape=pltpu.HBM((2, length, channels), F32),
        scratch_shapes=[pltpu.VMEM((length + HALO, channels), F32)],
        compiler_params=limit(8),
        name="local",
    )(in_hbm(streams), edge, taps)
    input_grad, filter_grad, medium_grad, short_grad = finish_call(
        returned, query_grad, next_grad, taps, local_features, medium_reach, small, scale
    )

    output = (own + near_core.astype(F32) + across_sum.astype(F32)).astype(BF16)
    return (
        output,
        input_grad.transpose(1, 0, 2),
        filter_grad,
        medium_grad,
        short_grad.transpose(1, 0, 2),
    )


def solution(mesh):
    return jax.shard_map(
        local,
        mesh=mesh,
        in_specs=(
            P("seq", None, "tensor"),
            P(None, None, "tensor"),
            P(None, "tensor"),
            P("seq", "tensor"),
            P(None, "tensor"),
            P("seq", "tensor"),
        ),
        out_specs=(
            P("seq", "tensor"),
            P("seq", None, "tensor"),
            P("seq", "tensor"),
            P(None, "tensor"),
            P(None, None, "tensor"),
        ),
        check_vma=False,
    )
```

```python
import math
from functools import partial

import jax
import jax.numpy as jnp
from jax import lax
from jax.experimental import pallas as pl
from jax.experimental.pallas import tpu as pltpu
from jax.sharding import PartitionSpec as P


F32 = jnp.float32
BF16 = jnp.bfloat16
HALO = 8
GROUP = 32
CHUNK = 512
TABLE_LIMIT = 1 << 22


def dot(a, b):
    return lax.dot_general(a, b, (((1,), (0,)), ((), ())), preferred_element_type=F32)


def exchange(value, axis, flip):
    count = lax.axis_size(axis)
    return lax.ppermute(value, axis, [(source, source ^ flip) for source in range(count)])


def shift(value, axis, steps):
    count = lax.axis_size(axis)
    pairs = [(s, s + steps) for s in range(count) if 0 <= s + steps < count]
    return lax.ppermute(value, axis, pairs)


def whole(shape):
    return pl.BlockSpec(shape, lambda *_: (0,) * len(shape))


def spectral_sizes(tokens, medium_reach):
    need = tokens + -(-(medium_reach - 2) // 2)
    freqs = -(-need // 384) * 384
    return freqs, 384


def dft_tables(freqs):
    period = 8 * freqs
    unit = 2.0 * math.pi / period
    odd = 2 * jnp.arange(freqs, dtype=jnp.int32) + 1
    start = 2 * GROUP * jnp.arange(freqs // GROUP, dtype=jnp.int32)
    inner = 2 * jnp.arange(GROUP, dtype=jnp.int32) + 1
    first = (start[:, None] * odd[None, :] % period).astype(F32) * unit
    second = (inner[:, None] * odd[None, :] % period).astype(F32) * unit
    fc, fs = jnp.cos(first)[:, None], jnp.sin(first)[:, None]
    sc, ss = jnp.cos(second)[None], jnp.sin(second)[None]
    cosine = (fc * sc - fs * ss).astype(BF16).reshape(freqs, freqs)
    sine = (fs * sc + fc * ss).astype(BF16).reshape(freqs, freqs)
    return cosine, sine


def in_hbm(value):
    return pltpu.with_memory_space_constraint(value, pltpu.HBM)


def limit(mebibytes):
    return pltpu.CompilerParams(vmem_limit_bytes=mebibytes << 20)


def pack_kernel(x_ref, filter_ref, out_ref, streams, taps, rounded, sems):
    parts, rows, width = out_ref.shape
    length = rows // 3
    read_filter = pltpu.make_async_copy(filter_ref, taps, sems.at[0])
    read_streams = pltpu.make_async_copy(x_ref.at[pl.ds(1, 2)], streams, sems.at[1])
    read_filter.start()
    read_streams.start()
    read_filter.wait()
    for j in range(parts):
        rounded[j, 2 * length :, :] = taps[:, j * width : (j + 1) * width].astype(BF16)
    read_streams.wait()
    writes = []
    for j in range(parts):
        lanes = slice(j * width, (j + 1) * width)
        rounded[j, 0:length, :] = streams[0, :, lanes]
        rounded[j, length : 2 * length, :] = streams[1, :, lanes]
        writes.append(pltpu.make_async_copy(rounded.at[j], out_ref.at[j], sems.at[2 + j]))
        writes[j].start()
    for write in writes:
        write.wait()


def weight_chunks(place_ref, weight_ref, buffer, sems, flips, features):
    deep = buffer.shape[1]
    per = features // deep
    copies = []
    for i, flip in enumerate(flips):
        for k in range(per):
            start = jnp.bitwise_xor(place_ref[0], flip) * features + k * deep
            slot = i * per + k
            copies.append(
                pltpu.make_async_copy(
                    weight_ref.at[pl.ds(pl.multiple_of(start, deep), deep), :], buffer.at[slot], sems.at[slot]
                )
            )
    return copies


def chunk_scratch(weight, features, shards):
    deep = math.gcd(features, CHUNK)
    count = shards * (features // deep)
    return [pltpu.VMEM((count, deep, weight.shape[1]), weight.dtype), pltpu.SemaphoreType.DMA((count,))]


def summed(x_refs, copies, buffer, total):
    deep = buffer.shape[1]
    per = len(copies) // len(x_refs)
    for slot, copy in enumerate(copies):
        copy.wait()
        lanes = slice(slot % per * deep, (slot % per + 1) * deep)
        part = dot(x_refs[slot // per][:, lanes], buffer[slot])
        total = part if total is None else total + part
    return total


def product_grad_kernel(place_ref, w_ref, *refs, flips, last):
    x_refs = refs[: len(flips)]
    copies_in = []
    if last:
        acc_ref, x_ref, taps_ref, out_ref, query_ref, sent_ref, buffer, sems, ext, held, in_sems = refs[len(flips) :]
    else:
        out_ref, buffer, sems, held, in_sems = refs[len(flips) :]
    for i, ref in enumerate(x_refs):
        copies_in.append(pltpu.make_async_copy(ref, held.at[i], in_sems.at[i]))
        copies_in[i].start()
    copies = weight_chunks(place_ref, w_ref, buffer, sems, flips, held.shape[2])
    for copy in copies:
        copy.start()
    if last:
        length = x_ref.shape[1]
        parts, _, width = ext.shape
        for j in range(parts):
            lanes = slice(j * width, (j + 1) * width)
            ext[j, 0:HALO, :] = jnp.zeros((HALO, width), F32)
            ext[j, HALO:, :] = x_ref[0, :, lanes].astype(F32)
            query = taps_ref[0, 0:1, lanes] * ext[j, HALO : HALO + length, :]
            for i in range(1, taps_ref.shape[1]):
                query = query + taps_ref[0, i : i + 1, lanes] * ext[j, HALO - i : HALO - i + length, :]
            query_ref[:, lanes] = query
    for copy in copies_in:
        copy.wait()
    total = summed([held.at[i] for i in range(len(flips))], copies, buffer, acc_ref[...] if last else None)
    out_ref[...] = total
    if last:
        parts, _, width = sent_ref.shape
        for j in range(parts):
            lanes = slice(j * width, (j + 1) * width)
            sent_ref[j] = (total[:, lanes] * query_ref[:, lanes]).astype(BF16)


def grad_scratch(shards, weight, length, features):
    return chunk_scratch(weight, features, shards), [
        pltpu.VMEM((shards, length, features), BF16),
        pltpu.SemaphoreType.DMA((shards,)),
    ]


def product_grad_first(shards, weight, place, flips):
    length, features = shards[0].shape
    channels = weight.shape[1]
    hbm = pl.BlockSpec(memory_space=pltpu.HBM)
    chunks, inputs = grad_scratch(len(flips), weight, length, features)
    return pl.pallas_call(
        partial(product_grad_kernel, flips=flips, last=False),
        in_specs=[pl.BlockSpec(memory_space=pltpu.SMEM), hbm] + [pl.BlockSpec(memory_space=pl.ANY)] * len(shards),
        out_specs=pl.BlockSpec(memory_space=pltpu.VMEM),
        out_shape=jax.ShapeDtypeStruct((length, channels), F32),
        scratch_shapes=chunks + inputs,
        compiler_params=limit(16),
        name="grad_first",
    )(place, weight, in_hbm(shards[0]), *shards[1:])


def product_grad_last(shards, weight, place, flips, acc, streams, taps, parts):
    length, features = shards[0].shape
    channels = weight.shape[1]
    hbm = pl.BlockSpec(memory_space=pltpu.HBM)
    vmem = pl.BlockSpec(memory_space=pltpu.VMEM)
    full = whole((length, channels))
    chunks, inputs = grad_scratch(len(flips), weight, length, features)
    return pl.pallas_call(
        partial(product_grad_kernel, flips=flips, last=True),
        grid=(1,),
        in_specs=[pl.BlockSpec(memory_space=pltpu.SMEM)]
        + [hbm]
        + [pl.BlockSpec(memory_space=pl.ANY)] * len(shards)
        + [full, whole((1, length, channels)), whole(taps.shape)],
        out_specs=[full, full, whole((parts, length, channels // parts))],
        out_shape=[
            pltpu.HBM((length, channels), F32),
            pltpu.HBM((length, channels), F32),
            pltpu.HBM((parts, length, channels // parts), BF16),
        ],
        scratch_shapes=chunks + [pltpu.VMEM((parts, length + HALO, channels // parts), F32)] + inputs,
        compiler_params=limit(24),
        name="grad_last",
    )(place, weight, *shards, acc, streams, taps)


def edge_kernel(x_ref, edge_ref, taps_ref, grad_ref, _, __, query_ref, sent_ref, ext, query, sent, sems):
    parts, _, width = sent.shape
    ext[0:HALO, :] = edge_ref[0].astype(F32)
    ext[HALO:, :] = x_ref[0].astype(F32)[0:HALO]
    total = taps_ref[0, 0:1, :] * ext[HALO : 2 * HALO, :]
    for i in range(1, taps_ref.shape[1]):
        total = total + taps_ref[0, i : i + 1, :] * ext[HALO - i : 2 * HALO - i, :]
    query[...] = total
    for j in range(parts):
        lanes = slice(j * width, (j + 1) * width)
        sent[j] = (grad_ref[:, lanes] * total[:, lanes]).astype(BF16)
    copies = [
        pltpu.make_async_copy(query, query_ref.at[pl.ds(0, HALO), :], sems.at[0]),
        pltpu.make_async_copy(sent, sent_ref.at[:, pl.ds(0, HALO), :], sems.at[1]),
    ]
    for copy in copies:
        copy.start()
    for copy in copies:
        copy.wait()


def with_edge(streams, edge, taps, grad, query, sent):
    channels = streams.shape[2]
    parts, _, width = sent.shape
    hbm = pl.BlockSpec(memory_space=pltpu.HBM)
    return pl.pallas_call(
        edge_kernel,
        grid=(1,),
        in_specs=[
            whole((1, 2 * HALO, channels)),
            whole((1, HALO, channels)),
            whole(taps.shape),
            whole((HALO, channels)),
            hbm,
            hbm,
        ],
        out_specs=[hbm, hbm],
        out_shape=[pltpu.HBM(query.shape, F32), pltpu.HBM(sent.shape, BF16)],
        scratch_shapes=[
            pltpu.VMEM((2 * HALO, channels), F32),
            pltpu.VMEM((HALO, channels), F32),
            pltpu.VMEM((parts, HALO, width), BF16),
            pltpu.SemaphoreType.DMA((2,)),
        ],
        input_output_aliases={4: 0, 5: 1},
        compiler_params=limit(4),
        name="edge_rows",
    )(streams, edge, taps, in_hbm(grad), in_hbm(query), in_hbm(sent))


def filtered(taps_ref, stream, ext, begin, length):
    total = taps_ref[stream + 1, 0:1, :] * ext[stream, HALO + begin : HALO + begin + length, :]
    for i in range(1, taps_ref.shape[1]):
        first = HALO + begin - i
        total = total + taps_ref[stream + 1, i : i + 1, :] * ext[stream, first : first + length, :]
    return total


def extend(got_ref, ext):
    parts, _, width = got_ref.shape
    length = (ext.shape[1] - HALO) // parts
    ext[:, 0:HALO, :] = jnp.zeros((2, HALO, width), F32)
    for s in range(parts):
        here = slice(HALO + s * length, HALO + (s + 1) * length)
        ext[0, here, :] = got_ref[s, 0:length, :].astype(F32)
        ext[1, here, :] = got_ref[s, length : 2 * length, :].astype(F32)


def forward_begin(got_ref, taps_ref, medium_ref, kept, ext, signals, medium):
    parts, rows, width = got_ref.shape
    length = rows // 3
    extend(got_ref, ext)
    for s in range(parts):
        here = slice(s * length, (s + 1) * length)
        key = filtered(taps_ref, 0, ext, s * length, length)
        value = filtered(taps_ref, 1, ext, s * length, length)
        kept[0, here, :] = key
        kept[1, here, :] = value
        signals[here, 0:width] = (key * value).astype(BF16)
        signals[here, width : 2 * width] = got_ref[s, 2 * length : 3 * length, :]
    medium[...] = jnp.zeros_like(medium)
    medium[0 : medium_ref.shape[0], :] = medium_ref[...].astype(BF16)


def forward_spectra(cosine, sine, signals, medium):
    tokens, double = signals.shape
    width = double // 2
    kept = medium.shape[0]
    both_c = dot(cosine[:, 0:tokens], signals[...])
    both_s = dot(sine[:, 0:tokens], signals[...])
    mc = dot(cosine[:, 0:kept], medium[...])
    ms = dot(sine[:, 0:kept], medium[...])
    ac, hc, as_, hs = (both_c[:, :width], both_c[:, width:], both_s[:, :width], both_s[:, width:])
    xc = ac * mc - as_ * ms
    xs = ac * ms + as_ * mc
    saved = (ac, as_, hc, hs)
    return saved, (xc * hc - xs * hs).astype(BF16), (xc * hs + xs * hc).astype(BF16)


def forward_end(out_ref, acc, freqs):
    parts, length, _ = out_ref.shape
    for s in range(parts):
        first = s * length + 1
        out_ref[s] = (acc[first : first + length, :] * (1.0 / freqs)).astype(BF16)


def block_copies(tables, held, spectra, spectra_held, sems, blocks):
    size = held.shape[1] // blocks
    groups = []
    for b in range(blocks):
        here = pl.ds(b * size, size)
        group = [pltpu.make_async_copy(t.at[here, :], held.at[i, here, :], sems.at[i, b]) for i, t in enumerate(tables)]
        if spectra is not None:
            group.append(pltpu.make_async_copy(spectra.at[:, here, :], spectra_held.at[:, here, :], sems.at[2, b]))
        groups.append(group)
    return groups


def start_all(copies):
    for copy in copies:
        copy.start()


def wait_all(copies):
    for copy in copies:
        copy.wait()


def forward_kernel(got_ref, taps_ref, medium_ref, cos_ref, sin_ref, *refs, freqs, block, resident):
    if not resident:
        cos_across_ref, sin_across_ref, *refs = refs
    out_ref, kept_ref, spectra_ref, ext, signals, medium, acc, kept, kept_sem, *refs = refs
    rows = acc.shape[0]
    step = pl.program_id(0)
    keep = pltpu.make_async_copy(kept, kept_ref, kept_sem)

    if resident:
        held, yc_all, ys_all, spectra_held, sems, out_sems = refs
        blocks = freqs // block
        groups = block_copies((cos_ref, sin_ref), held, None, None, sems, blocks)
        for group in groups:
            start_all(group)
        forward_begin(got_ref, taps_ref, medium_ref, kept, ext, signals, medium)
        keep.start()
        writes = []
        for b, group in enumerate(groups):
            wait_all(group)
            here = slice(b * block, (b + 1) * block)
            saved, yc, ys = forward_spectra(held[0, here, :], held[1, here, :], signals, medium)
            for i, spectrum in enumerate(saved):
                spectra_held[i, here, :] = spectrum
            there = pl.ds(b * block, block)
            writes.append(
                pltpu.make_async_copy(spectra_held.at[:, there, :], spectra_ref.at[:, there, :], out_sems.at[b])
            )
            writes[b].start()
            yc_all[here, :] = yc
            ys_all[here, :] = ys
        acc[...] = dot(held[0, 0:rows, :], yc_all[...]) + dot(held[1, 0:rows, :], ys_all[...])
        forward_end(out_ref, acc, freqs)
        wait_all(writes)
        keep.wait()
        return

    @pl.when(step == 0)
    def _():
        forward_begin(got_ref, taps_ref, medium_ref, kept, ext, signals, medium)
        keep.start()
        keep.wait()
        acc[...] = jnp.zeros_like(acc)

    saved, yc, ys = forward_spectra(cos_ref[...], sin_ref[...], signals, medium)
    for i, spectrum in enumerate(saved):
        spectra_ref[i] = spectrum
    acc[...] += dot(cos_across_ref[0:rows, :], yc) + dot(sin_across_ref[0:rows, :], ys)

    @pl.when(step == pl.num_programs(0) - 1)
    def _():
        forward_end(out_ref, acc, freqs)


def backward_begin(grads, medium_ref, delayed, signal, medium):
    parts, length, _ = grads.shape
    medium[...] = jnp.zeros_like(medium)
    medium[0 : medium_ref.shape[0], :] = medium_ref[...].astype(BF16)
    delayed[...] = jnp.zeros_like(delayed)
    for s in range(parts):
        delayed[s * length + 1 : (s + 1) * length + 1, :] = grads[s].astype(F32)
    signal[...] = delayed[...].astype(BF16)


def backward_spectra(cosine, sine, signal, medium, spectra):
    gc = dot(cosine, signal[...])
    gs = dot(sine, signal[...])
    ac, as_, hc, hs = spectra
    kept = medium.shape[0]
    mc = dot(cosine[:, 0:kept], medium[...])
    ms = dot(sine[:, 0:kept], medium[...])
    uc = hc * gc + hs * gs
    us = hc * gs - hs * gc
    xc = ac * mc - as_ * ms
    xs = ac * ms + as_ * mc
    both_c = jnp.concatenate([xc * gc + xs * gs, mc * uc + ms * us], 1).astype(BF16)
    both_s = jnp.concatenate([xc * gs - xs * gc, mc * us - ms * uc], 1).astype(BF16)
    return both_c, both_s, (ac * uc + as_ * us).astype(BF16), (ac * us - as_ * uc).astype(BF16)


def backward_end(
    streams, taps_ref, kept, out_ref, packed, small_ref, ext, after, acc, tap_acc, sems, freqs, scale, medium_reach
):
    parts, rows, width = packed.shape
    length = (ext.shape[1] - HALO) // parts
    tokens = parts * length
    reach = taps_ref.shape[1]
    inverse = 1.0 / freqs
    first = length + 2 * HALO
    head = first + length
    after[:, tokens : tokens + HALO, :] = jnp.zeros((2, HALO, width), F32)
    for s in range(parts):
        here = slice(s * length, (s + 1) * length)
        packed[s, first:head, :] = (acc[here, 0:width] * (inverse * scale)).astype(BF16)
        gated = acc[here, width : 2 * width] * inverse
        packed[s, 0:length, :] = gated.astype(BF16)
        after[0, here, :] = gated * kept[1, here, :]
        after[1, here, :] = gated * kept[0, here, :]
    for s in range(parts):
        end = (s + 1) * length
        for j in range(2):
            begin = length + j * HALO
            packed[s, begin : begin + HALO, :] = after[j, end : end + HALO, :].astype(BF16)
    writes = [
        pltpu.make_async_copy(packed.at[:, pl.ds(0, head), :], out_ref.at[:, pl.ds(0, head), :], sems.at[0]),
        pltpu.make_async_copy(
            packed.at[:, pl.ds(head, rows - head), :], out_ref.at[:, pl.ds(head, rows - head), :], sems.at[1]
        ),
    ]
    writes[0].start()
    extend(streams, ext)
    small_ref[...] = jnp.zeros_like(small_ref)
    small_ref[0:medium_reach, :] = tap_acc[0:medium_reach, :] * (inverse * scale)
    for j in range(2):
        sums = [jnp.zeros((8, width), F32) for _ in range(reach)]
        for s in range(parts):
            begin = s * length
            own = after[j, begin : begin + length, :]
            for i in range(reach):
                moved = ext[j, HALO + begin - i : HALO + begin - i + length, :]
                sums[i] = sums[i] + jnp.sum((moved * own).reshape(length // 8, 8, width), 0)
        for i in range(reach):
            row = medium_reach + j * reach + i
            small_ref[row : row + 1, :] = jnp.sum(sums[i], 0, keepdims=True) * scale
    small = small_ref[...].astype(BF16)
    for s in range(parts):
        packed[s, head:, :] = small
    writes[1].start()
    wait_all(writes)


def backward_kernel(
    taps_ref, medium_ref, grads_ref, got_ref, kept_ref, spectra_ref, cos_ref, sin_ref, *refs,
    freqs, block, scale, medium_reach, resident,
):
    if not resident:
        cos_across_ref, sin_across_ref, *refs = refs
    out_ref, packed, small, delayed, signal, ext, after, acc, tap_acc, streams, kept, grads, medium, *refs = refs
    late_sems, write_sems, *refs = refs
    step = pl.program_id(0)
    size = signal.shape[0]
    rows, taps_kept = (acc.shape[0], tap_acc.shape[0])
    late = [
        pltpu.make_async_copy(kept_ref, kept, late_sems.at[0]),
        pltpu.make_async_copy(got_ref.at[:, pl.ds(0, streams.shape[1]), :], streams, late_sems.at[1]),
    ]
    early = pltpu.make_async_copy(grads_ref, grads, late_sems.at[2])

    def end():
        wait_all(late)
        backward_end(
            streams, taps_ref, kept, out_ref, packed, small, ext, after, acc, tap_acc, write_sems,
            freqs, scale, medium_reach,
        )

    if resident:
        held, both_c_all, both_s_all, taps_c_all, taps_s_all, spectra_held, sems = refs
        groups = block_copies((cos_ref, sin_ref), held, spectra_ref, spectra_held, sems, freqs // block)
        early.start()
        for group in groups:
            start_all(group)
        start_all(late)
        early.wait()
        backward_begin(grads, medium_ref, delayed, signal, medium)
        for b, group in enumerate(groups):
            wait_all(group)
            here = slice(b * block, (b + 1) * block)
            spectra = [spectra_held[i, here, :] for i in range(spectra_held.shape[0])]
            both_c_all[here, :], both_s_all[here, :], taps_c_all[here, :], taps_s_all[here, :] = backward_spectra(
                held[0, here, 0:size], held[1, here, 0:size], signal, medium, spectra
            )
        acc[...] = dot(held[0, 0:rows, :], both_c_all[...]) + dot(held[1, 0:rows, :], both_s_all[...])
        tap_acc[...] = dot(held[0, 0:taps_kept, :], taps_c_all[...]) + dot(held[1, 0:taps_kept, :], taps_s_all[...])
        end()
        return

    @pl.when(step == 0)
    def _():
        early.start()
        early.wait()
        backward_begin(grads, medium_ref, delayed, signal, medium)
        acc[...] = jnp.zeros_like(acc)
        tap_acc[...] = jnp.zeros_like(tap_acc)

    spectra = [spectra_ref[i] for i in range(spectra_ref.shape[0])]
    both_c, both_s, taps_c, taps_s = backward_spectra(cos_ref[:, 0:size], sin_ref[:, 0:size], signal, medium, spectra)
    acc[...] += dot(cos_across_ref[0:rows, :], both_c) + dot(sin_across_ref[0:rows, :], both_s)
    tap_acc[...] += dot(cos_across_ref[0:taps_kept, :], taps_c) + dot(sin_across_ref[0:taps_kept, :], taps_s)

    @pl.when(step == pl.num_programs(0) - 1)
    def _():
        start_all(late)
        end()


def spectral_plan(freqs, block, tables):
    if freqs * freqs <= TABLE_LIMIT:
        hbm = pl.BlockSpec(memory_space=pltpu.HBM)
        return True, 1, [hbm, hbm], [in_hbm(t) for t in tables]
    rows = pl.BlockSpec((block, freqs), lambda j: (j, 0))
    columns = pl.BlockSpec((freqs, block), lambda j: (0, j))
    return False, freqs // block, [rows, rows, columns, columns], [*tables, *tables]


def held_scratch(freqs, block, width, widths, kinds):
    blocks = freqs // block
    return (
        [pltpu.VMEM((2, freqs, freqs), BF16)]
        + [pltpu.VMEM((freqs, w), BF16) for w in widths]
        + [pltpu.VMEM((4, freqs, width), F32), pltpu.SemaphoreType.DMA((kinds, blocks))]
    )


def forward_call(got, taps, medium_taps, tables, freqs, block):
    parts, tall, width = got.shape
    length = tall // 3
    tokens = parts * length
    padded = -(-medium_taps.shape[0] // 128) * 128
    resident, steps, specs, operands = spectral_plan(freqs, block, tables)
    per = freqs // steps
    hbm = pl.BlockSpec(memory_space=pltpu.HBM)
    return pl.pallas_call(
        partial(forward_kernel, freqs=freqs, block=block, resident=resident),
        grid=(steps,),
        in_specs=[whole(got.shape), whole(taps.shape), whole(medium_taps.shape)] + specs,
        out_specs=[
            whole((parts, length, width)),
            hbm,
            hbm if resident else pl.BlockSpec((4, per, width), lambda j: (0, j, 0)),
        ],
        out_shape=[
            pltpu.HBM((parts, length, width), BF16),
            pltpu.HBM((2, tokens, width), F32),
            pltpu.HBM((4, freqs, width), F32),
        ],
        scratch_shapes=[
            pltpu.VMEM((2, tokens + HALO, width), F32),
            pltpu.VMEM((tokens, 2 * width), BF16),
            pltpu.VMEM((padded, width), BF16),
            pltpu.VMEM((tokens + HALO, width), F32),
            pltpu.VMEM((2, tokens, width), F32),
            pltpu.SemaphoreType.DMA,
        ]
        + (
            held_scratch(freqs, block, width, (width, width), 2) + [pltpu.SemaphoreType.DMA((freqs // block,))]
            if resident
            else []
        ),
        compiler_params=limit(32 if resident else 60),
        name="forward_spectral",
    )(in_hbm(got), taps, medium_taps, *operands)


def backward_call(got, grads, taps, medium_taps, kept, spectra, tables, freqs, block, scale, medium_reach, rows, small, extra):
    parts, tall, width = got.shape
    length = tall // 3
    tokens = parts * length
    padded = -(-medium_reach // 128) * 128
    late = -(-(tokens + 1) // 128) * 128
    resident, steps, specs, operands = spectral_plan(freqs, block, tables)
    per = freqs // steps
    hbm = pl.BlockSpec(memory_space=pltpu.HBM)
    return pl.pallas_call(
        partial(
            backward_kernel, freqs=freqs, block=block, scale=scale, medium_reach=medium_reach, resident=resident
        ),
        grid=(steps,),
        in_specs=[
            whole(taps.shape),
            whole(medium_taps.shape),
            pl.BlockSpec(memory_space=pl.ANY),
            hbm,
            hbm,
            hbm if resident else pl.BlockSpec((4, per, width), lambda j: (0, j, 0)),
        ]
        + specs,
        out_specs=hbm,
        out_shape=pltpu.HBM((parts, rows + small + extra, width), BF16),
        scratch_shapes=[
            pltpu.VMEM((parts, rows + small, width), BF16),
            pltpu.VMEM((small, width), F32),
            pltpu.VMEM((late, width), F32),
            pltpu.VMEM((late, width), BF16),
            pltpu.VMEM((2, tokens + HALO, width), F32),
            pltpu.VMEM((2, tokens + HALO, width), F32),
            pltpu.VMEM((tokens, 2 * width), F32),
            pltpu.VMEM((padded, width), F32),
            pltpu.VMEM((parts, 2 * length, width), BF16),
            pltpu.VMEM((2, tokens, width), F32),
            pltpu.VMEM((parts, length, width), BF16),
            pltpu.VMEM((padded, width), BF16),
            pltpu.SemaphoreType.DMA((3,)),
            pltpu.SemaphoreType.DMA((2,)),
        ]
        + (held_scratch(freqs, block, width, (2 * width, 2 * width, width, width), 3) if resident else []),
        compiler_params=limit(40 if resident else 60),
        name="backward_spectral",
    )(taps, medium_taps, grads, in_hbm(got), in_hbm(kept), in_hbm(spectra), *operands)


def product_kernel(
    got_ref, query_ref, grad_ref, x_ref, edge_ref, _, product_ref, query_grad_ref, first_ref, back_ref,
    got, query, grad, x, product, query_grad, first, ext, taps, rounded, sems, *, reach, begin,
):
    parts, length, width = got.shape
    reads = [
        pltpu.make_async_copy(source, held, sems.at[i])
        for i, (source, held) in enumerate(((x_ref.at[0], x), (got_ref, got), (grad_ref, grad), (query_ref, query)))
    ]
    start_all(reads)
    taps[...] = jnp.zeros_like(taps)
    reads[0].wait()
    for j in range(parts):
        lanes = slice(j * width, (j + 1) * width)
        ext[j, 0:HALO, :] = edge_ref[0, :, lanes].astype(F32)
        ext[j, HALO:, :] = x[:, lanes].astype(F32)
    wait_all(reads[1:3])
    for j in range(parts):
        lanes = slice(j * width, (j + 1) * width)
        own = grad[:, lanes] * got[j].astype(F32)
        query_grad[j] = own
        first[:, lanes] = own[0:HALO].astype(BF16)
        for i in range(reach):
            moved = ext[j, HALO - i : HALO - i + length, :]
            taps[j * reach + i : j * reach + i + 1, :] = jnp.sum(moved * own, 0, keepdims=True)
    for s in range(parts):
        rounded[s] = taps[...].astype(BF16)
    writes = [
        pltpu.make_async_copy(rounded, back_ref.at[:, pl.ds(begin, taps.shape[0]), :], sems.at[4]),
        pltpu.make_async_copy(query_grad, query_grad_ref, sems.at[5]),
        pltpu.make_async_copy(first, first_ref, sems.at[6]),
        pltpu.make_async_copy(product, product_ref, sems.at[7]),
    ]
    start_all(writes[0:3])
    reads[3].wait()
    for j in range(parts):
        lanes = slice(j * width, (j + 1) * width)
        product[:, lanes] = (query[:, lanes] * got[j].astype(F32)).astype(BF16)
    writes[3].start()
    wait_all(writes)


def product_call(convolved, query, grad, streams, edge, back, reach, begin):
    parts, length, width = convolved.shape
    channels = parts * width
    extra = back.shape[1] - begin
    hbm = pl.BlockSpec(memory_space=pltpu.HBM)
    return pl.pallas_call(
        partial(product_kernel, reach=reach, begin=begin),
        grid=(1,),
        in_specs=[pl.BlockSpec(memory_space=pl.ANY), hbm, hbm, hbm, whole((1, HALO, channels)), hbm],
        out_specs=[hbm] * 4,
        out_shape=[
            pltpu.HBM((length, channels), BF16),
            pltpu.HBM((parts, length, width), F32),
            pltpu.HBM((HALO, channels), BF16),
            pltpu.HBM(back.shape, BF16),
        ],
        scratch_shapes=[
            pltpu.VMEM((parts, length, width), BF16),
            pltpu.VMEM((length, channels), F32),
            pltpu.VMEM((length, channels), F32),
            pltpu.VMEM((length, channels), BF16),
            pltpu.VMEM((length, channels), BF16),
            pltpu.VMEM((parts, length, width), F32),
            pltpu.VMEM((HALO, channels), BF16),
            pltpu.VMEM((parts, length + HALO, width), F32),
            pltpu.VMEM((extra, width), F32),
            pltpu.VMEM((parts, extra, width), BF16),
            pltpu.SemaphoreType.DMA((8,)),
        ],
        input_output_aliases={5: 3},
        compiler_params=limit(16),
        name="product",
    )(convolved, in_hbm(query), in_hbm(grad), in_hbm(streams), edge, in_hbm(back))


def project_kernel(place_ref, product_ref, w_ref, *refs, flips):
    out_refs = refs[: len(flips)]
    buffer, sems = refs[len(flips) :]
    copies = weight_chunks(place_ref, w_ref, buffer, sems, flips, out_refs[0].shape[1])
    start_all(copies)
    deep = buffer.shape[1]
    per = len(copies) // len(flips)
    for slot, copy in enumerate(copies):
        copy.wait()
        part = lax.dot_general(
            product_ref[...], buffer[slot], (((1,), (1,)), ((), ())), preferred_element_type=F32
        )
        lanes = slice(slot % per * deep, (slot % per + 1) * deep)
        out = out_refs[slot // per]
        out[:, lanes] = part.astype(out.dtype)


def project(product, weight, place, flips, features, dtypes):
    length = product.shape[0]
    vmem = pl.BlockSpec(memory_space=pltpu.VMEM)
    return pl.pallas_call(
        partial(project_kernel, flips=flips),
        in_specs=[pl.BlockSpec(memory_space=pltpu.SMEM), vmem, pl.BlockSpec(memory_space=pltpu.HBM)],
        out_specs=[vmem] * len(flips),
        out_shape=[jax.ShapeDtypeStruct((length, features), dtype) for dtype in dtypes],
        scratch_shapes=chunk_scratch(weight, features, len(flips)),
        compiler_params=limit(16),
        name="project",
    )(place, product, weight)


def local_kernel(x_ref, edge_ref, taps_ref, out_ref, ext):
    _, parts, length, width = out_ref.shape
    for j in range(2):
        for p in range(parts):
            lanes = slice(p * width, (p + 1) * width)
            ext[p, 0:HALO, :] = edge_ref[j + 1, :, lanes].astype(F32)
            ext[p, HALO:, :] = x_ref[j + 1, :, lanes].astype(F32)
            total = taps_ref[j + 1, 0:1, lanes] * ext[p, HALO : HALO + length, :]
            for i in range(1, taps_ref.shape[1]):
                total = total + taps_ref[j + 1, i : i + 1, lanes] * ext[p, HALO - i : HALO - i + length, :]
            out_ref[j, p] = total


def finish_kernel(
    got_ref, query_grad_ref, next_ref, taps_ref, local_ref,
    input_grad_ref, filter_ref, medium_ref, short_ref,
    got, local, ext, input_grad, filtering, medium, sums, sems, *, own_rows, scale,
):
    parts, _, width = got.shape
    length = filtering.shape[0]
    reach = taps_ref.shape[1]
    medium_reach = medium.shape[0]
    reads = [
        pltpu.make_async_copy(query_grad_ref, ext.at[0, :, pl.ds(0, length), :], sems.at[0]),
        pltpu.make_async_copy(got_ref, got, sems.at[1]),
        pltpu.make_async_copy(local_ref, local, sems.at[2]),
    ]
    start_all(reads)

    def convolve(k):
        for j in range(parts):
            lanes = slice(j * width, (j + 1) * width)
            total = taps_ref[k, 0:1, lanes] * ext[k, j, 0:length, :]
            for i in range(1, reach):
                total = total + taps_ref[k, i : i + 1, lanes] * ext[k, j, i : i + length, :]
            input_grad[k, :, lanes] = total.astype(BF16)

    writes = [
        pltpu.make_async_copy(input_grad.at[k], input_grad_ref.at[k], sems.at[3 + k]) for k in range(3)
    ]
    more = [
        pltpu.make_async_copy(filtering, filter_ref, sems.at[6]),
        pltpu.make_async_copy(medium, medium_ref, sems.at[7]),
    ]
    for j in range(parts):
        ext[0, j, length:, :] = next_ref[:, j * width : (j + 1) * width].astype(F32)
    reads[0].wait()
    convolve(0)
    writes[0].start()
    reads[1].wait()
    after = length + 2 * HALO
    first = after + length
    taps = first + own_rows
    total = got[0, taps:, :].astype(F32)
    for j in range(1, parts):
        total = total + got[j, taps:, :].astype(F32)
    sums[...] = total
    for j in range(parts):
        lanes = slice(j * width, (j + 1) * width)
        filtering[:, lanes] = got[j, after:first, :].astype(F32)
        small = got[j, first:taps, :].astype(F32)
        medium[:, lanes] = small[0:medium_reach, :]
        second = medium_reach + reach
        short_ref[0, :, lanes] = sums[j * reach : (j + 1) * reach, :] * scale
        short_ref[1, :, lanes] = small[medium_reach:second, :]
        short_ref[2, :, lanes] = small[second : second + reach, :]
    start_all(more)
    reads[2].wait()
    for k in range(1, 3):
        for j in range(parts):
            ext[k, j, 0:length, :] = got[j, 0:length, :].astype(F32) * local[2 - k, j]
            begin = length + (k - 1) * HALO
            ext[k, j, length:, :] = got[j, begin : begin + HALO, :].astype(F32)
        convolve(k)
        writes[k].start()
    wait_all(writes + more)


def finish_call(returned, query_grad, next_grad, taps, features, medium_reach, own_rows, scale):
    parts, _, width = returned.shape
    groups, reach, channels = taps.shape
    length = query_grad.shape[1]
    hbm = pl.BlockSpec(memory_space=pltpu.HBM)
    return pl.pallas_call(
        partial(finish_kernel, own_rows=own_rows, scale=scale),
        grid=(1,),
        in_specs=[pl.BlockSpec(memory_space=pl.ANY), hbm, whole((HALO, channels)), whole(taps.shape), hbm],
        out_specs=[hbm, hbm, hbm, whole((groups, reach, channels))],
        out_shape=[
            pltpu.HBM((groups, length, channels), BF16),
            pltpu.HBM((length, channels), F32),
            pltpu.HBM((medium_reach, channels), F32),
            jax.ShapeDtypeStruct((groups, reach, channels), F32),
        ],
        scratch_shapes=[
            pltpu.VMEM(returned.shape, BF16),
            pltpu.VMEM((2, parts, length, width), F32),
            pltpu.VMEM((groups, parts, length + HALO, width), F32),
            pltpu.VMEM((groups, length, channels), BF16),
            pltpu.VMEM((length, channels), F32),
            pltpu.VMEM((medium_reach, channels), F32),
            pltpu.VMEM((-(-parts * reach // 8) * 8, width), F32),
            pltpu.SemaphoreType.DMA((8,)),
        ],
        compiler_params=limit(24),
        name="finish",
    )(returned, in_hbm(query_grad), next_grad, taps, in_hbm(features))


def reshard(value):
    return lax.all_to_all(value, "seq", split_axis=0, concat_axis=0, tiled=True)


def local(inputs, short_taps, medium_taps, long_filter, out_weight, out_cotangent):
    length, _, channels = inputs.shape
    reach = short_taps.shape[0]
    medium_reach = medium_taps.shape[0]
    parts = lax.axis_size("seq")
    position = lax.axis_index("seq")
    place = lax.axis_index("tensor").astype(jnp.int32)[None]
    features = out_cotangent.shape[1]
    width = channels // parts
    tokens = length * parts
    scale = 1.0 / math.sqrt(tokens)
    freqs, block = spectral_sizes(tokens, medium_reach)
    vmem = pl.BlockSpec(memory_space=pltpu.VMEM)

    weight = pltpu.with_memory_space_constraint(out_weight, pltpu.HBM)
    streams = inputs.transpose(1, 0, 2)
    taps = short_taps.transpose(1, 0, 2)
    hbm = pl.BlockSpec(memory_space=pltpu.HBM)
    packed = pl.pallas_call(
        pack_kernel,
        in_specs=[hbm, hbm],
        out_specs=hbm,
        out_shape=pltpu.HBM((parts, 3 * length, width), BF16),
        scratch_shapes=[
            pltpu.VMEM((2, length, channels), BF16),
            pltpu.VMEM((length, channels), F32),
            pltpu.VMEM((parts, 3 * length, width), BF16),
            pltpu.SemaphoreType.DMA((2 + parts,)),
        ],
        compiler_params=limit(8),
        name="pack",
    )(
        pltpu.with_memory_space_constraint(streams, pltpu.HBM),
        pltpu.with_memory_space_constraint(long_filter, pltpu.HBM),
    )
    got = reshard(packed)
    edge = shift(streams[:, length - HALO :], "seq", 1)
    cot_x = exchange(out_cotangent, "tensor", 2)
    cot_core = exchange(out_cotangent, "tensor", 1)

    tables = dft_tables(freqs)
    own_taps = lax.dynamic_slice_in_dim(taps, position * width, width, 2)
    own_medium = lax.dynamic_slice_in_dim(medium_taps, position * width, width, 1)

    acc = product_grad_first((out_cotangent, cot_core), weight, place, (0, 1))
    cot_far = exchange(cot_x, "tensor", 1)
    product_grad, query, sent = product_grad_last((cot_x, cot_far), weight, place, (2, 3), acc, streams, taps, parts)
    query, sent = with_edge(streams, edge, taps, product_grad, query, sent)
    grads = reshard(sent)

    convolved, kept, spectra = forward_call(got, own_taps, own_medium, tables, freqs, block)
    convolved = reshard(convolved)

    rows = 2 * length + 2 * HALO
    small = -(-(medium_reach + 2 * reach) // 8) * 8
    extra = -(-parts * reach // 8) * 8
    back = backward_call(
        got, grads, own_taps, own_medium, kept, spectra, tables, freqs, block, scale, medium_reach, rows, small, extra
    )
    product, query_grad, first_rows, back = product_call(
        convolved, query, product_grad, streams, edge, back, reach, rows + small
    )
    returned = reshard(back)

    (far,) = project(product, weight, place, (3,), features, (BF16,))
    far_core = exchange(far, "tensor", 1)
    (across,) = project(product, weight, place, (2,), features, (F32,))
    across_sum = exchange((across + far_core.astype(F32)).astype(BF16), "tensor", 2)
    near, own = project(product, weight, place, (1, 0), features, (BF16, F32))
    near_core = exchange(near, "tensor", 1)
    next_grad = shift(first_rows, "seq", -1)

    local_features = pl.pallas_call(
        local_kernel,
        in_specs=[vmem] * 3,
        out_specs=vmem,
        out_shape=pltpu.HBM((2, parts, length, width), F32),
        scratch_shapes=[pltpu.VMEM((parts, length + HALO, width), F32)],
        compiler_params=limit(8),
        name="local",
    )(in_hbm(streams), edge, taps)
    input_grad, filter_grad, medium_grad, short_grad = finish_call(
        returned, query_grad, next_grad, taps, local_features, medium_reach, small, scale
    )

    output = (own + near_core.astype(F32) + across_sum.astype(F32)).astype(BF16)
    return (
        output,
        input_grad.transpose(1, 0, 2),
        filter_grad,
        medium_grad,
        short_grad.transpose(1, 0, 2),
    )


def solution(mesh):
    return jax.shard_map(
        local,
        mesh=mesh,
        in_specs=(
            P("seq", None, "tensor"),
            P(None, None, "tensor"),
            P(None, "tensor"),
            P("seq", "tensor"),
            P(None, "tensor"),
            P("seq", "tensor"),
        ),
        out_specs=(
            P("seq", "tensor"),
            P("seq", None, "tensor"),
            P("seq", "tensor"),
            P(None, "tensor"),
            P(None, None, "tensor"),
        ),
        check_vma=False,
    )
```

```python
import math
from functools import partial

import jax
import jax.numpy as jnp
from jax import lax
from jax.experimental import pallas as pl
from jax.experimental.pallas import tpu as pltpu
from jax.sharding import PartitionSpec as P


F32 = jnp.float32
BF16 = jnp.bfloat16
HALO = 8
GROUP = 32
CHUNK = 512
TABLE_LIMIT = 1 << 22


def dot(a, b):
    return lax.dot_general(a, b, (((1,), (0,)), ((), ())), preferred_element_type=F32)


def exchange(value, axis, flip):
    count = lax.axis_size(axis)
    return lax.ppermute(value, axis, [(source, source ^ flip) for source in range(count)])


def shift(value, axis, steps):
    count = lax.axis_size(axis)
    pairs = [(s, s + steps) for s in range(count) if 0 <= s + steps < count]
    return lax.ppermute(value, axis, pairs)


def whole(shape):
    return pl.BlockSpec(shape, lambda *_: (0,) * len(shape))


def spectral_sizes(tokens, medium_reach):
    need = tokens + -(-(medium_reach - 2) // 2)
    freqs = -(-need // 384) * 384
    return freqs, 384


def dft_tables(freqs):
    period = 8 * freqs
    unit = 2.0 * math.pi / period
    odd = 2 * jnp.arange(freqs, dtype=jnp.int32) + 1
    start = 2 * GROUP * jnp.arange(freqs // GROUP, dtype=jnp.int32)
    inner = 2 * jnp.arange(GROUP, dtype=jnp.int32) + 1
    first = (start[:, None] * odd[None, :] % period).astype(F32) * unit
    second = (inner[:, None] * odd[None, :] % period).astype(F32) * unit
    fc, fs = jnp.cos(first)[:, None], jnp.sin(first)[:, None]
    sc, ss = jnp.cos(second)[None], jnp.sin(second)[None]
    cosine = (fc * sc - fs * ss).astype(BF16).reshape(freqs, freqs)
    sine = (fs * sc + fc * ss).astype(BF16).reshape(freqs, freqs)
    return cosine, sine


def in_hbm(value):
    return pltpu.with_memory_space_constraint(value, pltpu.HBM)


def limit(mebibytes):
    return pltpu.CompilerParams(vmem_limit_bytes=mebibytes << 20)


def pack_kernel(x_ref, filter_ref, out_ref, streams, taps, rounded, sems):
    parts, rows, width = out_ref.shape
    length = rows // 3
    read_filter = pltpu.make_async_copy(filter_ref, taps, sems.at[0])
    read_streams = pltpu.make_async_copy(x_ref.at[pl.ds(1, 2)], streams, sems.at[1])
    read_filter.start()
    read_streams.start()
    read_filter.wait()
    for j in range(parts):
        rounded[j, 2 * length :, :] = taps[:, j * width : (j + 1) * width].astype(BF16)
    read_streams.wait()
    writes = []
    for j in range(parts):
        lanes = slice(j * width, (j + 1) * width)
        rounded[j, 0:length, :] = streams[0, :, lanes]
        rounded[j, length : 2 * length, :] = streams[1, :, lanes]
        writes.append(pltpu.make_async_copy(rounded.at[j], out_ref.at[j], sems.at[2 + j]))
        writes[j].start()
    for write in writes:
        write.wait()


def weight_chunks(place_ref, weight_ref, buffer, sems, flips, features):
    deep = buffer.shape[1]
    per = features // deep
    copies = []
    for i, flip in enumerate(flips):
        for k in range(per):
            start = jnp.bitwise_xor(place_ref[0], flip) * features + k * deep
            slot = i * per + k
            copies.append(
                pltpu.make_async_copy(
                    weight_ref.at[pl.ds(pl.multiple_of(start, deep), deep), :], buffer.at[slot], sems.at[slot]
                )
            )
    return copies


def chunk_scratch(weight, features, shards):
    deep = math.gcd(features, CHUNK)
    count = shards * (features // deep)
    return [pltpu.VMEM((count, deep, weight.shape[1]), weight.dtype), pltpu.SemaphoreType.DMA((count,))]


def summed(x_refs, copies, buffer, total):
    deep = buffer.shape[1]
    per = len(copies) // len(x_refs)
    for slot, copy in enumerate(copies):
        copy.wait()
        lanes = slice(slot % per * deep, (slot % per + 1) * deep)
        part = dot(x_refs[slot // per][:, lanes], buffer[slot])
        total = part if total is None else total + part
    return total


def product_grad_kernel(place_ref, w_ref, *refs, flips, last):
    x_refs = refs[: len(flips)]
    copies_in = []
    if last:
        acc_ref, x_ref, taps_ref, out_ref, query_ref, sent_ref, buffer, sems, ext, held, in_sems = refs[len(flips) :]
    else:
        out_ref, buffer, sems, held, in_sems = refs[len(flips) :]
    for i, ref in enumerate(x_refs):
        copies_in.append(pltpu.make_async_copy(ref, held.at[i], in_sems.at[i]))
        copies_in[i].start()
    copies = weight_chunks(place_ref, w_ref, buffer, sems, flips, held.shape[2])
    for copy in copies:
        copy.start()
    if last:
        length = x_ref.shape[1]
        parts, _, width = ext.shape
        for j in range(parts):
            lanes = slice(j * width, (j + 1) * width)
            ext[j, 0:HALO, :] = jnp.zeros((HALO, width), F32)
            ext[j, HALO:, :] = x_ref[0, :, lanes].astype(F32)
            query = taps_ref[0, 0:1, lanes] * ext[j, HALO : HALO + length, :]
            for i in range(1, taps_ref.shape[1]):
                query = query + taps_ref[0, i : i + 1, lanes] * ext[j, HALO - i : HALO - i + length, :]
            query_ref[:, lanes] = query
    for copy in copies_in:
        copy.wait()
    total = summed([held.at[i] for i in range(len(flips))], copies, buffer, acc_ref[...] if last else None)
    out_ref[...] = total
    if last:
        parts, _, width = sent_ref.shape
        for j in range(parts):
            lanes = slice(j * width, (j + 1) * width)
            sent_ref[j] = (total[:, lanes] * query_ref[:, lanes]).astype(BF16)


def grad_scratch(shards, weight, length, features):
    return chunk_scratch(weight, features, shards), [
        pltpu.VMEM((shards, length, features), BF16),
        pltpu.SemaphoreType.DMA((shards,)),
    ]


def product_grad_first(shards, weight, place, flips):
    length, features = shards[0].shape
    channels = weight.shape[1]
    hbm = pl.BlockSpec(memory_space=pltpu.HBM)
    chunks, inputs = grad_scratch(len(flips), weight, length, features)
    return pl.pallas_call(
        partial(product_grad_kernel, flips=flips, last=False),
        in_specs=[pl.BlockSpec(memory_space=pltpu.SMEM), hbm] + [pl.BlockSpec(memory_space=pl.ANY)] * len(shards),
        out_specs=pl.BlockSpec(memory_space=pltpu.VMEM),
        out_shape=jax.ShapeDtypeStruct((length, channels), F32),
        scratch_shapes=chunks + inputs,
        compiler_params=limit(16),
        name="grad_first",
    )(place, weight, in_hbm(shards[0]), *shards[1:])


def product_grad_last(shards, weight, place, flips, acc, streams, taps, parts):
    length, features = shards[0].shape
    channels = weight.shape[1]
    hbm = pl.BlockSpec(memory_space=pltpu.HBM)
    vmem = pl.BlockSpec(memory_space=pltpu.VMEM)
    full = whole((length, channels))
    chunks, inputs = grad_scratch(len(flips), weight, length, features)
    return pl.pallas_call(
        partial(product_grad_kernel, flips=flips, last=True),
        grid=(1,),
        in_specs=[pl.BlockSpec(memory_space=pltpu.SMEM)]
        + [hbm]
        + [pl.BlockSpec(memory_space=pl.ANY)] * len(shards)
        + [full, whole((1, length, channels)), whole(taps.shape)],
        out_specs=[full, full, whole((parts, length, channels // parts))],
        out_shape=[
            pltpu.HBM((length, channels), F32),
            pltpu.HBM((length, channels), F32),
            pltpu.HBM((parts, length, channels // parts), BF16),
        ],
        scratch_shapes=chunks + [pltpu.VMEM((parts, length + HALO, channels // parts), F32)] + inputs,
        compiler_params=limit(24),
        name="grad_last",
    )(place, weight, *shards, acc, streams, taps)


def edge_kernel(x_ref, edge_ref, taps_ref, grad_ref, _, __, query_ref, sent_ref, ext, query, sent, sems):
    parts, _, width = sent.shape
    ext[0:HALO, :] = edge_ref[0].astype(F32)
    ext[HALO:, :] = x_ref[0].astype(F32)[0:HALO]
    total = taps_ref[0, 0:1, :] * ext[HALO : 2 * HALO, :]
    for i in range(1, taps_ref.shape[1]):
        total = total + taps_ref[0, i : i + 1, :] * ext[HALO - i : 2 * HALO - i, :]
    query[...] = total
    for j in range(parts):
        lanes = slice(j * width, (j + 1) * width)
        sent[j] = (grad_ref[:, lanes] * total[:, lanes]).astype(BF16)
    copies = [
        pltpu.make_async_copy(query, query_ref.at[pl.ds(0, HALO), :], sems.at[0]),
        pltpu.make_async_copy(sent, sent_ref.at[:, pl.ds(0, HALO), :], sems.at[1]),
    ]
    for copy in copies:
        copy.start()
    for copy in copies:
        copy.wait()


def with_edge(streams, edge, taps, grad, query, sent):
    channels = streams.shape[2]
    parts, _, width = sent.shape
    hbm = pl.BlockSpec(memory_space=pltpu.HBM)
    return pl.pallas_call(
        edge_kernel,
        grid=(1,),
        in_specs=[
            whole((1, 2 * HALO, channels)),
            whole((1, HALO, channels)),
            whole(taps.shape),
            whole((HALO, channels)),
            hbm,
            hbm,
        ],
        out_specs=[hbm, hbm],
        out_shape=[pltpu.HBM(query.shape, F32), pltpu.HBM(sent.shape, BF16)],
        scratch_shapes=[
            pltpu.VMEM((2 * HALO, channels), F32),
            pltpu.VMEM((HALO, channels), F32),
            pltpu.VMEM((parts, HALO, width), BF16),
            pltpu.SemaphoreType.DMA((2,)),
        ],
        input_output_aliases={4: 0, 5: 1},
        compiler_params=limit(4),
        name="edge_rows",
    )(streams, edge, taps, in_hbm(grad), in_hbm(query), in_hbm(sent))


def filtered(taps_ref, stream, ext, begin, length):
    total = taps_ref[stream + 1, 0:1, :] * ext[stream, HALO + begin : HALO + begin + length, :]
    for i in range(1, taps_ref.shape[1]):
        first = HALO + begin - i
        total = total + taps_ref[stream + 1, i : i + 1, :] * ext[stream, first : first + length, :]
    return total


def extend(got_ref, ext):
    parts, _, width = got_ref.shape
    length = (ext.shape[1] - HALO) // parts
    ext[:, 0:HALO, :] = jnp.zeros((2, HALO, width), F32)
    for s in range(parts):
        here = slice(HALO + s * length, HALO + (s + 1) * length)
        ext[0, here, :] = got_ref[s, 0:length, :].astype(F32)
        ext[1, here, :] = got_ref[s, length : 2 * length, :].astype(F32)


def forward_begin(got_ref, taps_ref, medium_ref, kept, ext, signals, medium):
    parts, rows, width = got_ref.shape
    length = rows // 3
    extend(got_ref, ext)
    for s in range(parts):
        here = slice(s * length, (s + 1) * length)
        key = filtered(taps_ref, 0, ext, s * length, length)
        value = filtered(taps_ref, 1, ext, s * length, length)
        kept[0, here, :] = key
        kept[1, here, :] = value
        signals[here, 0:width] = (key * value).astype(BF16)
        signals[here, width : 2 * width] = got_ref[s, 2 * length : 3 * length, :]
    medium[...] = jnp.zeros_like(medium)
    medium[0 : medium_ref.shape[0], :] = medium_ref[...].astype(BF16)


def forward_spectra(cosine, sine, signals, medium):
    tokens, double = signals.shape
    width = double // 2
    kept = medium.shape[0]
    both_c = dot(cosine[:, 0:tokens], signals[...])
    both_s = dot(sine[:, 0:tokens], signals[...])
    mc = dot(cosine[:, 0:kept], medium[...])
    ms = dot(sine[:, 0:kept], medium[...])
    ac, hc, as_, hs = (both_c[:, :width], both_c[:, width:], both_s[:, :width], both_s[:, width:])
    xc = ac * mc - as_ * ms
    xs = ac * ms + as_ * mc
    saved = (ac, as_, hc, hs)
    return saved, (xc * hc - xs * hs).astype(BF16), (xc * hs + xs * hc).astype(BF16)


def forward_end(out_ref, acc, freqs):
    parts, length, _ = out_ref.shape
    for s in range(parts):
        first = s * length + 1
        out_ref[s] = (acc[first : first + length, :] * (1.0 / freqs)).astype(BF16)


def block_copies(tables, held, spectra, spectra_held, sems, blocks):
    size = held.shape[1] // blocks
    groups = []
    for b in range(blocks):
        here = pl.ds(b * size, size)
        group = [pltpu.make_async_copy(t.at[here, :], held.at[i, here, :], sems.at[i, b]) for i, t in enumerate(tables)]
        if spectra is not None:
            group.append(pltpu.make_async_copy(spectra.at[:, here, :], spectra_held.at[:, here, :], sems.at[2, b]))
        groups.append(group)
    return groups


def start_all(copies):
    for copy in copies:
        copy.start()


def wait_all(copies):
    for copy in copies:
        copy.wait()


def forward_kernel(got_ref, taps_ref, medium_ref, cos_ref, sin_ref, *refs, freqs, block, resident):
    if not resident:
        cos_across_ref, sin_across_ref, *refs = refs
    out_ref, kept_ref, spectra_ref, ext, signals, medium, acc, kept, kept_sem, *refs = refs
    rows = acc.shape[0]
    step = pl.program_id(0)
    keep = pltpu.make_async_copy(kept, kept_ref, kept_sem)

    if resident:
        held, yc_all, ys_all, spectra_held, sems, out_sems = refs
        blocks = freqs // block
        groups = block_copies((cos_ref, sin_ref), held, None, None, sems, blocks)
        for group in groups:
            start_all(group)
        forward_begin(got_ref, taps_ref, medium_ref, kept, ext, signals, medium)
        keep.start()
        writes = []
        for b, group in enumerate(groups):
            wait_all(group)
            here = slice(b * block, (b + 1) * block)
            saved, yc, ys = forward_spectra(held[0, here, :], held[1, here, :], signals, medium)
            for i, spectrum in enumerate(saved):
                spectra_held[i, here, :] = spectrum
            there = pl.ds(b * block, block)
            writes.append(
                pltpu.make_async_copy(spectra_held.at[:, there, :], spectra_ref.at[:, there, :], out_sems.at[b])
            )
            writes[b].start()
            yc_all[here, :] = yc
            ys_all[here, :] = ys
        acc[...] = dot(held[0, 0:rows, :], yc_all[...]) + dot(held[1, 0:rows, :], ys_all[...])
        forward_end(out_ref, acc, freqs)
        wait_all(writes)
        keep.wait()
        return

    @pl.when(step == 0)
    def _():
        forward_begin(got_ref, taps_ref, medium_ref, kept, ext, signals, medium)
        keep.start()
        keep.wait()
        acc[...] = jnp.zeros_like(acc)

    saved, yc, ys = forward_spectra(cos_ref[...], sin_ref[...], signals, medium)
    for i, spectrum in enumerate(saved):
        spectra_ref[i] = spectrum
    acc[...] += dot(cos_across_ref[0:rows, :], yc) + dot(sin_across_ref[0:rows, :], ys)

    @pl.when(step == pl.num_programs(0) - 1)
    def _():
        forward_end(out_ref, acc, freqs)


def backward_begin(grads, medium_ref, delayed, signal, medium):
    parts, length, _ = grads.shape
    medium[...] = jnp.zeros_like(medium)
    medium[0 : medium_ref.shape[0], :] = medium_ref[...].astype(BF16)
    delayed[...] = jnp.zeros_like(delayed)
    for s in range(parts):
        delayed[s * length + 1 : (s + 1) * length + 1, :] = grads[s].astype(F32)
    signal[...] = delayed[...].astype(BF16)


def backward_spectra(cosine, sine, signal, medium, spectra):
    gc = dot(cosine, signal[...])
    gs = dot(sine, signal[...])
    ac, as_, hc, hs = spectra
    kept = medium.shape[0]
    mc = dot(cosine[:, 0:kept], medium[...])
    ms = dot(sine[:, 0:kept], medium[...])
    uc = hc * gc + hs * gs
    us = hc * gs - hs * gc
    xc = ac * mc - as_ * ms
    xs = ac * ms + as_ * mc
    both_c = jnp.concatenate([xc * gc + xs * gs, mc * uc + ms * us], 1).astype(BF16)
    both_s = jnp.concatenate([xc * gs - xs * gc, mc * us - ms * uc], 1).astype(BF16)
    return both_c, both_s, (ac * uc + as_ * us).astype(BF16), (ac * us - as_ * uc).astype(BF16)


def backward_end(
    streams, taps_ref, kept, out_ref, packed, small_ref, ext, after, acc, tap_acc, sems, freqs, scale, medium_reach
):
    parts, rows, width = packed.shape
    length = (ext.shape[1] - HALO) // parts
    tokens = parts * length
    reach = taps_ref.shape[1]
    inverse = 1.0 / freqs
    first = length + 2 * HALO
    head = first + length
    after[:, tokens : tokens + HALO, :] = jnp.zeros((2, HALO, width), F32)
    for s in range(parts):
        here = slice(s * length, (s + 1) * length)
        packed[s, first:head, :] = (acc[here, 0:width] * (inverse * scale)).astype(BF16)
        gated = acc[here, width : 2 * width] * inverse
        packed[s, 0:length, :] = gated.astype(BF16)
        after[0, here, :] = gated * kept[1, here, :]
        after[1, here, :] = gated * kept[0, here, :]
    for s in range(parts):
        end = (s + 1) * length
        for j in range(2):
            begin = length + j * HALO
            packed[s, begin : begin + HALO, :] = after[j, end : end + HALO, :].astype(BF16)
    writes = [
        pltpu.make_async_copy(packed.at[:, pl.ds(0, head), :], out_ref.at[:, pl.ds(0, head), :], sems.at[0]),
        pltpu.make_async_copy(
            packed.at[:, pl.ds(head, rows - head), :], out_ref.at[:, pl.ds(head, rows - head), :], sems.at[1]
        ),
    ]
    writes[0].start()
    extend(streams, ext)
    small_ref[...] = jnp.zeros_like(small_ref)
    small_ref[0:medium_reach, :] = tap_acc[0:medium_reach, :] * (inverse * scale)
    for j in range(2):
        sums = [jnp.zeros((8, width), F32) for _ in range(reach)]
        for s in range(parts):
            begin = s * length
            own = after[j, begin : begin + length, :]
            for i in range(reach):
                moved = ext[j, HALO + begin - i : HALO + begin - i + length, :]
                sums[i] = sums[i] + jnp.sum((moved * own).reshape(length // 8, 8, width), 0)
        for i in range(reach):
            row = medium_reach + j * reach + i
            small_ref[row : row + 1, :] = jnp.sum(sums[i], 0, keepdims=True) * scale
    small = small_ref[...].astype(BF16)
    for s in range(parts):
        packed[s, head:, :] = small
    writes[1].start()
    wait_all(writes)


def backward_kernel(
    taps_ref, medium_ref, grads_ref, got_ref, kept_ref, spectra_ref, cos_ref, sin_ref, *refs,
    freqs, block, scale, medium_reach, resident,
):
    if not resident:
        cos_across_ref, sin_across_ref, *refs = refs
    out_ref, packed, small, delayed, signal, ext, after, acc, tap_acc, streams, kept, grads, medium, *refs = refs
    late_sems, write_sems, *refs = refs
    step = pl.program_id(0)
    size = signal.shape[0]
    rows, taps_kept = (acc.shape[0], tap_acc.shape[0])
    late = [
        pltpu.make_async_copy(kept_ref, kept, late_sems.at[0]),
        pltpu.make_async_copy(got_ref.at[:, pl.ds(0, streams.shape[1]), :], streams, late_sems.at[1]),
    ]
    early = pltpu.make_async_copy(grads_ref, grads, late_sems.at[2])

    def end():
        wait_all(late)
        backward_end(
            streams, taps_ref, kept, out_ref, packed, small, ext, after, acc, tap_acc, write_sems,
            freqs, scale, medium_reach,
        )

    if resident:
        held, both_c_all, both_s_all, taps_c_all, taps_s_all, spectra_held, sems = refs
        groups = block_copies((cos_ref, sin_ref), held, spectra_ref, spectra_held, sems, freqs // block)
        early.start()
        for group in groups:
            start_all(group)
        start_all(late)
        early.wait()
        backward_begin(grads, medium_ref, delayed, signal, medium)
        for b, group in enumerate(groups):
            wait_all(group)
            here = slice(b * block, (b + 1) * block)
            spectra = [spectra_held[i, here, :] for i in range(spectra_held.shape[0])]
            both_c_all[here, :], both_s_all[here, :], taps_c_all[here, :], taps_s_all[here, :] = backward_spectra(
                held[0, here, 0:size], held[1, here, 0:size], signal, medium, spectra
            )
        acc[...] = dot(held[0, 0:rows, :], both_c_all[...]) + dot(held[1, 0:rows, :], both_s_all[...])
        tap_acc[...] = dot(held[0, 0:taps_kept, :], taps_c_all[...]) + dot(held[1, 0:taps_kept, :], taps_s_all[...])
        end()
        return

    @pl.when(step == 0)
    def _():
        early.start()
        early.wait()
        backward_begin(grads, medium_ref, delayed, signal, medium)
        acc[...] = jnp.zeros_like(acc)
        tap_acc[...] = jnp.zeros_like(tap_acc)

    spectra = [spectra_ref[i] for i in range(spectra_ref.shape[0])]
    both_c, both_s, taps_c, taps_s = backward_spectra(cos_ref[:, 0:size], sin_ref[:, 0:size], signal, medium, spectra)
    acc[...] += dot(cos_across_ref[0:rows, :], both_c) + dot(sin_across_ref[0:rows, :], both_s)
    tap_acc[...] += dot(cos_across_ref[0:taps_kept, :], taps_c) + dot(sin_across_ref[0:taps_kept, :], taps_s)

    @pl.when(step == pl.num_programs(0) - 1)
    def _():
        start_all(late)
        end()


def spectral_plan(freqs, block, tables):
    if freqs * freqs <= TABLE_LIMIT:
        hbm = pl.BlockSpec(memory_space=pltpu.HBM)
        return True, 1, [hbm, hbm], [in_hbm(t) for t in tables]
    rows = pl.BlockSpec((block, freqs), lambda j: (j, 0))
    columns = pl.BlockSpec((freqs, block), lambda j: (0, j))
    return False, freqs // block, [rows, rows, columns, columns], [*tables, *tables]


def held_scratch(freqs, block, width, widths, kinds):
    blocks = freqs // block
    return (
        [pltpu.VMEM((2, freqs, freqs), BF16)]
        + [pltpu.VMEM((freqs, w), BF16) for w in widths]
        + [pltpu.VMEM((4, freqs, width), F32), pltpu.SemaphoreType.DMA((kinds, blocks))]
    )


def forward_call(got, taps, medium_taps, tables, freqs, block):
    parts, tall, width = got.shape
    length = tall // 3
    tokens = parts * length
    padded = -(-medium_taps.shape[0] // 128) * 128
    resident, steps, specs, operands = spectral_plan(freqs, block, tables)
    per = freqs // steps
    hbm = pl.BlockSpec(memory_space=pltpu.HBM)
    return pl.pallas_call(
        partial(forward_kernel, freqs=freqs, block=block, resident=resident),
        grid=(steps,),
        in_specs=[whole(got.shape), whole(taps.shape), whole(medium_taps.shape)] + specs,
        out_specs=[
            whole((parts, length, width)),
            hbm,
            hbm if resident else pl.BlockSpec((4, per, width), lambda j: (0, j, 0)),
        ],
        out_shape=[
            pltpu.HBM((parts, length, width), BF16),
            pltpu.HBM((2, tokens, width), F32),
            pltpu.HBM((4, freqs, width), F32),
        ],
        scratch_shapes=[
            pltpu.VMEM((2, tokens + HALO, width), F32),
            pltpu.VMEM((tokens, 2 * width), BF16),
            pltpu.VMEM((padded, width), BF16),
            pltpu.VMEM((tokens + HALO, width), F32),
            pltpu.VMEM((2, tokens, width), F32),
            pltpu.SemaphoreType.DMA,
        ]
        + (
            held_scratch(freqs, block, width, (width, width), 2) + [pltpu.SemaphoreType.DMA((freqs // block,))]
            if resident
            else []
        ),
        compiler_params=limit(32 if resident else 60),
        name="forward_spectral",
    )(in_hbm(got), taps, medium_taps, *operands)


def backward_call(got, grads, taps, medium_taps, kept, spectra, tables, freqs, block, scale, medium_reach, rows, small, extra):
    parts, tall, width = got.shape
    length = tall // 3
    tokens = parts * length
    padded = -(-medium_reach // 128) * 128
    late = -(-(tokens + 1) // 128) * 128
    resident, steps, specs, operands = spectral_plan(freqs, block, tables)
    per = freqs // steps
    hbm = pl.BlockSpec(memory_space=pltpu.HBM)
    return pl.pallas_call(
        partial(
            backward_kernel, freqs=freqs, block=block, scale=scale, medium_reach=medium_reach, resident=resident
        ),
        grid=(steps,),
        in_specs=[
            whole(taps.shape),
            whole(medium_taps.shape),
            pl.BlockSpec(memory_space=pl.ANY),
            hbm,
            hbm,
            hbm if resident else pl.BlockSpec((4, per, width), lambda j: (0, j, 0)),
        ]
        + specs,
        out_specs=hbm,
        out_shape=pltpu.HBM((parts, rows + small + extra, width), BF16),
        scratch_shapes=[
            pltpu.VMEM((parts, rows + small, width), BF16),
            pltpu.VMEM((small, width), F32),
            pltpu.VMEM((late, width), F32),
            pltpu.VMEM((late, width), BF16),
            pltpu.VMEM((2, tokens + HALO, width), F32),
            pltpu.VMEM((2, tokens + HALO, width), F32),
            pltpu.VMEM((tokens, 2 * width), F32),
            pltpu.VMEM((padded, width), F32),
            pltpu.VMEM((parts, 2 * length, width), BF16),
            pltpu.VMEM((2, tokens, width), F32),
            pltpu.VMEM((parts, length, width), BF16),
            pltpu.VMEM((padded, width), BF16),
            pltpu.SemaphoreType.DMA((3,)),
            pltpu.SemaphoreType.DMA((2,)),
        ]
        + (held_scratch(freqs, block, width, (2 * width, 2 * width, width, width), 3) if resident else []),
        compiler_params=limit(40 if resident else 60),
        name="backward_spectral",
    )(taps, medium_taps, grads, in_hbm(got), in_hbm(kept), in_hbm(spectra), *operands)


def product_kernel(
    got_ref, query_ref, grad_ref, x_ref, edge_ref, _, product_ref, query_grad_ref, first_ref, back_ref,
    got, query, grad, x, product, query_grad, first, ext, taps, rounded, sems, *, reach, begin,
):
    parts, length, width = got.shape
    reads = [
        pltpu.make_async_copy(source, held, sems.at[i])
        for i, (source, held) in enumerate(((x_ref.at[0], x), (got_ref, got), (grad_ref, grad), (query_ref, query)))
    ]
    start_all(reads)
    taps[...] = jnp.zeros_like(taps)
    reads[0].wait()
    for j in range(parts):
        lanes = slice(j * width, (j + 1) * width)
        ext[j, 0:HALO, :] = edge_ref[0, :, lanes].astype(F32)
        ext[j, HALO:, :] = x[:, lanes].astype(F32)
    wait_all(reads[1:3])
    for j in range(parts):
        lanes = slice(j * width, (j + 1) * width)
        own = grad[:, lanes] * got[j].astype(F32)
        query_grad[j] = own
        first[:, lanes] = own[0:HALO].astype(BF16)
        for i in range(reach):
            moved = ext[j, HALO - i : HALO - i + length, :]
            taps[j * reach + i : j * reach + i + 1, :] = jnp.sum(moved * own, 0, keepdims=True)
    for s in range(parts):
        rounded[s] = taps[...].astype(BF16)
    writes = [
        pltpu.make_async_copy(rounded, back_ref.at[:, pl.ds(begin, taps.shape[0]), :], sems.at[4]),
        pltpu.make_async_copy(query_grad, query_grad_ref, sems.at[5]),
        pltpu.make_async_copy(first, first_ref, sems.at[6]),
        pltpu.make_async_copy(product, product_ref, sems.at[7]),
    ]
    start_all(writes[0:3])
    reads[3].wait()
    for j in range(parts):
        lanes = slice(j * width, (j + 1) * width)
        product[:, lanes] = (query[:, lanes] * got[j].astype(F32)).astype(BF16)
    writes[3].start()
    wait_all(writes)


def product_call(convolved, query, grad, streams, edge, back, reach, begin):
    parts, length, width = convolved.shape
    channels = parts * width
    extra = back.shape[1] - begin
    hbm = pl.BlockSpec(memory_space=pltpu.HBM)
    return pl.pallas_call(
        partial(product_kernel, reach=reach, begin=begin),
        grid=(1,),
        in_specs=[pl.BlockSpec(memory_space=pl.ANY), hbm, hbm, hbm, whole((1, HALO, channels)), hbm],
        out_specs=[hbm] * 4,
        out_shape=[
            pltpu.HBM((length, channels), BF16),
            pltpu.HBM((parts, length, width), F32),
            pltpu.HBM((HALO, channels), BF16),
            pltpu.HBM(back.shape, BF16),
        ],
        scratch_shapes=[
            pltpu.VMEM((parts, length, width), BF16),
            pltpu.VMEM((length, channels), F32),
            pltpu.VMEM((length, channels), F32),
            pltpu.VMEM((length, channels), BF16),
            pltpu.VMEM((length, channels), BF16),
            pltpu.VMEM((parts, length, width), F32),
            pltpu.VMEM((HALO, channels), BF16),
            pltpu.VMEM((parts, length + HALO, width), F32),
            pltpu.VMEM((extra, width), F32),
            pltpu.VMEM((parts, extra, width), BF16),
            pltpu.SemaphoreType.DMA((8,)),
        ],
        input_output_aliases={5: 3},
        compiler_params=limit(16),
        name="product",
    )(convolved, in_hbm(query), in_hbm(grad), in_hbm(streams), edge, in_hbm(back))


def project_kernel(place_ref, product_ref, w_ref, *refs, flips):
    out_refs = refs[: len(flips)]
    buffer, sems = refs[len(flips) :]
    copies = weight_chunks(place_ref, w_ref, buffer, sems, flips, out_refs[0].shape[1])
    start_all(copies)
    deep = buffer.shape[1]
    per = len(copies) // len(flips)
    for slot, copy in enumerate(copies):
        copy.wait()
        part = lax.dot_general(
            product_ref[...], buffer[slot], (((1,), (1,)), ((), ())), preferred_element_type=F32
        )
        lanes = slice(slot % per * deep, (slot % per + 1) * deep)
        out = out_refs[slot // per]
        out[:, lanes] = part.astype(out.dtype)


def project(product, weight, place, flips, features, dtypes):
    length = product.shape[0]
    vmem = pl.BlockSpec(memory_space=pltpu.VMEM)
    return pl.pallas_call(
        partial(project_kernel, flips=flips),
        in_specs=[pl.BlockSpec(memory_space=pltpu.SMEM), vmem, pl.BlockSpec(memory_space=pltpu.HBM)],
        out_specs=[vmem] * len(flips),
        out_shape=[jax.ShapeDtypeStruct((length, features), dtype) for dtype in dtypes],
        scratch_shapes=chunk_scratch(weight, features, len(flips)),
        compiler_params=limit(16),
        name="project",
    )(place, product, weight)


def local_kernel(x_ref, edge_ref, taps_ref, out_ref, ext):
    _, parts, length, width = out_ref.shape
    for j in range(2):
        for p in range(parts):
            lanes = slice(p * width, (p + 1) * width)
            ext[p, 0:HALO, :] = edge_ref[j + 1, :, lanes].astype(F32)
            ext[p, HALO:, :] = x_ref[j + 1, :, lanes].astype(F32)
            total = taps_ref[j + 1, 0:1, lanes] * ext[p, HALO : HALO + length, :]
            for i in range(1, taps_ref.shape[1]):
                total = total + taps_ref[j + 1, i : i + 1, lanes] * ext[p, HALO - i : HALO - i + length, :]
            out_ref[j, p] = total


def finish_kernel(
    got_ref, query_grad_ref, next_ref, taps_ref, local_ref,
    input_grad_ref, filter_ref, medium_ref, short_ref,
    got, local, ext, input_grad, filtering, medium, short, sums, sems, *, own_rows, scale,
):
    parts, _, width = got.shape
    length = filtering.shape[0]
    reach = taps_ref.shape[1]
    medium_reach = medium.shape[0]
    reads = [
        pltpu.make_async_copy(query_grad_ref, ext.at[0, :, pl.ds(0, length), :], sems.at[0]),
        pltpu.make_async_copy(got_ref, got, sems.at[1]),
        pltpu.make_async_copy(local_ref, local, sems.at[2]),
    ]
    start_all(reads)

    def convolve(k):
        for j in range(parts):
            lanes = slice(j * width, (j + 1) * width)
            total = taps_ref[k, 0:1, lanes] * ext[k, j, 0:length, :]
            for i in range(1, reach):
                total = total + taps_ref[k, i : i + 1, lanes] * ext[k, j, i : i + length, :]
            input_grad[k, :, lanes] = total.astype(BF16)

    writes = [
        pltpu.make_async_copy(input_grad.at[k], input_grad_ref.at[k], sems.at[3 + k]) for k in range(3)
    ]
    more = [
        pltpu.make_async_copy(filtering, filter_ref, sems.at[6]),
        pltpu.make_async_copy(medium, medium_ref, sems.at[7]),
        pltpu.make_async_copy(short, short_ref, sems.at[8]),
    ]
    for j in range(parts):
        ext[0, j, length:, :] = next_ref[:, j * width : (j + 1) * width].astype(F32)
    reads[0].wait()
    convolve(0)
    writes[0].start()
    reads[1].wait()
    after = length + 2 * HALO
    first = after + length
    taps = first + own_rows
    total = got[0, taps:, :].astype(F32)
    for j in range(1, parts):
        total = total + got[j, taps:, :].astype(F32)
    sums[...] = total
    for j in range(parts):
        lanes = slice(j * width, (j + 1) * width)
        filtering[:, lanes] = got[j, after:first, :].astype(F32)
        small = got[j, first:taps, :].astype(F32)
        medium[:, lanes] = small[0:medium_reach, :]
        second = medium_reach + reach
        short[0, :, lanes] = sums[j * reach : (j + 1) * reach, :] * scale
        short[1, :, lanes] = small[medium_reach:second, :]
        short[2, :, lanes] = small[second : second + reach, :]
    start_all(more)
    reads[2].wait()
    for k in range(1, 3):
        for j in range(parts):
            ext[k, j, 0:length, :] = got[j, 0:length, :].astype(F32) * local[2 - k, j]
            begin = length + (k - 1) * HALO
            ext[k, j, length:, :] = got[j, begin : begin + HALO, :].astype(F32)
        convolve(k)
        writes[k].start()
    wait_all(writes + more)


def finish_call(returned, query_grad, next_grad, taps, features, medium_reach, own_rows, scale):
    parts, _, width = returned.shape
    groups, reach, channels = taps.shape
    length = query_grad.shape[1]
    hbm = pl.BlockSpec(memory_space=pltpu.HBM)
    return pl.pallas_call(
        partial(finish_kernel, own_rows=own_rows, scale=scale),
        grid=(1,),
        in_specs=[pl.BlockSpec(memory_space=pl.ANY), hbm, whole((HALO, channels)), whole(taps.shape), hbm],
        out_specs=[hbm] * 4,
        out_shape=[
            pltpu.HBM((groups, length, channels), BF16),
            pltpu.HBM((length, channels), F32),
            pltpu.HBM((medium_reach, channels), F32),
            pltpu.HBM((groups, reach, channels), F32),
        ],
        scratch_shapes=[
            pltpu.VMEM(returned.shape, BF16),
            pltpu.VMEM((2, parts, length, width), F32),
            pltpu.VMEM((groups, parts, length + HALO, width), F32),
            pltpu.VMEM((groups, length, channels), BF16),
            pltpu.VMEM((length, channels), F32),
            pltpu.VMEM((medium_reach, channels), F32),
            pltpu.VMEM((groups, reach, channels), F32),
            pltpu.VMEM((-(-parts * reach // 8) * 8, width), F32),
            pltpu.SemaphoreType.DMA((9,)),
        ],
        compiler_params=limit(24),
        name="finish",
    )(returned, in_hbm(query_grad), next_grad, taps, in_hbm(features))


def reshard(value):
    return lax.all_to_all(value, "seq", split_axis=0, concat_axis=0, tiled=True)


def local(inputs, short_taps, medium_taps, long_filter, out_weight, out_cotangent):
    length, _, channels = inputs.shape
    reach = short_taps.shape[0]
    medium_reach = medium_taps.shape[0]
    parts = lax.axis_size("seq")
    position = lax.axis_index("seq")
    place = lax.axis_index("tensor").astype(jnp.int32)[None]
    features = out_cotangent.shape[1]
    width = channels // parts
    tokens = length * parts
    scale = 1.0 / math.sqrt(tokens)
    freqs, block = spectral_sizes(tokens, medium_reach)
    vmem = pl.BlockSpec(memory_space=pltpu.VMEM)

    weight = pltpu.with_memory_space_constraint(out_weight, pltpu.HBM)
    streams = inputs.transpose(1, 0, 2)
    taps = short_taps.transpose(1, 0, 2)
    hbm = pl.BlockSpec(memory_space=pltpu.HBM)
    packed = pl.pallas_call(
        pack_kernel,
        in_specs=[hbm, hbm],
        out_specs=hbm,
        out_shape=pltpu.HBM((parts, 3 * length, width), BF16),
        scratch_shapes=[
            pltpu.VMEM((2, length, channels), BF16),
            pltpu.VMEM((length, channels), F32),
            pltpu.VMEM((parts, 3 * length, width), BF16),
            pltpu.SemaphoreType.DMA((2 + parts,)),
        ],
        compiler_params=limit(8),
        name="pack",
    )(
        pltpu.with_memory_space_constraint(streams, pltpu.HBM),
        pltpu.with_memory_space_constraint(long_filter, pltpu.HBM),
    )
    got = reshard(packed)
    edge = shift(streams[:, length - HALO :], "seq", 1)
    cot_x = exchange(out_cotangent, "tensor", 2)
    cot_core = exchange(out_cotangent, "tensor", 1)

    tables = dft_tables(freqs)
    own_taps = lax.dynamic_slice_in_dim(taps, position * width, width, 2)
    own_medium = lax.dynamic_slice_in_dim(medium_taps, position * width, width, 1)

    acc = product_grad_first((out_cotangent, cot_core), weight, place, (0, 1))
    cot_far = exchange(cot_x, "tensor", 1)
    product_grad, query, sent = product_grad_last((cot_x, cot_far), weight, place, (2, 3), acc, streams, taps, parts)
    query, sent = with_edge(streams, edge, taps, product_grad, query, sent)
    grads = reshard(sent)

    convolved, kept, spectra = forward_call(got, own_taps, own_medium, tables, freqs, block)
    convolved = reshard(convolved)

    rows = 2 * length + 2 * HALO
    small = -(-(medium_reach + 2 * reach) // 8) * 8
    extra = -(-parts * reach // 8) * 8
    back = backward_call(
        got, grads, own_taps, own_medium, kept, spectra, tables, freqs, block, scale, medium_reach, rows, small, extra
    )
    product, query_grad, first_rows, back = product_call(
        convolved, query, product_grad, streams, edge, back, reach, rows + small
    )
    returned = reshard(back)

    (far,) = project(product, weight, place, (3,), features, (BF16,))
    far_core = exchange(far, "tensor", 1)
    (across,) = project(product, weight, place, (2,), features, (F32,))
    across_sum = exchange((across + far_core.astype(F32)).astype(BF16), "tensor", 2)
    near, own = project(product, weight, place, (1, 0), features, (BF16, F32))
    near_core = exchange(near, "tensor", 1)
    next_grad = shift(first_rows, "seq", -1)

    local_features = pl.pallas_call(
        local_kernel,
        in_specs=[vmem] * 3,
        out_specs=vmem,
        out_shape=pltpu.HBM((2, parts, length, width), F32),
        scratch_shapes=[pltpu.VMEM((parts, length + HALO, width), F32)],
        compiler_params=limit(8),
        name="local",
    )(in_hbm(streams), edge, taps)
    input_grad, filter_grad, medium_grad, short_grad = finish_call(
        returned, query_grad, next_grad, taps, local_features, medium_reach, small, scale
    )

    output = (own + near_core.astype(F32) + across_sum.astype(F32)).astype(BF16)
    return (
        output,
        input_grad.transpose(1, 0, 2),
        filter_grad,
        medium_grad,
        short_grad.transpose(1, 0, 2),
    )


def solution(mesh):
    return jax.shard_map(
        local,
        mesh=mesh,
        in_specs=(
            P("seq", None, "tensor"),
            P(None, None, "tensor"),
            P(None, "tensor"),
            P("seq", "tensor"),
            P(None, "tensor"),
            P("seq", "tensor"),
        ),
        out_specs=(
            P("seq", "tensor"),
            P("seq", None, "tensor"),
            P("seq", "tensor"),
            P(None, "tensor"),
            P(None, None, "tensor"),
        ),
        check_vma=False,
    )
```

```python
import math
from functools import partial

import jax
import jax.numpy as jnp
from jax import lax
from jax.experimental import pallas as pl
from jax.experimental.pallas import tpu as pltpu
from jax.sharding import PartitionSpec as P


F32 = jnp.float32
BF16 = jnp.bfloat16
HALO = 8
GROUP = 32
CHUNK = 512
TABLE_LIMIT = 1 << 22


def dot(a, b):
    return lax.dot_general(a, b, (((1,), (0,)), ((), ())), preferred_element_type=F32)


def exchange(value, axis, flip):
    count = lax.axis_size(axis)
    return lax.ppermute(value, axis, [(source, source ^ flip) for source in range(count)])


def shift(value, axis, steps):
    count = lax.axis_size(axis)
    pairs = [(s, s + steps) for s in range(count) if 0 <= s + steps < count]
    return lax.ppermute(value, axis, pairs)


def whole(shape):
    return pl.BlockSpec(shape, lambda *_: (0,) * len(shape))


def spectral_sizes(tokens, medium_reach):
    need = tokens + -(-(medium_reach - 2) // 2)
    freqs = -(-need // 384) * 384
    return freqs, 384


def dft_tables(freqs):
    period = 8 * freqs
    unit = 2.0 * math.pi / period
    odd = 2 * jnp.arange(freqs, dtype=jnp.int32) + 1
    start = 2 * GROUP * jnp.arange(freqs // GROUP, dtype=jnp.int32)
    inner = 2 * jnp.arange(GROUP, dtype=jnp.int32) + 1
    first = (start[:, None] * odd[None, :] % period).astype(F32) * unit
    second = (inner[:, None] * odd[None, :] % period).astype(F32) * unit
    fc, fs = jnp.cos(first)[:, None], jnp.sin(first)[:, None]
    sc, ss = jnp.cos(second)[None], jnp.sin(second)[None]
    cosine = (fc * sc - fs * ss).astype(BF16).reshape(freqs, freqs)
    sine = (fs * sc + fc * ss).astype(BF16).reshape(freqs, freqs)
    return cosine, sine


def in_hbm(value):
    return pltpu.with_memory_space_constraint(value, pltpu.HBM)


def limit(mebibytes):
    return pltpu.CompilerParams(vmem_limit_bytes=mebibytes << 20)


def pack_kernel(x_ref, filter_ref, out_ref, edge_ref, streams, taps, rounded, edge, sems, edge_sems):
    parts, rows, width = out_ref.shape
    length = rows // 3
    read_edge = pltpu.make_async_copy(x_ref.at[:, pl.ds(length - HALO, HALO), :], edge, edge_sems.at[0])
    write_edge = pltpu.make_async_copy(edge, edge_ref, edge_sems.at[1])
    read_edge.start()
    read_filter = pltpu.make_async_copy(filter_ref, taps, sems.at[0])
    read_streams = pltpu.make_async_copy(x_ref.at[pl.ds(1, 2)], streams, sems.at[1])
    read_filter.start()
    read_streams.start()
    read_filter.wait()
    for j in range(parts):
        rounded[j, 2 * length :, :] = taps[:, j * width : (j + 1) * width].astype(BF16)
    read_edge.wait()
    write_edge.start()
    read_streams.wait()
    writes = []
    for j in range(parts):
        lanes = slice(j * width, (j + 1) * width)
        rounded[j, 0:length, :] = streams[0, :, lanes]
        rounded[j, length : 2 * length, :] = streams[1, :, lanes]
        writes.append(pltpu.make_async_copy(rounded.at[j], out_ref.at[j], sems.at[2 + j]))
        writes[j].start()
    for write in writes:
        write.wait()
    write_edge.wait()


def weight_chunks(place_ref, weight_ref, buffer, sems, flips, features):
    deep = buffer.shape[1]
    per = features // deep
    copies = []
    for i, flip in enumerate(flips):
        for k in range(per):
            start = jnp.bitwise_xor(place_ref[0], flip) * features + k * deep
            slot = i * per + k
            copies.append(
                pltpu.make_async_copy(
                    weight_ref.at[pl.ds(pl.multiple_of(start, deep), deep), :], buffer.at[slot], sems.at[slot]
                )
            )
    return copies


def chunk_scratch(weight, features, shards):
    deep = math.gcd(features, CHUNK)
    count = shards * (features // deep)
    return [pltpu.VMEM((count, deep, weight.shape[1]), weight.dtype), pltpu.SemaphoreType.DMA((count,))]


def summed(x_refs, copies, buffer, total):
    deep = buffer.shape[1]
    per = len(copies) // len(x_refs)
    for slot, copy in enumerate(copies):
        copy.wait()
        lanes = slice(slot % per * deep, (slot % per + 1) * deep)
        part = dot(x_refs[slot // per][:, lanes], buffer[slot])
        total = part if total is None else total + part
    return total


def product_grad_kernel(place_ref, w_ref, *refs, flips, last):
    x_refs = refs[: len(flips)]
    copies_in = []
    if last:
        acc_ref, x_ref, taps_ref, out_ref, query_ref, sent_ref, buffer, sems, ext, held, in_sems = refs[len(flips) :]
    else:
        out_ref, buffer, sems, held, in_sems = refs[len(flips) :]
    for i, ref in enumerate(x_refs):
        copies_in.append(pltpu.make_async_copy(ref, held.at[i], in_sems.at[i]))
        copies_in[i].start()
    copies = weight_chunks(place_ref, w_ref, buffer, sems, flips, held.shape[2])
    for copy in copies:
        copy.start()
    if last:
        length = x_ref.shape[1]
        parts, _, width = ext.shape
        for j in range(parts):
            lanes = slice(j * width, (j + 1) * width)
            ext[j, 0:HALO, :] = jnp.zeros((HALO, width), F32)
            ext[j, HALO:, :] = x_ref[0, :, lanes].astype(F32)
            query = taps_ref[0, 0:1, lanes] * ext[j, HALO : HALO + length, :]
            for i in range(1, taps_ref.shape[1]):
                query = query + taps_ref[0, i : i + 1, lanes] * ext[j, HALO - i : HALO - i + length, :]
            query_ref[:, lanes] = query
    for copy in copies_in:
        copy.wait()
    total = summed([held.at[i] for i in range(len(flips))], copies, buffer, acc_ref[...] if last else None)
    out_ref[...] = total
    if last:
        parts, _, width = sent_ref.shape
        for j in range(parts):
            lanes = slice(j * width, (j + 1) * width)
            sent_ref[j] = (total[:, lanes] * query_ref[:, lanes]).astype(BF16)


def grad_scratch(shards, weight, length, features):
    return chunk_scratch(weight, features, shards), [
        pltpu.VMEM((shards, length, features), BF16),
        pltpu.SemaphoreType.DMA((shards,)),
    ]


def product_grad_first(shards, weight, place, flips):
    length, features = shards[0].shape
    channels = weight.shape[1]
    hbm = pl.BlockSpec(memory_space=pltpu.HBM)
    chunks, inputs = grad_scratch(len(flips), weight, length, features)
    return pl.pallas_call(
        partial(product_grad_kernel, flips=flips, last=False),
        in_specs=[pl.BlockSpec(memory_space=pltpu.SMEM), hbm] + [pl.BlockSpec(memory_space=pl.ANY)] * len(shards),
        out_specs=pl.BlockSpec(memory_space=pltpu.VMEM),
        out_shape=jax.ShapeDtypeStruct((length, channels), F32),
        scratch_shapes=chunks + inputs,
        compiler_params=limit(16),
        name="grad_first",
    )(place, weight, in_hbm(shards[0]), *shards[1:])


def product_grad_last(shards, weight, place, flips, acc, streams, taps, parts):
    length, features = shards[0].shape
    channels = weight.shape[1]
    hbm = pl.BlockSpec(memory_space=pltpu.HBM)
    vmem = pl.BlockSpec(memory_space=pltpu.VMEM)
    full = whole((length, channels))
    chunks, inputs = grad_scratch(len(flips), weight, length, features)
    return pl.pallas_call(
        partial(product_grad_kernel, flips=flips, last=True),
        grid=(1,),
        in_specs=[pl.BlockSpec(memory_space=pltpu.SMEM)]
        + [hbm]
        + [pl.BlockSpec(memory_space=pl.ANY)] * len(shards)
        + [full, whole((1, length, channels)), whole(taps.shape)],
        out_specs=[full, full, whole((parts, length, channels // parts))],
        out_shape=[
            pltpu.HBM((length, channels), F32),
            pltpu.HBM((length, channels), F32),
            pltpu.HBM((parts, length, channels // parts), BF16),
        ],
        scratch_shapes=chunks + [pltpu.VMEM((parts, length + HALO, channels // parts), F32)] + inputs,
        compiler_params=limit(24),
        name="grad_last",
    )(place, weight, *shards, acc, streams, taps)


def edge_kernel(x_ref, edge_ref, taps_ref, grad_ref, _, __, query_ref, sent_ref, ext, query, sent, sems):
    parts, _, width = sent.shape
    ext[0:HALO, :] = edge_ref[0].astype(F32)
    ext[HALO:, :] = x_ref[0].astype(F32)[0:HALO]
    total = taps_ref[0, 0:1, :] * ext[HALO : 2 * HALO, :]
    for i in range(1, taps_ref.shape[1]):
        total = total + taps_ref[0, i : i + 1, :] * ext[HALO - i : 2 * HALO - i, :]
    query[...] = total
    for j in range(parts):
        lanes = slice(j * width, (j + 1) * width)
        sent[j] = (grad_ref[:, lanes] * total[:, lanes]).astype(BF16)
    copies = [
        pltpu.make_async_copy(query, query_ref.at[pl.ds(0, HALO), :], sems.at[0]),
        pltpu.make_async_copy(sent, sent_ref.at[:, pl.ds(0, HALO), :], sems.at[1]),
    ]
    for copy in copies:
        copy.start()
    for copy in copies:
        copy.wait()


def with_edge(streams, edge, taps, grad, query, sent):
    channels = streams.shape[2]
    parts, _, width = sent.shape
    hbm = pl.BlockSpec(memory_space=pltpu.HBM)
    return pl.pallas_call(
        edge_kernel,
        grid=(1,),
        in_specs=[
            whole((1, 2 * HALO, channels)),
            whole((1, HALO, channels)),
            whole(taps.shape),
            whole((HALO, channels)),
            hbm,
            hbm,
        ],
        out_specs=[hbm, hbm],
        out_shape=[pltpu.HBM(query.shape, F32), pltpu.HBM(sent.shape, BF16)],
        scratch_shapes=[
            pltpu.VMEM((2 * HALO, channels), F32),
            pltpu.VMEM((HALO, channels), F32),
            pltpu.VMEM((parts, HALO, width), BF16),
            pltpu.SemaphoreType.DMA((2,)),
        ],
        input_output_aliases={4: 0, 5: 1},
        compiler_params=limit(4),
        name="edge_rows",
    )(streams, edge, taps, in_hbm(grad), in_hbm(query), in_hbm(sent))


def filtered(taps_ref, stream, ext, begin, length):
    total = taps_ref[stream + 1, 0:1, :] * ext[stream, HALO + begin : HALO + begin + length, :]
    for i in range(1, taps_ref.shape[1]):
        first = HALO + begin - i
        total = total + taps_ref[stream + 1, i : i + 1, :] * ext[stream, first : first + length, :]
    return total


def extend(got_ref, ext):
    parts, _, width = got_ref.shape
    length = (ext.shape[1] - HALO) // parts
    ext[:, 0:HALO, :] = jnp.zeros((2, HALO, width), F32)
    for s in range(parts):
        here = slice(HALO + s * length, HALO + (s + 1) * length)
        ext[0, here, :] = got_ref[s, 0:length, :].astype(F32)
        ext[1, here, :] = got_ref[s, length : 2 * length, :].astype(F32)


def forward_begin(got_ref, taps_ref, medium_ref, kept, ext, signals, medium):
    parts, rows, width = got_ref.shape
    length = rows // 3
    extend(got_ref, ext)
    for s in range(parts):
        here = slice(s * length, (s + 1) * length)
        key = filtered(taps_ref, 0, ext, s * length, length)
        value = filtered(taps_ref, 1, ext, s * length, length)
        kept[0, here, :] = key
        kept[1, here, :] = value
        signals[here, 0:width] = (key * value).astype(BF16)
        signals[here, width : 2 * width] = got_ref[s, 2 * length : 3 * length, :]
    medium[...] = jnp.zeros_like(medium)
    medium[0 : medium_ref.shape[0], :] = medium_ref[...].astype(BF16)


def forward_spectra(cosine, sine, signals, medium):
    tokens, double = signals.shape
    width = double // 2
    kept = medium.shape[0]
    both_c = dot(cosine[:, 0:tokens], signals[...])
    both_s = dot(sine[:, 0:tokens], signals[...])
    mc = dot(cosine[:, 0:kept], medium[...])
    ms = dot(sine[:, 0:kept], medium[...])
    ac, hc, as_, hs = (both_c[:, :width], both_c[:, width:], both_s[:, :width], both_s[:, width:])
    xc = ac * mc - as_ * ms
    xs = ac * ms + as_ * mc
    saved = (ac, as_, hc, hs)
    return saved, (xc * hc - xs * hs).astype(BF16), (xc * hs + xs * hc).astype(BF16)


def forward_end(out_ref, acc, freqs):
    parts, length, _ = out_ref.shape
    for s in range(parts):
        first = s * length + 1
        out_ref[s] = (acc[first : first + length, :] * (1.0 / freqs)).astype(BF16)


def block_copies(tables, held, spectra, spectra_held, sems, blocks):
    size = held.shape[1] // blocks
    groups = []
    for b in range(blocks):
        here = pl.ds(b * size, size)
        group = [pltpu.make_async_copy(t.at[here, :], held.at[i, here, :], sems.at[i, b]) for i, t in enumerate(tables)]
        if spectra is not None:
            group.append(pltpu.make_async_copy(spectra.at[:, here, :], spectra_held.at[:, here, :], sems.at[2, b]))
        groups.append(group)
    return groups


def start_all(copies):
    for copy in copies:
        copy.start()


def wait_all(copies):
    for copy in copies:
        copy.wait()


def forward_kernel(got_ref, taps_ref, medium_ref, cos_ref, sin_ref, *refs, freqs, block, resident):
    if not resident:
        cos_across_ref, sin_across_ref, *refs = refs
    out_ref, kept_ref, spectra_ref, ext, signals, medium, acc, kept, kept_sem, *refs = refs
    rows = acc.shape[0]
    step = pl.program_id(0)
    keep = pltpu.make_async_copy(kept, kept_ref, kept_sem)

    if resident:
        held, yc_all, ys_all, spectra_held, sems, out_sems = refs
        blocks = freqs // block
        groups = block_copies((cos_ref, sin_ref), held, None, None, sems, blocks)
        for group in groups:
            start_all(group)
        forward_begin(got_ref, taps_ref, medium_ref, kept, ext, signals, medium)
        keep.start()
        writes = []
        for b, group in enumerate(groups):
            wait_all(group)
            here = slice(b * block, (b + 1) * block)
            saved, yc, ys = forward_spectra(held[0, here, :], held[1, here, :], signals, medium)
            for i, spectrum in enumerate(saved):
                spectra_held[i, here, :] = spectrum
            there = pl.ds(b * block, block)
            writes.append(
                pltpu.make_async_copy(spectra_held.at[:, there, :], spectra_ref.at[:, there, :], out_sems.at[b])
            )
            writes[b].start()
            yc_all[here, :] = yc
            ys_all[here, :] = ys
        acc[...] = dot(held[0, 0:rows, :], yc_all[...]) + dot(held[1, 0:rows, :], ys_all[...])
        forward_end(out_ref, acc, freqs)
        wait_all(writes)
        keep.wait()
        return

    @pl.when(step == 0)
    def _():
        forward_begin(got_ref, taps_ref, medium_ref, kept, ext, signals, medium)
        keep.start()
        keep.wait()
        acc[...] = jnp.zeros_like(acc)

    saved, yc, ys = forward_spectra(cos_ref[...], sin_ref[...], signals, medium)
    for i, spectrum in enumerate(saved):
        spectra_ref[i] = spectrum
    acc[...] += dot(cos_across_ref[0:rows, :], yc) + dot(sin_across_ref[0:rows, :], ys)

    @pl.when(step == pl.num_programs(0) - 1)
    def _():
        forward_end(out_ref, acc, freqs)


def backward_begin(grads, medium_ref, delayed, signal, medium):
    parts, length, _ = grads.shape
    medium[...] = jnp.zeros_like(medium)
    medium[0 : medium_ref.shape[0], :] = medium_ref[...].astype(BF16)
    delayed[...] = jnp.zeros_like(delayed)
    for s in range(parts):
        delayed[s * length + 1 : (s + 1) * length + 1, :] = grads[s].astype(F32)
    signal[...] = delayed[...].astype(BF16)


def backward_spectra(cosine, sine, signal, medium, spectra):
    gc = dot(cosine, signal[...])
    gs = dot(sine, signal[...])
    ac, as_, hc, hs = spectra
    kept = medium.shape[0]
    mc = dot(cosine[:, 0:kept], medium[...])
    ms = dot(sine[:, 0:kept], medium[...])
    uc = hc * gc + hs * gs
    us = hc * gs - hs * gc
    xc = ac * mc - as_ * ms
    xs = ac * ms + as_ * mc
    both_c = jnp.concatenate([xc * gc + xs * gs, mc * uc + ms * us], 1).astype(BF16)
    both_s = jnp.concatenate([xc * gs - xs * gc, mc * us - ms * uc], 1).astype(BF16)
    return both_c, both_s, (ac * uc + as_ * us).astype(BF16), (ac * us - as_ * uc).astype(BF16)


def backward_end(
    streams, taps_ref, kept, out_ref, packed, small_ref, ext, after, acc, tap_acc, sems, freqs, scale, medium_reach
):
    parts, rows, width = packed.shape
    length = (ext.shape[1] - HALO) // parts
    tokens = parts * length
    reach = taps_ref.shape[1]
    inverse = 1.0 / freqs
    first = length + 2 * HALO
    head = first + length
    after[:, tokens : tokens + HALO, :] = jnp.zeros((2, HALO, width), F32)
    for s in range(parts):
        here = slice(s * length, (s + 1) * length)
        packed[s, first:head, :] = (acc[here, 0:width] * (inverse * scale)).astype(BF16)
        gated = acc[here, width : 2 * width] * inverse
        packed[s, 0:length, :] = gated.astype(BF16)
        after[0, here, :] = gated * kept[1, here, :]
        after[1, here, :] = gated * kept[0, here, :]
    for s in range(parts):
        end = (s + 1) * length
        for j in range(2):
            begin = length + j * HALO
            packed[s, begin : begin + HALO, :] = after[j, end : end + HALO, :].astype(BF16)
    writes = [
        pltpu.make_async_copy(packed.at[:, pl.ds(0, head), :], out_ref.at[:, pl.ds(0, head), :], sems.at[0]),
        pltpu.make_async_copy(
            packed.at[:, pl.ds(head, rows - head), :], out_ref.at[:, pl.ds(head, rows - head), :], sems.at[1]
        ),
    ]
    writes[0].start()
    extend(streams, ext)
    small_ref[...] = jnp.zeros_like(small_ref)
    small_ref[0:medium_reach, :] = tap_acc[0:medium_reach, :] * (inverse * scale)
    for j in range(2):
        sums = [jnp.zeros((8, width), F32) for _ in range(reach)]
        for s in range(parts):
            begin = s * length
            own = after[j, begin : begin + length, :]
            for i in range(reach):
                moved = ext[j, HALO + begin - i : HALO + begin - i + length, :]
                sums[i] = sums[i] + jnp.sum((moved * own).reshape(length // 8, 8, width), 0)
        for i in range(reach):
            row = medium_reach + j * reach + i
            small_ref[row : row + 1, :] = jnp.sum(sums[i], 0, keepdims=True) * scale
    small = small_ref[...].astype(BF16)
    for s in range(parts):
        packed[s, head:, :] = small
    writes[1].start()
    wait_all(writes)


def backward_kernel(
    taps_ref, medium_ref, grads_ref, got_ref, kept_ref, spectra_ref, cos_ref, sin_ref, *refs,
    freqs, block, scale, medium_reach, resident,
):
    if not resident:
        cos_across_ref, sin_across_ref, *refs = refs
    out_ref, packed, small, delayed, signal, ext, after, acc, tap_acc, streams, kept, grads, medium, *refs = refs
    late_sems, write_sems, *refs = refs
    step = pl.program_id(0)
    size = signal.shape[0]
    rows, taps_kept = (acc.shape[0], tap_acc.shape[0])
    late = [
        pltpu.make_async_copy(kept_ref, kept, late_sems.at[0]),
        pltpu.make_async_copy(got_ref.at[:, pl.ds(0, streams.shape[1]), :], streams, late_sems.at[1]),
    ]
    early = pltpu.make_async_copy(grads_ref, grads, late_sems.at[2])

    def end():
        wait_all(late)
        backward_end(
            streams, taps_ref, kept, out_ref, packed, small, ext, after, acc, tap_acc, write_sems,
            freqs, scale, medium_reach,
        )

    if resident:
        held, both_c_all, both_s_all, taps_c_all, taps_s_all, spectra_held, sems = refs
        groups = block_copies((cos_ref, sin_ref), held, spectra_ref, spectra_held, sems, freqs // block)
        early.start()
        for group in groups:
            start_all(group)
        start_all(late)
        early.wait()
        backward_begin(grads, medium_ref, delayed, signal, medium)
        for b, group in enumerate(groups):
            wait_all(group)
            here = slice(b * block, (b + 1) * block)
            spectra = [spectra_held[i, here, :] for i in range(spectra_held.shape[0])]
            both_c_all[here, :], both_s_all[here, :], taps_c_all[here, :], taps_s_all[here, :] = backward_spectra(
                held[0, here, 0:size], held[1, here, 0:size], signal, medium, spectra
            )
        acc[...] = dot(held[0, 0:rows, :], both_c_all[...]) + dot(held[1, 0:rows, :], both_s_all[...])
        tap_acc[...] = dot(held[0, 0:taps_kept, :], taps_c_all[...]) + dot(held[1, 0:taps_kept, :], taps_s_all[...])
        end()
        return

    @pl.when(step == 0)
    def _():
        early.start()
        early.wait()
        backward_begin(grads, medium_ref, delayed, signal, medium)
        acc[...] = jnp.zeros_like(acc)
        tap_acc[...] = jnp.zeros_like(tap_acc)

    spectra = [spectra_ref[i] for i in range(spectra_ref.shape[0])]
    both_c, both_s, taps_c, taps_s = backward_spectra(cos_ref[:, 0:size], sin_ref[:, 0:size], signal, medium, spectra)
    acc[...] += dot(cos_across_ref[0:rows, :], both_c) + dot(sin_across_ref[0:rows, :], both_s)
    tap_acc[...] += dot(cos_across_ref[0:taps_kept, :], taps_c) + dot(sin_across_ref[0:taps_kept, :], taps_s)

    @pl.when(step == pl.num_programs(0) - 1)
    def _():
        start_all(late)
        end()


def spectral_plan(freqs, block, tables):
    if freqs * freqs <= TABLE_LIMIT:
        hbm = pl.BlockSpec(memory_space=pltpu.HBM)
        return True, 1, [hbm, hbm], [in_hbm(t) for t in tables]
    rows = pl.BlockSpec((block, freqs), lambda j: (j, 0))
    columns = pl.BlockSpec((freqs, block), lambda j: (0, j))
    return False, freqs // block, [rows, rows, columns, columns], [*tables, *tables]


def held_scratch(freqs, block, width, widths, kinds):
    blocks = freqs // block
    return (
        [pltpu.VMEM((2, freqs, freqs), BF16)]
        + [pltpu.VMEM((freqs, w), BF16) for w in widths]
        + [pltpu.VMEM((4, freqs, width), F32), pltpu.SemaphoreType.DMA((kinds, blocks))]
    )


def forward_call(got, taps, medium_taps, tables, freqs, block):
    parts, tall, width = got.shape
    length = tall // 3
    tokens = parts * length
    padded = -(-medium_taps.shape[0] // 128) * 128
    resident, steps, specs, operands = spectral_plan(freqs, block, tables)
    per = freqs // steps
    hbm = pl.BlockSpec(memory_space=pltpu.HBM)
    return pl.pallas_call(
        partial(forward_kernel, freqs=freqs, block=block, resident=resident),
        grid=(steps,),
        in_specs=[whole(got.shape), whole(taps.shape), whole(medium_taps.shape)] + specs,
        out_specs=[
            whole((parts, length, width)),
            hbm,
            hbm if resident else pl.BlockSpec((4, per, width), lambda j: (0, j, 0)),
        ],
        out_shape=[
            pltpu.HBM((parts, length, width), BF16),
            pltpu.HBM((2, tokens, width), F32),
            pltpu.HBM((4, freqs, width), F32),
        ],
        scratch_shapes=[
            pltpu.VMEM((2, tokens + HALO, width), F32),
            pltpu.VMEM((tokens, 2 * width), BF16),
            pltpu.VMEM((padded, width), BF16),
            pltpu.VMEM((tokens + HALO, width), F32),
            pltpu.VMEM((2, tokens, width), F32),
            pltpu.SemaphoreType.DMA,
        ]
        + (
            held_scratch(freqs, block, width, (width, width), 2) + [pltpu.SemaphoreType.DMA((freqs // block,))]
            if resident
            else []
        ),
        compiler_params=limit(32 if resident else 60),
        name="forward_spectral",
    )(in_hbm(got), taps, medium_taps, *operands)


def backward_call(got, grads, taps, medium_taps, kept, spectra, tables, freqs, block, scale, medium_reach, rows, small, extra):
    parts, tall, width = got.shape
    length = tall // 3
    tokens = parts * length
    padded = -(-medium_reach // 128) * 128
    late = -(-(tokens + 1) // 128) * 128
    resident, steps, specs, operands = spectral_plan(freqs, block, tables)
    per = freqs // steps
    hbm = pl.BlockSpec(memory_space=pltpu.HBM)
    return pl.pallas_call(
        partial(
            backward_kernel, freqs=freqs, block=block, scale=scale, medium_reach=medium_reach, resident=resident
        ),
        grid=(steps,),
        in_specs=[
            whole(taps.shape),
            whole(medium_taps.shape),
            pl.BlockSpec(memory_space=pl.ANY),
            hbm,
            hbm,
            hbm if resident else pl.BlockSpec((4, per, width), lambda j: (0, j, 0)),
        ]
        + specs,
        out_specs=hbm,
        out_shape=pltpu.HBM((parts, rows + small + extra, width), BF16),
        scratch_shapes=[
            pltpu.VMEM((parts, rows + small, width), BF16),
            pltpu.VMEM((small, width), F32),
            pltpu.VMEM((late, width), F32),
            pltpu.VMEM((late, width), BF16),
            pltpu.VMEM((2, tokens + HALO, width), F32),
            pltpu.VMEM((2, tokens + HALO, width), F32),
            pltpu.VMEM((tokens, 2 * width), F32),
            pltpu.VMEM((padded, width), F32),
            pltpu.VMEM((parts, 2 * length, width), BF16),
            pltpu.VMEM((2, tokens, width), F32),
            pltpu.VMEM((parts, length, width), BF16),
            pltpu.VMEM((padded, width), BF16),
            pltpu.SemaphoreType.DMA((3,)),
            pltpu.SemaphoreType.DMA((2,)),
        ]
        + (held_scratch(freqs, block, width, (2 * width, 2 * width, width, width), 3) if resident else []),
        compiler_params=limit(40 if resident else 60),
        name="backward_spectral",
    )(taps, medium_taps, grads, in_hbm(got), in_hbm(kept), in_hbm(spectra), *operands)


def product_kernel(
    got_ref, query_ref, grad_ref, x_ref, edge_ref, _, product_ref, query_grad_ref, first_ref, back_ref,
    got, query, grad, x, product, query_grad, first, ext, taps, rounded, sems, *, reach, begin,
):
    parts, length, width = got.shape
    reads = [
        pltpu.make_async_copy(source, held, sems.at[i])
        for i, (source, held) in enumerate(((x_ref.at[0], x), (got_ref, got), (grad_ref, grad), (query_ref, query)))
    ]
    start_all(reads)
    taps[...] = jnp.zeros_like(taps)
    reads[0].wait()
    for j in range(parts):
        lanes = slice(j * width, (j + 1) * width)
        ext[j, 0:HALO, :] = edge_ref[0, :, lanes].astype(F32)
        ext[j, HALO:, :] = x[:, lanes].astype(F32)
    wait_all(reads[1:3])
    for j in range(parts):
        lanes = slice(j * width, (j + 1) * width)
        own = grad[:, lanes] * got[j].astype(F32)
        query_grad[j] = own
        first[:, lanes] = own[0:HALO].astype(BF16)
        for i in range(reach):
            moved = ext[j, HALO - i : HALO - i + length, :]
            taps[j * reach + i : j * reach + i + 1, :] = jnp.sum(moved * own, 0, keepdims=True)
    for s in range(parts):
        rounded[s] = taps[...].astype(BF16)
    writes = [
        pltpu.make_async_copy(rounded, back_ref.at[:, pl.ds(begin, taps.shape[0]), :], sems.at[4]),
        pltpu.make_async_copy(query_grad, query_grad_ref, sems.at[5]),
        pltpu.make_async_copy(first, first_ref, sems.at[6]),
        pltpu.make_async_copy(product, product_ref, sems.at[7]),
    ]
    start_all(writes[0:3])
    reads[3].wait()
    for j in range(parts):
        lanes = slice(j * width, (j + 1) * width)
        product[:, lanes] = (query[:, lanes] * got[j].astype(F32)).astype(BF16)
    writes[3].start()
    wait_all(writes)


def product_call(convolved, query, grad, streams, edge, back, reach, begin):
    parts, length, width = convolved.shape
    channels = parts * width
    extra = back.shape[1] - begin
    hbm = pl.BlockSpec(memory_space=pltpu.HBM)
    return pl.pallas_call(
        partial(product_kernel, reach=reach, begin=begin),
        grid=(1,),
        in_specs=[pl.BlockSpec(memory_space=pl.ANY), hbm, hbm, hbm, whole((1, HALO, channels)), hbm],
        out_specs=[hbm] * 4,
        out_shape=[
            pltpu.HBM((length, channels), BF16),
            pltpu.HBM((parts, length, width), F32),
            pltpu.HBM((HALO, channels), BF16),
            pltpu.HBM(back.shape, BF16),
        ],
        scratch_shapes=[
            pltpu.VMEM((parts, length, width), BF16),
            pltpu.VMEM((length, channels), F32),
            pltpu.VMEM((length, channels), F32),
            pltpu.VMEM((length, channels), BF16),
            pltpu.VMEM((length, channels), BF16),
            pltpu.VMEM((parts, length, width), F32),
            pltpu.VMEM((HALO, channels), BF16),
            pltpu.VMEM((parts, length + HALO, width), F32),
            pltpu.VMEM((extra, width), F32),
            pltpu.VMEM((parts, extra, width), BF16),
            pltpu.SemaphoreType.DMA((8,)),
        ],
        input_output_aliases={5: 3},
        compiler_params=limit(16),
        name="product",
    )(convolved, in_hbm(query), in_hbm(grad), in_hbm(streams), edge, in_hbm(back))


def project_kernel(place_ref, product_ref, w_ref, *refs, flips):
    out_refs = refs[: len(flips)]
    buffer, sems = refs[len(flips) :]
    copies = weight_chunks(place_ref, w_ref, buffer, sems, flips, out_refs[0].shape[1])
    start_all(copies)
    deep = buffer.shape[1]
    per = len(copies) // len(flips)
    for slot, copy in enumerate(copies):
        copy.wait()
        part = lax.dot_general(
            product_ref[...], buffer[slot], (((1,), (1,)), ((), ())), preferred_element_type=F32
        )
        lanes = slice(slot % per * deep, (slot % per + 1) * deep)
        out = out_refs[slot // per]
        out[:, lanes] = part.astype(out.dtype)


def project(product, weight, place, flips, features, dtypes):
    length = product.shape[0]
    vmem = pl.BlockSpec(memory_space=pltpu.VMEM)
    return pl.pallas_call(
        partial(project_kernel, flips=flips),
        in_specs=[pl.BlockSpec(memory_space=pltpu.SMEM), vmem, pl.BlockSpec(memory_space=pltpu.HBM)],
        out_specs=[vmem] * len(flips),
        out_shape=[jax.ShapeDtypeStruct((length, features), dtype) for dtype in dtypes],
        scratch_shapes=chunk_scratch(weight, features, len(flips)),
        compiler_params=limit(16),
        name="project",
    )(place, product, weight)


def local_kernel(x_ref, edge_ref, taps_ref, out_ref, ext):
    _, parts, length, width = out_ref.shape
    for j in range(2):
        for p in range(parts):
            lanes = slice(p * width, (p + 1) * width)
            ext[p, 0:HALO, :] = edge_ref[j + 1, :, lanes].astype(F32)
            ext[p, HALO:, :] = x_ref[j + 1, :, lanes].astype(F32)
            total = taps_ref[j + 1, 0:1, lanes] * ext[p, HALO : HALO + length, :]
            for i in range(1, taps_ref.shape[1]):
                total = total + taps_ref[j + 1, i : i + 1, lanes] * ext[p, HALO - i : HALO - i + length, :]
            out_ref[j, p] = total


def finish_kernel(
    got_ref, query_grad_ref, next_ref, taps_ref, local_ref,
    input_grad_ref, filter_ref, medium_ref, short_ref,
    got, local, ext, input_grad, filtering, medium, short, sums, sems, *, own_rows, scale,
):
    parts, _, width = got.shape
    length = filtering.shape[0]
    reach = taps_ref.shape[1]
    medium_reach = medium.shape[0]
    reads = [
        pltpu.make_async_copy(query_grad_ref, ext.at[0, :, pl.ds(0, length), :], sems.at[0]),
        pltpu.make_async_copy(got_ref, got, sems.at[1]),
        pltpu.make_async_copy(local_ref, local, sems.at[2]),
    ]
    start_all(reads)

    def convolve(k):
        for j in range(parts):
            lanes = slice(j * width, (j + 1) * width)
            total = taps_ref[k, 0:1, lanes] * ext[k, j, 0:length, :]
            for i in range(1, reach):
                total = total + taps_ref[k, i : i + 1, lanes] * ext[k, j, i : i + length, :]
            input_grad[k, :, lanes] = total.astype(BF16)

    writes = [
        pltpu.make_async_copy(input_grad.at[k], input_grad_ref.at[k], sems.at[3 + k]) for k in range(3)
    ]
    more = [
        pltpu.make_async_copy(filtering, filter_ref, sems.at[6]),
        pltpu.make_async_copy(medium, medium_ref, sems.at[7]),
        pltpu.make_async_copy(short, short_ref, sems.at[8]),
    ]
    for j in range(parts):
        ext[0, j, length:, :] = next_ref[:, j * width : (j + 1) * width].astype(F32)
    reads[0].wait()
    convolve(0)
    writes[0].start()
    reads[1].wait()
    after = length + 2 * HALO
    first = after + length
    taps = first + own_rows
    total = got[0, taps:, :].astype(F32)
    for j in range(1, parts):
        total = total + got[j, taps:, :].astype(F32)
    sums[...] = total
    for j in range(parts):
        lanes = slice(j * width, (j + 1) * width)
        filtering[:, lanes] = got[j, after:first, :].astype(F32)
        small = got[j, first:taps, :].astype(F32)
        medium[:, lanes] = small[0:medium_reach, :]
        second = medium_reach + reach
        short[0, :, lanes] = sums[j * reach : (j + 1) * reach, :] * scale
        short[1, :, lanes] = small[medium_reach:second, :]
        short[2, :, lanes] = small[second : second + reach, :]
    start_all(more)
    reads[2].wait()
    for k in range(1, 3):
        for j in range(parts):
            ext[k, j, 0:length, :] = got[j, 0:length, :].astype(F32) * local[2 - k, j]
            begin = length + (k - 1) * HALO
            ext[k, j, length:, :] = got[j, begin : begin + HALO, :].astype(F32)
        convolve(k)
        writes[k].start()
    wait_all(writes + more)


def finish_call(returned, query_grad, next_grad, taps, features, medium_reach, own_rows, scale):
    parts, _, width = returned.shape
    groups, reach, channels = taps.shape
    length = query_grad.shape[1]
    hbm = pl.BlockSpec(memory_space=pltpu.HBM)
    return pl.pallas_call(
        partial(finish_kernel, own_rows=own_rows, scale=scale),
        grid=(1,),
        in_specs=[pl.BlockSpec(memory_space=pl.ANY), hbm, whole((HALO, channels)), whole(taps.shape), hbm],
        out_specs=[hbm] * 4,
        out_shape=[
            pltpu.HBM((groups, length, channels), BF16),
            pltpu.HBM((length, channels), F32),
            pltpu.HBM((medium_reach, channels), F32),
            pltpu.HBM((groups, reach, channels), F32),
        ],
        scratch_shapes=[
            pltpu.VMEM(returned.shape, BF16),
            pltpu.VMEM((2, parts, length, width), F32),
            pltpu.VMEM((groups, parts, length + HALO, width), F32),
            pltpu.VMEM((groups, length, channels), BF16),
            pltpu.VMEM((length, channels), F32),
            pltpu.VMEM((medium_reach, channels), F32),
            pltpu.VMEM((groups, reach, channels), F32),
            pltpu.VMEM((-(-parts * reach // 8) * 8, width), F32),
            pltpu.SemaphoreType.DMA((9,)),
        ],
        compiler_params=limit(24),
        name="finish",
    )(returned, in_hbm(query_grad), next_grad, taps, in_hbm(features))


def reshard(value):
    return lax.all_to_all(value, "seq", split_axis=0, concat_axis=0, tiled=True)


def local(inputs, short_taps, medium_taps, long_filter, out_weight, out_cotangent):
    length, groups, channels = inputs.shape
    reach = short_taps.shape[0]
    medium_reach = medium_taps.shape[0]
    parts = lax.axis_size("seq")
    position = lax.axis_index("seq")
    place = lax.axis_index("tensor").astype(jnp.int32)[None]
    features = out_cotangent.shape[1]
    width = channels // parts
    tokens = length * parts
    scale = 1.0 / math.sqrt(tokens)
    freqs, block = spectral_sizes(tokens, medium_reach)
    vmem = pl.BlockSpec(memory_space=pltpu.VMEM)

    weight = pltpu.with_memory_space_constraint(out_weight, pltpu.HBM)
    streams = inputs.transpose(1, 0, 2)
    taps = short_taps.transpose(1, 0, 2)
    hbm = pl.BlockSpec(memory_space=pltpu.HBM)
    packed, last_rows = pl.pallas_call(
        pack_kernel,
        in_specs=[hbm, hbm],
        out_specs=[hbm, hbm],
        out_shape=[
            pltpu.HBM((parts, 3 * length, width), BF16),
            pltpu.HBM((groups, HALO, channels), BF16),
        ],
        scratch_shapes=[
            pltpu.VMEM((2, length, channels), BF16),
            pltpu.VMEM((length, channels), F32),
            pltpu.VMEM((parts, 3 * length, width), BF16),
            pltpu.VMEM((groups, HALO, channels), BF16),
            pltpu.SemaphoreType.DMA((2 + parts,)),
            pltpu.SemaphoreType.DMA((2,)),
        ],
        compiler_params=limit(8),
        name="pack",
    )(
        pltpu.with_memory_space_constraint(streams, pltpu.HBM),
        pltpu.with_memory_space_constraint(long_filter, pltpu.HBM),
    )
    got = reshard(packed)
    edge = shift(last_rows, "seq", 1)
    cot_x = exchange(out_cotangent, "tensor", 2)
    cot_core = exchange(out_cotangent, "tensor", 1)

    tables = dft_tables(freqs)
    own_taps = lax.dynamic_slice_in_dim(taps, position * width, width, 2)
    own_medium = lax.dynamic_slice_in_dim(medium_taps, position * width, width, 1)

    acc = product_grad_first((out_cotangent, cot_core), weight, place, (0, 1))
    cot_far = exchange(cot_x, "tensor", 1)
    product_grad, query, sent = product_grad_last((cot_x, cot_far), weight, place, (2, 3), acc, streams, taps, parts)
    query, sent = with_edge(streams, edge, taps, product_grad, query, sent)
    grads = reshard(sent)

    convolved, kept, spectra = forward_call(got, own_taps, own_medium, tables, freqs, block)
    convolved = reshard(convolved)

    rows = 2 * length + 2 * HALO
    small = -(-(medium_reach + 2 * reach) // 8) * 8
    extra = -(-parts * reach // 8) * 8
    back = backward_call(
        got, grads, own_taps, own_medium, kept, spectra, tables, freqs, block, scale, medium_reach, rows, small, extra
    )
    product, query_grad, first_rows, back = product_call(
        convolved, query, product_grad, streams, edge, back, reach, rows + small
    )
    returned = reshard(back)

    (far,) = project(product, weight, place, (3,), features, (BF16,))
    far_core = exchange(far, "tensor", 1)
    (across,) = project(product, weight, place, (2,), features, (F32,))
    across_sum = exchange((across + far_core.astype(F32)).astype(BF16), "tensor", 2)
    near, own = project(product, weight, place, (1, 0), features, (BF16, F32))
    near_core = exchange(near, "tensor", 1)
    next_grad = shift(first_rows, "seq", -1)

    local_features = pl.pallas_call(
        local_kernel,
        in_specs=[vmem] * 3,
        out_specs=vmem,
        out_shape=pltpu.HBM((2, parts, length, width), F32),
        scratch_shapes=[pltpu.VMEM((parts, length + HALO, width), F32)],
        compiler_params=limit(8),
        name="local",
    )(in_hbm(streams), edge, taps)
    input_grad, filter_grad, medium_grad, short_grad = finish_call(
        returned, query_grad, next_grad, taps, local_features, medium_reach, small, scale
    )

    output = (own + near_core.astype(F32) + across_sum.astype(F32)).astype(BF16)
    return (
        output,
        input_grad.transpose(1, 0, 2),
        filter_grad,
        medium_grad,
        short_grad.transpose(1, 0, 2),
    )


def solution(mesh):
    return jax.shard_map(
        local,
        mesh=mesh,
        in_specs=(
            P("seq", None, "tensor"),
            P(None, None, "tensor"),
            P(None, "tensor"),
            P("seq", "tensor"),
            P(None, "tensor"),
            P("seq", "tensor"),
        ),
        out_specs=(
            P("seq", "tensor"),
            P("seq", None, "tensor"),
            P("seq", "tensor"),
            P(None, "tensor"),
            P(None, None, "tensor"),
        ),
        check_vma=False,
    )
```
